32 devices in a mesh: seq: 16 (over z, x, core), fsdp: 2 (over y).
Axes of the slice: x: 2, y: 2, z: 4, core: 2. Of those that a mesh axis runs over, the one named last changes fastest.
Arguments:
- hidden_in: bfloat16 [16, 1024, 1024], P('fsdp', 'seq'), may hold values from -10 to 10
- out_grad: bfloat16 [16, 1024, 1024], P('fsdp', 'seq'), may hold values from -6 to 6
- qkv_weight: bfloat16 [1024, 3072], P(('seq', 'fsdp')), may hold values from -0.25 to 0.25
- attn_out_weight: bfloat16 [1024, 1024], P(('seq', 'fsdp')), may hold values from -1 to 1
- in_weight: bfloat16 [1024, 5248], P(('seq', 'fsdp')), may hold values from -0.1875 to 0.1875
- down_weight: bfloat16 [2624, 1024], P(None, ('seq', 'fsdp')), may hold values from -0.25 to 0.25
- attn_gain: bfloat16 [1024], P(('seq', 'fsdp')), may hold values from 0.25 to 1.75
- mlp_gain: bfloat16 [1024], P(('seq', 'fsdp')), may hold values from 0.25 to 1.75
- seq_lengths: int32 [16], replicated, may hold values from 256 to 1024, as said below
- slot_order: int32 [16], replicated, may hold values from 0 to 15, each once
Outputs:
- output: bfloat16 [16, 1024, 1024], P('fsdp', 'seq')
- input_grad: bfloat16 [16, 1024, 1024], P('fsdp', 'seq')
- qkv_grad: float32 [1024, 3072], P(('seq', 'fsdp'))
- attn_out_grad: float32 [1024, 1024], P(('seq', 'fsdp'))
- in_grad: float32 [1024, 5248], P(('seq', 'fsdp'))
- down_grad: float32 [2624, 1024], P(None, ('seq', 'fsdp'))
- attn_gain_grad: float32 [1024], P(('seq', 'fsdp'))
- mlp_gain_grad: float32 [1024], P(('seq', 'fsdp'))
- root_squares: float32 [5], replicated
The draws below stay inside these ranges and needn't reach their ends.
Inputs may be any that keep to these rules, and one draw needn't show every extreme that they name: `seq_lengths`: one sequence has exactly 1024 valid positions.
All inputs are finite; a program needn't handle non-finite values.
Results may differ from the reference program's by a relative error of at most 0.025.
Values may be sent and summed in bfloat16 or wider, within the bound.
A program may use at most 320 MiB of HBM per device.

```python
import jax
import jax.numpy as jnp
from jax import lax

D = 1024
HEADS = 16
HEAD_DIM = 64
FF = 2624
SLOT = 1024
SLOTS = 16


def draw_hidden_in(key, part):
    first_key = jax.random.fold_in(key, 0)
    ramp = jnp.arange(SLOT, dtype=jnp.float32) / SLOT
    rising = (0.5 + 1.5 * ramp)[None, :, None]
    values = jax.random.normal(first_key, (SLOTS, SLOT, D), jnp.float32) * rising
    return jnp.clip(values, -10.0, 10.0).astype(jnp.bfloat16)


def draw_seq_lengths(key, part):
    first_key, second_key = jax.random.split(key)
    drawn = jax.random.randint(first_key, (SLOTS,), SLOT // 4, SLOT + 1)
    longest = jax.random.randint(second_key, (), 0, SLOTS)
    return jnp.where(jnp.arange(SLOTS) == longest, SLOT, drawn).astype(jnp.int32)


def level_of(stream_key, dims, cuts, least, top_value):
    gain = 1.0
    for axis_at, shards_of in cuts:
        draws = jax.random.uniform(jax.random.fold_in(jax.random.fold_in(stream_key, 6), axis_at), (shards_of,), jnp.float32, least / len(cuts), top_value / len(cuts))
        gain = gain * jnp.repeat(jnp.exp(draws), dims[axis_at] // shards_of).reshape((-1,) + (1,) * (len(dims) - 1 - axis_at))
    return gain


def scatter_about(own_key, dims, deviation, bound, shards=(), kind=jnp.bfloat16):
    values = jax.random.normal(own_key, dims, jnp.float32) * deviation
    if len(shards) > 0:
        values = level_of(own_key, dims, shards, -0.22, 0.18) * values
    return jnp.clip(values, min=-bound, max=bound).astype(kind)


def setup_inputs(seed: int = 0) -> dict:
    splits = jax.random.split(jax.random.key(seed), 11)
    return {
        "hidden_in": draw_hidden_in(jax.random.fold_in(splits[10], 71), 0),
        "out_grad": scatter_about(splits[1], (SLOTS, SLOT, D), 1.0, 6.0, ((0, 2), (1, 16))),
        "qkv_weight": scatter_about(splits[2], (D, 3 * D), (D // 2) ** -0.5, 0.25, ((0, 32),)),
        "attn_out_weight": scatter_about(splits[3], (D, D), 32 ** -0.5, 1.0, ((0, 32),)),
        "in_weight": scatter_about(splits[4], (D, 2 * FF), D ** -0.5, 0.1875, ((0, 32),)),
        "down_weight": scatter_about(splits[5], (FF, D), (FF // 4) ** -0.5, 0.25, ((1, 32),)),
        "attn_gain": jnp.clip(1.0 + 0.15 * jax.random.normal(splits[6], (D,), jnp.float32), 0.25, 1.75).astype(jnp.bfloat16),
        "mlp_gain": jnp.clip(1.0 + 0.15 * jax.random.normal(splits[7], (D,), jnp.float32), 0.25, 1.75).astype(jnp.bfloat16),
        "seq_lengths": draw_seq_lengths(jax.random.fold_in(splits[10], 71), 0),
        "slot_order": jax.random.permutation(splits[9], SLOTS).astype(jnp.int32),
    }


EPS = 1e-05
THETA = 160000.0
HIGH = lax.Precision.HIGHEST

@jax.custom_vjp
def low(v):
    return lax.optimization_barrier(v.astype(jnp.bfloat16)).astype(jnp.float32)

@jax.custom_vjp
def low_back(v):
    return v

def low_keep(v):
    return (low(v), None)

def low_pass(kept, grad):
    return (grad,)

def back_keep(v):
    return (v, None)

def back_low(kept, grad):
    return (low(grad),)
low.defvjp(low_keep, low_pass)
low_back.defvjp(back_keep, back_low)

def normalize(values):
    average = lax.optimization_barrier(jnp.mean(values, axis=-1, keepdims=True))
    centered = values - average
    variance = lax.optimization_barrier(jnp.mean(centered * centered, axis=-1, keepdims=True))
    return centered * lax.rsqrt(variance + EPS)

def rotary_tables(places, head_size):
    halfway = head_size // 2
    ladder = jnp.arange(halfway, dtype=jnp.float32) * (2.0 / head_size)
    inverse = 1.0 / THETA ** ladder
    angles = places.astype(jnp.float32)[:, None] * inverse[None, :]
    angles = jnp.concatenate([angles, angles], axis=-1)
    return (jnp.cos(angles), jnp.sin(angles))

def rotate(values, cosine, sine):
    halfway = values.shape[-1] // 2
    turned = jnp.concatenate([-values[..., halfway:], values[..., :halfway]], axis=-1)
    return values * cosine + turned * sine

def gelu_exact(values):
    return jax.nn.gelu(values, approximate=False)

def layer(inputs, w_qkv, w_attn, w_input, w_down, gain_attn, gain_mlp, length):
    places = jnp.arange(SLOT, dtype=jnp.int32)
    usable = places < length
    valid = usable.astype(jnp.float32)[:, None]
    act_one = low(normalize(inputs) * gain_attn)
    mixed = low_back(jnp.dot(act_one, w_qkv, precision=HIGH)).reshape(SLOT, 3, HEADS, HEAD_DIM)
    cosine, sine = rotary_tables(places, HEAD_DIM)
    cosine = cosine[:, None, :]
    sine = sine[:, None, :]
    queries = low_back(low(rotate(mixed[:, 0], cosine, sine)))
    keys_all = low_back(low(rotate(mixed[:, 1], cosine, sine)))
    values_all = low_back(low(mixed[:, 2]))
    factor = HEAD_DIM ** (-0.5)

    def one_head(pieces):
        head_q, head_k, head_v = pieces
        scores = low_back(jnp.dot(head_q, head_k.T, precision=HIGH) * factor)
        scores = jnp.where(usable[None, :], scores, -jnp.inf)
        probs = jax.nn.softmax(scores, axis=-1)
        return low_back(low(jnp.dot(low(probs), head_v, precision=HIGH)))
    per_head = lax.map(jax.checkpoint(one_head), (queries.transpose(1, 0, 2), keys_all.transpose(1, 0, 2), values_all.transpose(1, 0, 2)))
    attn_rows = per_head.transpose(1, 0, 2).reshape(SLOT, D)
    attn = low_back(jnp.dot(attn_rows, w_attn, precision=HIGH))
    middle = inputs + attn
    act_two = low(normalize(middle) * gain_mlp)
    joined = low_back(jnp.dot(act_two, w_input, precision=HIGH))
    input_half = joined[:, :FF]
    gate_half = joined[:, FF:]
    product = low(gelu_exact(input_half) * gate_half)
    branch = low_back(jnp.dot(product, w_down, precision=HIGH))
    result = (middle + branch) * valid
    squares = jnp.stack([jnp.sum(valid * tensor * tensor) for tensor in (inputs, middle, result, attn, branch)])
    return (result, squares)

def reference(hidden_in, out_grad, qkv_weight, attn_out_weight, in_weight, down_weight, attn_gain, mlp_gain, seq_lengths, slot_order):
    weights = tuple((tensor.astype(jnp.float32) for tensor in (qkv_weight, attn_out_weight, in_weight, down_weight, attn_gain, mlp_gain)))
    by_slot = seq_lengths[slot_order]

    def one_slot(totals, pieces):
        slot_in, slot_grad, length = pieces

        def run(inputs, w_qkv, w_attn, w_input, w_down, gain_attn, gain_mlp):
            return layer(inputs, w_qkv, w_attn, w_input, w_down, gain_attn, gain_mlp, length)
        result, pull, squares = jax.vjp(run, slot_in.astype(jnp.float32), *weights, has_aux=True)
        grads = pull(slot_grad.astype(jnp.float32))
        added = tuple((total + extra for total, extra in zip(totals, tuple(grads[1:]) + (squares,))))
        return (added, (result.astype(jnp.bfloat16), grads[0].astype(jnp.bfloat16)))
    begin = tuple((jnp.zeros_like(tensor) for tensor in weights)) + (jnp.zeros((5,), jnp.float32),)
    totals, (outputs, input_grads) = lax.scan(one_slot, begin, (hidden_in, out_grad, by_slot))
    tokens_valid = jnp.sum(seq_lengths).astype(jnp.float32)
    root_squares = jnp.sqrt(totals[6] / (tokens_valid * D))
    return (outputs, input_grads, totals[0], totals[1], totals[2], totals[3], totals[4], totals[5], root_squares)
```

```python
import functools

import jax
import jax.numpy as jnp
from jax import lax
from jax.experimental import pallas as pl
from jax.experimental.pallas import tpu as pltpu
from jax.sharding import PartitionSpec as P

HEADS = 16
LINE = 4
LANES = 128
EPS = 1e-05
THETA = 160000.0
F32 = jnp.float32
BF16 = jnp.bfloat16
MESH = pl.DeviceIdType.MESH


def up_to(size, unit):
    return -(-size // unit) * unit


class Place:
    def __init__(self, seq_size, fsdp_size):
        self.seq_size, self.fsdp_size = seq_size, fsdp_size
        self.rest = seq_size // (2 * LINE)
        self.swap = self.rest == fsdp_size
        self.nf, self.ng = self.rest, fsdp_size
        self.blocks = LINE * self.nf * self.ng
        self.seq = lax.axis_index("seq")
        self.y = lax.axis_index("fsdp")
        self.core = self.seq % 2
        self.r = (self.seq // 2) % self.rest
        self.z = self.seq // (2 * self.rest)
        self.f, self.g = self.split(self.r, self.y, self.core)

    def split(self, r, y, core):
        if not self.swap:
            return r, y
        return (1 - core) * r + core * y, (1 - core) * y + core * r

    def device(self, z, f, g, core=None):
        core = self.core if core is None else core
        r, y = self.split(f, g, core)
        return (z * self.rest + r) * 2 + core, y

    def row_block(self, z, f, g, core=None):
        seq, y = self.device(z, f, g, core)
        return seq * self.fsdp_size + y

    def index(self, z, f, g):
        return (z * self.nf + f) * self.ng + g

    def partner(self):
        return self.seq + 1 - 2 * self.core, self.y


def both(first, second):
    if first is True:
        return second
    if second is True:
        return first
    return jnp.logical_and(first, second)


def when(condition, body):
    if condition is True:
        body()
    else:
        pl.when(condition)(body)


def meet(peers, awaited):
    barrier = pltpu.get_barrier_semaphore()
    for condition, device in peers:
        when(
            condition,
            functools.partial(
                pl.semaphore_signal, barrier, inc=1, device_id=device, device_id_type=MESH
            ),
        )
    pl.semaphore_wait(barrier, awaited)


def plane_peers(at):
    below, above = at.z > 0, at.z < LINE - 1
    peers = [
        (below, at.device(at.z - 1, at.f, at.g)),
        (above, at.device(at.z + 1, at.f, at.g)),
        (True, at.partner()),
    ]
    for step in range(1, at.nf):
        peers.append((True, at.device(at.z, (at.f + step) % at.nf, at.g)))
    for step in range(1, at.ng):
        peers.append((True, at.device(at.z, at.f, (at.g + step) % at.ng)))
    count = 1 + (at.nf - 1) + (at.ng - 1)
    count = count + jnp.where(below, 1, 0) + jnp.where(above, 1, 0)
    return peers, count


def slot_peers(at, slots):
    group = at.seq_size // slots
    own_slot, own_part = at.seq // group, at.seq % group
    same = at.seq // slots == own_part
    peers = []
    for step in range(slots):
        wide = ((own_slot + step) % slots) * group + at.seq // slots
        narrow = own_part * slots + (at.seq + step) % slots
        condition = True if step else jnp.logical_not(same)
        peers.append((condition, (wide, at.y)))
        peers.append((condition, (narrow, at.y)))
    return peers, 2 * slots - 2 * jnp.where(same, 1, 0)


def steps_of(at):
    out = []
    for dz in (0, -1, 1, -2, 2, -3, 3):
        for df in range(at.nf):
            for dg in range(at.ng):
                out.append((abs(dz) + (df > 0) + (dg > 0), dz, df, dg))
    out.sort(key=lambda item: item[0])
    return [item[1:] for item in out]


def present(at, dz):
    if dz == 0:
        return True
    return at.z + dz >= 0 if dz < 0 else at.z + dz < LINE


class Gather:
    def __init__(self, at, sections, sems, phase):
        self.at, self.sections, self.phase = at, sections, phase
        self.send_sems, self.plane_sems, self.pair_sems = sems

    @staticmethod
    def scratch(count, nf, ng):
        dma = pltpu.SemaphoreType.DMA
        blocks, kinds = LINE * nf * ng, 3 + (nf - 1) + (ng - 1)
        return [dma((count, blocks, kinds)), dma((count, blocks)), dma((count, blocks + 1))]

    def own(self, number):
        source, _, columns, _ = self.sections[number]
        return source.at[:, columns]

    def block(self, number, z, f, g):
        source, whole, columns, _ = self.sections[number]
        rows = source.shape[0]
        start = pl.multiple_of(self.at.row_block(z, f, g) * rows, rows)
        return whole.at[pl.ds(start, rows), columns]

    def forward(self, number, condition, source, dz, df, dg):
        at, order = self.at, self.sections[number][3]
        z, f, g = at.z + dz, (at.f + df) % at.nf, (at.g + dg) % at.ng
        place, target = at.index(z, f, g), self.block(number, z, f, g)
        moved = {"z": dz, "f": df, "g": dg}
        last = max([i for i, axis in enumerate(order) if moved[axis]], default=-1)

        def send(allowed, kind, device, pair=False):
            sem = (self.pair_sems if pair else self.plane_sems).at[number, place]
            start_copy(
                self.phase,
                both(condition, allowed),
                source,
                target,
                self.send_sems.at[number, place, kind],
                sem,
                device,
            )

        for i, axis in enumerate(order):
            if axis == "z" and i >= last:
                rising, sinking = dz <= 0, dz >= 0
                if rising:
                    send(at.z < LINE - 1, 0, at.device(at.z + 1, at.f, at.g))
                if sinking:
                    send(at.z > 0, 1, at.device(at.z - 1, at.f, at.g))
            if axis == "f" and i > last:
                for step in range(1, at.nf):
                    send(True, 1 + step, at.device(at.z, (at.f + step) % at.nf, at.g))
            if axis == "g" and i > last:
                for step in range(1, at.ng):
                    send(True, at.nf + step, at.device(at.z, at.f, (at.g + step) % at.ng))
        send(True, at.nf + at.ng, at.partner(), pair=True)

    def begin(self):
        at = self.at
        for number in range(len(self.sections)):
            self.forward(number, True, self.own(number), 0, 0, 0)
            own = pltpu.make_async_copy(
                self.own(number),
                self.block(number, at.z, at.f, at.g),
                self.pair_sems.at[number, at.blocks],
            )
            if self.phase.ending:
                own.wait()
            else:
                own.start()

    def arrival(self, number, dz, df, dg):
        at = self.at
        z, f, g = at.z + dz, (at.f + df) % at.nf, (at.g + dg) % at.ng
        condition = present(at, dz)
        block = self.block(number, z, f, g)
        sem = self.plane_sems.at[number, at.index(z, f, g)]
        if not self.phase.ending:
            when(condition, functools.partial(await_block, block, sem))
        self.forward(number, condition, block, dz, df, dg)

    def events(self):
        return [
            functools.partial(self.arrival, number, *item)
            for item in steps_of(self.at)[1:]
            for number in range(len(self.sections))
        ]

    def finish(self):
        for number in range(len(self.sections)):
            for place in range(self.at.blocks):
                await_block(self.block(number, 0, 0, 0), self.pair_sems.at[number, place])


def trade_in(at, source_ref, target_ref, send_sems, recv_sems, phase):
    slots, positions = source_ref.shape[0], source_ref.shape[1]
    group = at.seq_size // slots
    own_slot, own_part = at.seq // group, at.seq % group
    same = at.seq // slots == own_part
    lane = at.seq % slots
    target = target_ref.at[pl.ds(pl.multiple_of(lane * positions, positions), positions), :]
    for step in range(slots):
        slot = (own_slot + step) % slots
        if step == 0 and not phase.ending:
            local = pltpu.make_async_copy(source_ref.at[slot], target, recv_sems.at[lane])
            when(same, local.start)
        start_copy(
            phase,
            True if step else jnp.logical_not(same),
            source_ref.at[slot],
            target,
            send_sems.at[step],
            recv_sems.at[lane],
            (slot * group + at.seq // slots, at.y),
        )
        if phase.ending:
            await_block(target_ref.at[pl.ds(step * positions, positions), :], recv_sems.at[step])


def trade_out(at, source_ref, target_ref, send_sems, recv_sems, phase):
    slots, positions = target_ref.shape[0], target_ref.shape[1]
    group = at.seq_size // slots
    own_slot, own_part = at.seq // group, at.seq % group
    same = at.seq // slots == own_part
    target = target_ref.at[own_slot]
    for step in range(slots):
        lane = (at.seq + step) % slots
        source = source_ref.at[pl.ds(pl.multiple_of(lane * positions, positions), positions), :]
        if step == 0 and not phase.ending:
            local = pltpu.make_async_copy(source, target, recv_sems.at[own_slot])
            when(same, local.start)
        start_copy(
            phase,
            True if step else jnp.logical_not(same),
            source,
            target,
            send_sems.at[step],
            recv_sems.at[own_slot],
            (own_part * slots + lane, at.y),
        )
        if phase.ending:
            await_block(target_ref.at[step], recv_sems.at[step])


def first_kernel(sizes, *refs):
    at = Place(*sizes)
    weight_ref, gains_ref, hidden_ref, whole_ref, all_gains_ref, rows_ref = refs[:6]
    sems, (trade_send, trade_recv) = refs[6:9], refs[9:]
    peers, count = plane_peers(at)
    more, extra = slot_peers(at, hidden_ref.shape[0])
    meet(peers + more, count + extra)
    phase = Phase()
    sections = [
        (weight_ref, whole_ref, pl.ds(0, weight_ref.shape[1]), "zfg"),
        (gains_ref, all_gains_ref, pl.ds(0, gains_ref.shape[1]), "zfg"),
    ]
    gather = Gather(at, sections, sems, phase)
    events = gather.events()
    for phase.ending in (False, True):
        gather.begin()
        trade_in(at, hidden_ref, rows_ref, trade_send, trade_recv, phase)
        run_all(events)
    gather.finish()


def gather_first(weight, gains, hidden, seq_size, fsdp_size):
    slots, positions, model = hidden.shape
    nf, ng = seq_size // (2 * LINE), fsdp_size
    devices = seq_size * fsdp_size
    dma = pltpu.SemaphoreType.DMA
    return pl.pallas_call(
        functools.partial(first_kernel, (seq_size, fsdp_size)),
        out_shape=(
            jax.ShapeDtypeStruct((weight.shape[0] * devices, weight.shape[1]), BF16),
            jax.ShapeDtypeStruct((gains.shape[0] * devices, gains.shape[1]), BF16),
            jax.ShapeDtypeStruct((slots * positions, model), BF16),
        ),
        in_specs=[pl.BlockSpec(memory_space=pltpu.VMEM)] * 3,
        out_specs=[pl.BlockSpec(memory_space=pl.ANY)] * 3,
        scratch_shapes=Gather.scratch(2, nf, ng) + [dma((slots,)), dma((slots,))],
        compiler_params=pltpu.CompilerParams(collective_id=0, has_side_effects=True),
        name="gather_first",
    )(weight, gains, hidden)


def add_blocks(target, others, width):
    pieces = 5 if width % (5 * LANES) == 0 else 1
    piece = width // pieces

    def body(number, carry):
        columns = pl.ds(pl.multiple_of(number * piece, LANES), piece)
        total = target[:, columns].astype(F32)
        for other in others:
            total = total + other[:, columns].astype(F32)
        target[:, columns] = total.astype(target.dtype)
        return carry

    lax.fori_loop(0, pieces, body, 0)


def line_targets(at):
    order = []
    for dz in (-3, 3, -2, 2, -1, 1, 0):
        for df in list(range(1, at.nf)) + [0]:
            for dg in list(range(1, at.ng)) + [0]:
                order.append((dg == 0, df == 0, -abs(dz), dz, df, dg))
    order.sort(key=lambda item: item[:3])
    return [item[3:] for item in order]


class Phase:
    def __init__(self):
        self.ending = False


def start_copy(phase, condition, source, target, send_sem, recv_sem, device):
    copy = pltpu.make_async_remote_copy(
        src_ref=source,
        dst_ref=target,
        send_sem=send_sem,
        recv_sem=recv_sem,
        device_id=device,
        device_id_type=MESH,
    )
    when(condition, copy.wait_send if phase.ending else copy.start)


def run_all(events):
    for event in events:
        event()


def await_block(buffer, sem):
    pltpu.make_async_copy(buffer, buffer, sem).wait()


def scatter_scratch(nf, ng, rows, width):
    dma = pltpu.SemaphoreType.DMA
    blocks, beyond_g, beyond_f = LINE * nf * ng, (ng - 1) * LINE * nf, (nf - 1) * LINE
    counts = (blocks, blocks, beyond_g, beyond_f, LINE, LINE)
    buffers = [pltpu.VMEM((count, rows, width), BF16) for count in counts]
    sems = (blocks, blocks, blocks, beyond_g, beyond_g, beyond_f, beyond_f, LINE, LINE, LINE, LINE)
    return buffers + [dma((count,)) for count in sems]


SCATTER_SCRATCH = 17


def scatter_events(at, sources, owned, scratch, phase):
    acc, from_pair, from_g, from_f, from_below, from_above = scratch[:6]
    load_sems, pair_send, pair_recv, g_send, g_recv, f_send, f_recv = scratch[6:13]
    up_send, up_recv, down_send, down_recv = scratch[13:]
    rows, width = acc.shape[1], acc.shape[2]
    order = line_targets(at)
    other = 1 - at.core
    send = functools.partial(start_copy, phase)

    def where_is(dz, df, dg):
        return at.z + dz, (at.f + df) % at.nf, (at.g + dg) % at.ng

    def spans():
        start = 0
        for source in sources:
            yield source, pl.ds(start, source.shape[1])
            start += source.shape[1]

    def rows_of(source, z, f, g, core=None):
        start = pl.multiple_of(at.row_block(z, f, g, core) * rows, rows)
        return source.at[pl.ds(start, rows), :]

    def begin(dz, df, dg):
        z, f, g = where_is(dz, df, dg)
        condition = present(at, dz)
        place = at.index(z, f, g)
        pf, pg = at.split(*at.split(f, g, at.core), other)
        there = at.index(z, pf, pg)

        def body():
            if phase.ending:
                await_block(from_pair.at[there], pair_send.at[there])
                return
            for source, columns in spans():
                pltpu.make_async_copy(
                    rows_of(source, z, f, g), acc.at[place, :, columns], load_sems.at[place]
                ).start()
                pltpu.make_async_remote_copy(
                    src_ref=rows_of(source, z, pf, pg, other),
                    dst_ref=from_pair.at[there, :, columns],
                    send_sem=pair_send.at[there],
                    recv_sem=pair_recv.at[there],
                    device_id=at.partner(),
                    device_id_type=MESH,
                ).start()

        when(condition, body)

    def over_pair(dz, df, dg):
        z, f, g = where_is(dz, df, dg)
        condition = present(at, dz)
        place = at.index(z, f, g)

        def join():
            await_block(acc.at[place], load_sems.at[place])
            await_block(from_pair.at[place], pair_recv.at[place])
            add_blocks(acc.at[place], [from_pair.at[place]], width)

        if not phase.ending:
            when(condition, join)
        if dg:
            slot = (dg - 1) * LINE * at.nf + z * at.nf + f
            device = at.device(at.z, at.f, g)
            send(condition, acc.at[place], from_g.at[slot], g_send.at[slot], g_recv.at[slot], device)

    def over_g(dz, df):
        z, f, g = where_is(dz, df, 0)
        condition = present(at, dz)
        place = at.index(z, f, g)

        def join():
            parts = []
            for step in range(1, at.ng):
                slot = (step - 1) * LINE * at.nf + z * at.nf + f
                await_block(from_g.at[slot], g_recv.at[slot])
                parts.append(from_g.at[slot])
            add_blocks(acc.at[place], parts, width)

        if not phase.ending:
            when(condition, join)
        if df:
            slot = (df - 1) * LINE + z
            device = at.device(at.z, f, at.g)
            send(condition, acc.at[place], from_f.at[slot], f_send.at[slot], f_recv.at[slot], device)

    def over_f(dz):
        z = at.z + dz
        condition = present(at, dz)
        place = at.index(z, at.f, at.g)

        def join():
            parts = []
            for step in range(1, at.nf):
                slot = (step - 1) * LINE + z
                await_block(from_f.at[slot], f_recv.at[slot])
                parts.append(from_f.at[slot])
            add_blocks(acc.at[place], parts, width)

            def rise():
                await_block(from_below.at[z], up_recv.at[z])
                add_blocks(acc.at[place], [from_below.at[z]], width)

            def sink():
                await_block(from_above.at[z], down_recv.at[z])
                add_blocks(acc.at[place], [from_above.at[z]], width)

            if 0 <= dz < LINE - 1:
                pl.when(at.z > 0)(rise)
            if 1 - LINE < dz <= 0:
                pl.when(at.z < LINE - 1)(sink)

        if not phase.ending:
            when(condition, join)
        if dz > 0:
            device = at.device(at.z + 1, at.f, at.g)
            send(condition, acc.at[place], from_below.at[z], up_send.at[z], up_recv.at[z], device)
        elif dz < 0:
            device = at.device(at.z - 1, at.f, at.g)
            send(condition, acc.at[place], from_above.at[z], down_send.at[z], down_recv.at[z], device)

    def finish():
        place = at.index(at.z, at.f, at.g)
        start = 0
        for source, target in zip(sources, owned):
            size = source.shape[1]
            if target.shape[1] <= size:
                target[...] = acc[place, :, start : start + target.shape[1]].astype(F32)
            start += size

    part = functools.partial
    return (
        [part(begin, *item) for item in order],
        [part(over_pair, *item) for item in order],
        [part(over_g, *item[:2]) for item in order if item[2] == 0],
        [part(over_f, dz) for dz in (-3, 3, -2, 2, -1, 1, 0)],
        finish,
    )


def scatter_kernel(sizes, count, *refs):
    at = Place(*sizes)
    sources, refs = refs[:count], refs[count:]
    result_ref, input_ref, vector_ref = refs[:3]
    owned, refs = refs[3 : 3 + count], refs[3 + count :]
    out_ref, grad_ref, total_ref = refs[:3]
    scratch, refs = refs[3 : 3 + SCATTER_SCRATCH], refs[3 + SCATTER_SCRATCH :]
    sq_g, sq_f, sq_z, sq_c, trade_send, trade_recv, sq_send, sq_recv = refs
    slots, positions = out_ref.shape[0], out_ref.shape[1]
    group = at.seq_size // slots
    peers, number = plane_peers(at)
    more, extra = slot_peers(at, slots)
    meet(peers + more, number + extra)
    phase = Phase()
    send = functools.partial(start_copy, phase)
    begins, pairs, gs, fs, finish = scatter_events(at, sources, owned, scratch, phase)
    other = 1 - at.core

    def vectors_g():
        for step in range(1, at.ng):
            device = at.device(at.z, at.f, (at.g + step) % at.ng)
            send(True, sq_g.at[at.g], sq_g.at[at.g], sq_send.at[0, step], sq_recv.at[0, at.g], device)

    def vectors_f():
        for step in range(1, at.nf):
            device = at.device(at.z, (at.f + step) % at.nf, at.g)
            send(True, sq_f.at[at.f], sq_f.at[at.f], sq_send.at[1, step], sq_recv.at[1, at.f], device)

    def line_send(condition, held, kind):
        device = at.device(at.z - 1 if kind else at.z + 1, at.f, at.g)
        send(condition, sq_z.at[held], sq_z.at[held], sq_send.at[2 + kind, held], sq_recv.at[2, held], device)

    def vectors_line(distance):
        for kind, held in enumerate((at.z - distance, at.z + distance)):
            there = held < LINE if kind else held >= 0
            onward = at.z > 0 if kind else at.z < LINE - 1
            if distance and not phase.ending:
                when(
                    there,
                    functools.partial(await_block, sq_z.at[held], sq_recv.at[2, held]),
                )
            line_send(both(there, onward), held, kind)

    def vectors_pair():
        send(
            True,
            sq_c.at[at.core],
            sq_c.at[at.core],
            sq_send.at[4, 0],
            sq_recv.at[3, at.core],
            at.partner(),
        )

    run_all(begins)
    trade_out(at, result_ref, out_ref, trade_send.at[0], trade_recv.at[0], phase)
    trade_out(at, input_ref, grad_ref, trade_send.at[1], trade_recv.at[1], phase)
    sq_g[at.g] = vector_ref[...]
    vectors_g()
    run_all(pairs)
    for step in range(1, at.ng):
        peer = (at.g + step) % at.ng
        await_block(sq_g.at[peer], sq_recv.at[0, peer])
    total = sq_g[0]
    for number in range(1, at.ng):
        total = total + sq_g[number]
    sq_f[at.f] = total
    vectors_f()
    run_all(gs)
    for step in range(1, at.nf):
        peer = (at.f + step) % at.nf
        await_block(sq_f.at[peer], sq_recv.at[1, peer])
    total = sq_f[0]
    for number in range(1, at.nf):
        total = total + sq_f[number]
    sq_z[at.z] = total
    vectors_line(0)
    run_all(fs[:-1])
    for distance in range(1, LINE):
        vectors_line(distance)
    total = sq_z[0]
    for number in range(1, LINE):
        total = total + sq_z[number]
    sq_c[at.core] = total
    vectors_pair()
    fs[-1]()
    finish()
    await_block(sq_c.at[other], sq_recv.at[3, other])
    total_ref[...] = sq_c[0] + sq_c[1]

    phase.ending = True
    run_all(begins + pairs + gs + fs)
    trade_out(at, result_ref, out_ref, trade_send.at[0], trade_recv.at[0], phase)
    trade_out(at, input_ref, grad_ref, trade_send.at[1], trade_recv.at[1], phase)
    vectors_g()
    vectors_f()
    for distance in range(LINE):
        vectors_line(distance)
    vectors_pair()


def scatter_all(sources, result, input_grad, vectors, slots, seq_size, fsdp_size):
    rows = sources[0].shape[0] // (seq_size * fsdp_size)
    width = sum(source.shape[1] for source in sources)
    own_rows, model = result.shape
    positions = own_rows // slots
    nf, ng = seq_size // (2 * LINE), fsdp_size
    dma = pltpu.SemaphoreType.DMA
    widest = max(nf, ng, LINE)
    vmem = pl.BlockSpec(memory_space=pltpu.VMEM)
    count = len(sources)
    return pl.pallas_call(
        functools.partial(scatter_kernel, (seq_size, fsdp_size), count),
        out_shape=tuple(
            [jax.ShapeDtypeStruct((rows, source.shape[1]), F32) for source in sources]
            + [jax.ShapeDtypeStruct((slots, positions, model), BF16)] * 2
            + [jax.ShapeDtypeStruct(vectors.shape, F32)]
        ),
        in_specs=[pl.BlockSpec(memory_space=pl.ANY)] * count + [vmem] * 3,
        out_specs=[vmem] * (count + 3),
        scratch_shapes=scatter_scratch(nf, ng, rows, width)
        + [pltpu.VMEM((size, *vectors.shape), F32) for size in (ng, nf, LINE, 2)]
        + [dma((2, slots)), dma((2, slots)), dma((5, widest)), dma((4, widest))],
        compiler_params=pltpu.CompilerParams(
            collective_id=3, has_side_effects=True, vmem_limit_bytes=63_000_000
        ),
        name="scatter_all",
    )(*sources, result, input_grad, vectors)


def meet_group(at, group):
    base, part = (at.seq // group) * group, at.seq % group
    members = [base + (part + step) % group for step in range(1, group)]
    meet([(True, (member, at.y)) for member in members], group - 1)
    return part, members


def first_half(shape):
    lane = lax.broadcasted_iota(jnp.int32, shape, 1)
    return lane % 64 < 32


def turn(values, cosine, sine):
    half = first_half(values.shape)
    away = jnp.where(half, -pltpu.roll(values, 96, 1), pltpu.roll(values, 32, 1))
    return values * cosine + away * sine


def turn_back(grads, cosine, sine):
    half = first_half(grads.shape)
    moved = grads * sine
    away = jnp.where(half, pltpu.roll(moved, 96, 1), -pltpu.roll(moved, 32, 1))
    return grads * cosine + away


def sum_kernel(
    sizes, group, keys_ref, values_ref, cos_ref, sin_ref, out_ref, arrived, send_sems, recv_sems
):
    at = Place(*sizes)
    rows, width = out_ref.shape
    half = width // 2
    part, members = meet_group(at, group)
    waits = []
    for kind, parts_ref in enumerate((keys_ref, values_ref)):
        for step, member in enumerate(members):
            owner = (part + step + 1) % group
            copy = pltpu.make_async_remote_copy(
                src_ref=parts_ref.at[pl.ds(pl.multiple_of(owner * rows, rows), rows), :],
                dst_ref=arrived.at[kind, step],
                send_sem=send_sems.at[kind, step],
                recv_sem=recv_sems.at[kind, step],
                device_id=(member, at.y),
                device_id_type=MESH,
            )
            copy.start()
            waits.append(copy.wait_send)
    own = pl.ds(pl.multiple_of(part * rows, rows), rows)
    cosine, sine = cos_ref[...], sin_ref[...]
    for kind, parts_ref in enumerate((keys_ref, values_ref)):
        for step in range(group - 1):
            await_block(arrived.at[kind, step], recv_sems.at[kind, step])

        def body(number, carry, kind=kind, parts_ref=parts_ref):
            start = pl.multiple_of(number * LANES, LANES)
            total = parts_ref[own, pl.ds(start, LANES)].astype(F32)
            for step in range(group - 1):
                total = total + arrived[kind, step, :, pl.ds(start, LANES)].astype(F32)
            if kind == 0:
                total = turn_back(total, cosine, sine)
            target = pl.ds(pl.multiple_of(kind * half + number * LANES, LANES), LANES)
            out_ref[:, target] = total.astype(BF16)
            return carry

        lax.fori_loop(0, half // LANES, body, 0)
    for wait in waits:
        wait()


def sum_rows(keys, values, cosine, sine, group, seq_size, fsdp_size):
    rows, width = keys.shape[0] // group, keys.shape[1]
    dma = pltpu.SemaphoreType.DMA
    vmem = pl.BlockSpec(memory_space=pltpu.VMEM)
    return pl.pallas_call(
        functools.partial(sum_kernel, (seq_size, fsdp_size), group),
        out_shape=jax.ShapeDtypeStruct((rows, 2 * width), BF16),
        in_specs=[vmem] * 4,
        out_specs=vmem,
        scratch_shapes=[
            pltpu.VMEM((2, group - 1, rows, width), BF16),
            dma((2, group)),
            dma((2, group)),
        ],
        compiler_params=pltpu.CompilerParams(
            collective_id=2, has_side_effects=True, vmem_limit_bytes=63_000_000
        ),
        name="sum_rows",
    )(keys, values, cosine, sine)


def normalize(values):
    average = jnp.mean(values, axis=-1, keepdims=True)
    centered = values - average
    variance = jnp.mean(centered * centered, axis=-1, keepdims=True)
    inverse = lax.rsqrt(variance + EPS)
    return centered * inverse, inverse


def norm_back(grad_normed, normed, inverse, gain_values):
    scaled = grad_normed * gain_values
    first_mean = jnp.mean(scaled, axis=-1, keepdims=True)
    second_mean = jnp.mean(scaled * normed, axis=-1, keepdims=True)
    return inverse * (scaled - first_mean - normed * second_mean)


def head_lanes(shape, head):
    return lax.broadcasted_iota(jnp.int32, shape, 1) // 64 == head


def scores_of(keys, queries, bias):
    scores = lax.dot_general(keys, queries, (((1,), (1,)), ((), ())), preferred_element_type=F32)
    return scores + bias


def key_bias(length, shape):
    return jnp.where(lax.broadcasted_iota(jnp.int32, shape, 0) < length, 0.0, -jnp.inf)


def attend(length, queries, keys, values):
    queries = queries * 0.125
    bias = key_bias(length, (keys.shape[0], 1))
    zero = jnp.zeros((), BF16)
    total, logs = None, []
    for head in range(2):
        only = head_lanes(queries.shape, head)
        scores = scores_of(keys, jnp.where(only, queries, zero), bias)
        largest = jnp.max(scores, axis=0, keepdims=True)
        weights = jnp.exp(scores - largest)
        summed = jnp.sum(weights, axis=0, keepdims=True)
        logs.append(largest + jnp.log(summed))
        held = jnp.where(head_lanes(values.shape, head), values, zero)
        part = lax.dot_general(
            held, weights.astype(BF16), (((0,), (0,)), ((), ())), preferred_element_type=F32
        )
        part = part / summed
        total = part if total is None else total + part
    return total.T.astype(BF16), logs


FRONT_TILE = 512


def front_kernel(sizes, group, spans, *refs):
    at = Place(*sizes)
    count = len(spans)
    length_ref, x_ref, gains_ref, cos_ref, sin_ref, w_ref, dy_ref = refs[:7]
    sources, refs = refs[7 : 7 + count], refs[7 + count :]
    act_ref, gain_ref, q_ref, shared_out, o_ref, log_ref, dy_rows_ref = refs[:7]
    wholes, refs = refs[7 : 7 + count], refs[7 + count :]
    sems, (trade_send, trade_recv, share_send, share_recv, shared_ref, out_sem) = refs[:3], refs[3:]
    step = pl.program_id(0)
    rows, model = q_ref.shape
    slots = dy_ref.shape[0]
    tile = o_ref.shape[0]
    tiles = rows // tile
    projecting = 3 * model // FRONT_TILE
    steps = projecting + model // LANES * tiles
    kept = 2 * model // FRONT_TILE
    phase = Phase()
    sections = []
    for number, parts in enumerate(spans):
        start = 0
        for size, order in parts:
            sections.append((sources[number], wholes[number], pl.ds(start, size), order))
            start += size
    gather = Gather(at, sections, sems, phase)
    base, part = (at.seq // group) * group, at.seq % group
    members = [base + (part + other) % group for other in range(1, group)]
    own_rows = pl.ds(pl.multiple_of(part * rows, rows), rows)

    @pl.when(step == 0)
    def _():
        peers, number = plane_peers(at)
        more, extra = slot_peers(at, slots)
        others = [(True, (member, at.y)) for member in members]
        meet(peers + more + others, number + extra + group - 1)

    @pl.when(step == 0)
    def _():
        gather.begin()
        trade_in(at, dy_ref, dy_rows_ref, trade_send, trade_recv, phase)

    @pl.when(step == 0)
    def _():
        normed, _ = normalize(x_ref[...].astype(F32))
        turned = gains_ref[...].astype(F32).T
        gain_ref[...] = turned[:8]
        act_ref[...] = (normed * turned[:1]).astype(BF16)

    def share(number):
        place = shared_ref.at[own_rows, pl.ds(number * FRONT_TILE, FRONT_TILE)]
        for other, member in enumerate(members):
            start_copy(
                phase,
                True,
                place,
                place,
                share_send.at[number, other],
                share_recv.at[number, part],
                (member, at.y),
            )

    def receive():
        for number in range(kept):
            for other in range(1, group):
                source = (part + other) % group
                place = shared_ref.at[
                    pl.ds(pl.multiple_of(source * rows, rows), rows),
                    pl.ds(number * FRONT_TILE, FRONT_TILE),
                ]
                await_block(place, share_recv.at[number, source])
        pltpu.make_async_copy(shared_ref, shared_out, out_sem).start()

    for number in range(kept):
        pl.when(step == number + 1)(functools.partial(share, number))
    pl.when(step == projecting)(receive)

    @pl.when(step < projecting)
    def _():
        mixed = jnp.dot(act_ref[...], w_ref[...], preferred_element_type=F32)

        def turned():
            cosine, sine = cos_ref[...], sin_ref[...]
            pieces = [
                turn(mixed[:, start : start + LANES], cosine, sine).astype(BF16)
                for start in range(0, FRONT_TILE, LANES)
            ]
            return jnp.concatenate(pieces, axis=1)

        @pl.when(step < kept // 2)
        def _():
            columns = pl.ds(pl.multiple_of(step * FRONT_TILE, FRONT_TILE), FRONT_TILE)
            shared_ref[own_rows, columns] = turned()

        @pl.when(both(step >= kept // 2, step < kept))
        def _():
            columns = pl.ds(pl.multiple_of(step * FRONT_TILE, FRONT_TILE), FRONT_TILE)
            shared_ref[own_rows, columns] = mixed.astype(BF16)

        @pl.when(step >= kept)
        def _():
            columns = pl.ds(pl.multiple_of((step - kept) * FRONT_TILE, FRONT_TILE), FRONT_TILE)
            q_ref[:, columns] = turned()

    @pl.when(step >= projecting)
    def _():
        pair, piece = (step - projecting) // tiles, (step - projecting) % tiles
        start = pl.multiple_of(pair * LANES, LANES)
        out, logs = attend(
            length_ref[0],
            q_ref[pl.ds(pl.multiple_of(piece * tile, tile), tile), pl.ds(start, LANES)],
            shared_ref[:, pl.ds(start, LANES)],
            shared_ref[:, pl.ds(pl.multiple_of(model + start, LANES), LANES)],
        )
        o_ref[...] = out
        for head in range(2):
            log_ref[0, head : head + 1, :] = logs[head]

    events = gather.events()
    pace = FRONT_PACE
    for number in range(steps - 1):
        group_events = events[number * pace : (number + 1) * pace]
        if group_events:
            pl.when(step == number)(functools.partial(run_all, group_events))

    @pl.when(step == steps - 1)
    def _():
        run_all(events[(steps - 1) * pace :])
        phase.ending = True
        gather.begin()
        trade_in(at, dy_ref, dy_rows_ref, trade_send, trade_recv, phase)
        run_all(events)
        for number in range(kept):
            share(number)
        gather.finish()
        pltpu.make_async_copy(shared_ref, shared_out, out_sem).wait()
        phase.ending = False


FRONT_PACE = 2


def front(length, x_rows, gains, cosine, sine, weight, dy, sources, spans, group, tile, seq_size, fsdp_size):
    rows, model = x_rows.shape
    slots, positions, _ = dy.shape
    pairs, tiles = model // LANES, rows // tile
    projecting, kept = 3 * model // FRONT_TILE, 2 * model // FRONT_TILE
    nf, ng = seq_size // (2 * LINE), fsdp_size
    devices = seq_size * fsdp_size
    count = sum(len(parts) for parts in spans)
    dma = pltpu.SemaphoreType.DMA
    vmem, anywhere = pl.BlockSpec(memory_space=pltpu.VMEM), pl.BlockSpec(memory_space=pl.ANY)

    def pair_of(i):
        return jnp.maximum(i - projecting, 0) // tiles

    def tile_of(i):
        return jnp.maximum(i - projecting, 0) % tiles

    return pl.pallas_call(
        functools.partial(front_kernel, (seq_size, fsdp_size), group, spans),
        grid=(projecting + pairs * tiles,),
        out_shape=tuple(
            [
                jax.ShapeDtypeStruct((rows, model), BF16),
                jax.ShapeDtypeStruct((8, model), F32),
                jax.ShapeDtypeStruct((rows, model), BF16),
                jax.ShapeDtypeStruct((rows * group, 2 * model), BF16),
                jax.ShapeDtypeStruct((rows, model), BF16),
                jax.ShapeDtypeStruct((pairs, 8, rows), F32),
                jax.ShapeDtypeStruct((slots * positions, model), BF16),
            ]
            + [
                jax.ShapeDtypeStruct((source.shape[0] * devices, source.shape[1]), BF16)
                for source in sources
            ]
        ),
        in_specs=[pl.BlockSpec(memory_space=pltpu.SMEM), vmem, vmem, vmem, vmem]
        + [
            pl.BlockSpec(
                (model, FRONT_TILE),
                lambda i: (0, (jnp.minimum(i, projecting - 1) + projecting - kept) % projecting),
            )
        ]
        + [vmem] * (1 + len(sources)),
        out_specs=[
            vmem,
            vmem,
            vmem,
            anywhere,
            pl.BlockSpec((tile, LANES), lambda i: (tile_of(i), pair_of(i))),
            pl.BlockSpec((1, 8, tile), lambda i: (pair_of(i), 0, tile_of(i))),
        ]
        + [anywhere] * (1 + len(sources)),
        scratch_shapes=Gather.scratch(count, nf, ng)
        + [dma((slots,)), dma((slots,)), dma((kept, group)), dma((kept, group))]
        + [pltpu.VMEM((rows * group, 2 * model), BF16), dma],
        compiler_params=pltpu.CompilerParams(
            collective_id=1, has_side_effects=True, vmem_limit_bytes=63_000_000
        ),
        name="front",
    )(length, x_rows, gains, cosine, sine, weight, dy, *sources)


def attend_back_kernel(
    length_ref,
    q_ref,
    k_ref,
    v_ref,
    g_ref,
    o_ref,
    log_ref,
    cos_ref,
    sin_ref,
    dq_ref,
    dk_ref,
    dv_ref,
    dk_acc,
    dv_acc,
):
    step = pl.program_id(1)
    keys, values, queries = k_ref[...], v_ref[...], q_ref[...] * 0.125
    grads = g_ref[...]
    bias = key_bias(length_ref[0], (keys.shape[0], 1))
    zero = jnp.zeros((), BF16)
    product = (grads.astype(F32) * o_ref[...].astype(F32)).T
    dq = dk = dv = None
    for head in range(2):
        only = head_lanes(queries.shape, head)
        query = jnp.where(only, queries, zero)
        grad = jnp.where(only, grads, zero)
        key = jnp.where(head_lanes(keys.shape, head), keys, zero)
        delta = jnp.sum(product[64 * head : 64 * head + 64], axis=0, keepdims=True)
        scores = scores_of(keys, query, bias)
        probs = jnp.exp(scores - log_ref[0, head : head + 1, :])
        grad_probs = lax.dot_general(
            values, grad, (((1,), (1,)), ((), ())), preferred_element_type=F32
        )
        grad_scores = (probs * (grad_probs - delta)).astype(BF16)
        value_part = jnp.dot(probs.astype(BF16), grad, preferred_element_type=F32)
        key_part = jnp.dot(grad_scores, query, preferred_element_type=F32)
        query_part = lax.dot_general(
            key, grad_scores, (((0,), (0,)), ((), ())), preferred_element_type=F32
        )
        dq = query_part if dq is None else dq + query_part
        dk = key_part if dk is None else dk + key_part
        dv = value_part if dv is None else dv + value_part
    dq_ref[...] = turn_back(dq.T * 0.125, cos_ref[...], sin_ref[...]).astype(BF16)

    @pl.when(step == 0)
    def _():
        dk_acc[...] = dk
        dv_acc[...] = dv

    @pl.when(step > 0)
    def _():
        dk_acc[...] += dk
        dv_acc[...] += dv

    @pl.when(step == pl.num_programs(1) - 1)
    def _():
        dk_ref[...] = dk_acc[...].astype(BF16)
        dv_ref[...] = dv_acc[...].astype(BF16)


def attend_back(lengths, queries, shared, grads, heads_out, logs, cosine, sine, model, tile):
    rows, keys = queries.shape[0], shared.shape[0]
    pairs = model // LANES
    by_row = pl.BlockSpec((tile, LANES), lambda p, i: (i, p))
    by_key = pl.BlockSpec((keys, LANES), lambda p, i: (0, p))
    table = pl.BlockSpec((tile, LANES), lambda p, i: (i, 0))
    return pl.pallas_call(
        attend_back_kernel,
        grid=(pairs, rows // tile),
        out_shape=(
            jax.ShapeDtypeStruct((rows, model), BF16),
            jax.ShapeDtypeStruct((keys, model), BF16),
            jax.ShapeDtypeStruct((keys, model), BF16),
        ),
        in_specs=[
            pl.BlockSpec(memory_space=pltpu.SMEM),
            by_row,
            by_key,
            pl.BlockSpec((keys, LANES), lambda p, i: (0, pairs + p)),
            by_row,
            by_row,
            pl.BlockSpec((1, 8, tile), lambda p, i: (p, 0, i)),
            table,
            table,
        ],
        out_specs=(by_row, by_key, by_key),
        scratch_shapes=[pltpu.VMEM((keys, LANES), F32), pltpu.VMEM((keys, LANES), F32)],
        name="attend_back",
    )(lengths, queries, shared, shared, grads, heads_out, logs, cosine, sine)


def rotary_tables(places, head_size):
    halfway = head_size // 2
    ladder = jnp.arange(halfway, dtype=F32) * (2.0 / head_size)
    inverse = 1.0 / THETA**ladder
    angles = places.astype(F32)[:, None] * inverse[None, :]
    angles = jnp.concatenate([angles] * 4, axis=-1)
    return jnp.cos(angles), jnp.sin(angles)


def gelu_exact(values):
    return jax.nn.gelu(values, approximate=False)


def mm(left, right):
    return jnp.dot(left, right, preferred_element_type=F32)


def mm_right_t(left, right):
    return lax.dot_general(left, right, (((1,), (1,)), ((), ())), preferred_element_type=F32)


def mm_left_t(left, right):
    return lax.dot_general(left, right, (((0,), (0,)), ((), ())), preferred_element_type=F32)


def shards(
    hidden_in,
    out_grad,
    qkv_weight,
    attn_out_weight,
    in_weight,
    down_weight,
    attn_gain,
    mlp_gain,
    seq_lengths,
    slot_order,
):
    seq_size, fsdp_size = lax.axis_size("seq"), lax.axis_size("fsdp")
    seq_place, fsdp_place = lax.axis_index("seq"), lax.axis_index("fsdp")
    slots, positions, model = hidden_in.shape
    shard = qkv_weight.shape[0]
    ff = down_weight.shape[0]
    wide = up_to(ff, LANES)
    spare = wide - ff
    group = seq_size // slots
    rows = slots * positions
    head_size = model // HEADS

    lead = jnp.zeros((shard, spare), BF16)
    gains = jnp.concatenate(
        [attn_gain[:, None], mlp_gain[:, None], jnp.zeros((shard, LANES - 2), BF16)], axis=1
    )
    in_pack = jnp.concatenate([in_weight[:, :ff], lead, in_weight[:, ff:], lead], axis=1)
    down_pack = jnp.concatenate([down_weight.T, lead], axis=1)
    w_qkv, all_gains, x_rows = gather_first(qkv_weight, gains, hidden_in, seq_size, fsdp_size)

    slot = fsdp_place * slots + seq_place // group
    order = jnp.sum(jnp.where(jnp.arange(slot_order.shape[0]) == slot, slot_order, 0))
    length = jnp.sum(jnp.where(jnp.arange(seq_lengths.shape[0]) == order, seq_lengths, 0))
    lengths = length.astype(jnp.int32)[None]
    places = (seq_place % group) * rows + jnp.arange(rows, dtype=jnp.int32)
    valid = (places < length).astype(F32)[:, None]
    cosine, sine = rotary_tables(places, head_size)

    tile = 512 if rows % 512 == 0 and rows * group <= 1024 else 128
    act_one, gain_rows, queries, shared, heads_out, logs, dy_rows, w_attn, w_input, w_down = front(
        lengths,
        x_rows,
        all_gains,
        cosine,
        sine,
        w_qkv,
        out_grad,
        (attn_out_weight, in_pack, down_pack),
        (((model, "fzg"),), ((wide, "zfg"), (wide, "zfg")), ((wide, "fzg"),)),
        group,
        tile,
        seq_size,
        fsdp_size,
    )
    gain_attn, gain_mlp = gain_rows[0:1], gain_rows[1:2]

    x_wide = x_rows.astype(F32)
    attn = mm(heads_out, w_attn)
    middle = x_wide + attn
    normed_two, inverse_two = normalize(middle)
    act_two = (normed_two * gain_mlp).astype(BF16)
    joined = mm(act_two, w_input)
    input_half = joined[:, :wide]
    gate_half = joined[:, wide:]
    active, active_pull = jax.vjp(gelu_exact, input_half)
    product = (active * gate_half).astype(BF16)
    branch = mm_right_t(product, w_down)
    result = (middle + branch) * valid
    squares = [
        jnp.sum(valid * tensor * tensor, axis=0) for tensor in (x_wide, middle, result, attn, branch)
    ]

    grad_y = dy_rows.astype(F32) * valid
    grad_branch = grad_y.astype(BF16)
    down_part = mm_left_t(grad_branch, product).astype(BF16)
    grad_product = mm(grad_branch, w_down)
    grad_joined = jnp.concatenate(
        [active_pull(grad_product * gate_half)[0], grad_product * active], axis=1
    ).astype(BF16)
    input_part = mm_left_t(act_two, grad_joined).astype(BF16)
    grad_act_two = mm_right_t(grad_joined, w_input)
    mlp_gain_part = jnp.sum(grad_act_two * normed_two, axis=0)
    grad_middle = grad_y + norm_back(grad_act_two, normed_two, inverse_two, gain_mlp)
    grad_attn = grad_middle.astype(BF16)
    attn_part = mm_left_t(heads_out, grad_attn).astype(BF16)
    grad_heads = mm_right_t(grad_attn, w_attn).astype(BF16)

    grad_q, grad_k, grad_v = attend_back(
        lengths, queries, shared, grad_heads, heads_out, logs, cosine, sine, model, tile
    )
    grad_kv = sum_rows(grad_k, grad_v, cosine, sine, group, seq_size, fsdp_size)
    grad_mixed = jnp.concatenate([grad_q, grad_kv], axis=1)
    qkv_part = mm_left_t(act_one, grad_mixed).astype(BF16)
    grad_act_one = mm_right_t(grad_mixed, w_qkv)
    normed_one, inverse_one = normalize(x_wide)
    attn_gain_part = jnp.sum(grad_act_one * normed_one, axis=0)
    grad_x = grad_middle + norm_back(grad_act_one, normed_one, inverse_one, gain_attn)

    vectors = jnp.stack(squares + [attn_gain_part, mlp_gain_part, jnp.zeros((model,), F32)])
    own_qkv, own_attn, own_in, own_down, out_rows, grad_rows, totals = scatter_all(
        [qkv_part, attn_part, input_part, down_part],
        result.astype(BF16),
        grad_x.astype(BF16),
        vectors,
        slots,
        seq_size,
        fsdp_size,
    )
    tokens_valid = jnp.sum(seq_lengths).astype(F32)
    root_squares = jnp.sqrt(jnp.sum(totals[:5], axis=1) / (tokens_valid * model))
    own_gains = lax.dynamic_slice_in_dim(totals, (seq_place * fsdp_size + fsdp_place) * shard, shard, 1)
    return (
        out_rows,
        grad_rows,
        own_qkv,
        own_attn,
        jnp.concatenate([own_in[:, :ff], own_in[:, wide : wide + ff]], axis=1),
        own_down[:, :ff].T,
        own_gains[5],
        own_gains[6],
        root_squares,
    )


def solution(mesh):
    placed = (
        P("fsdp", "seq", None),
        P("fsdp", "seq", None),
        P(("seq", "fsdp"), None),
        P(("seq", "fsdp"), None),
        P(("seq", "fsdp"), None),
        P(None, ("seq", "fsdp")),
        P(("seq", "fsdp")),
        P(("seq", "fsdp")),
        P(),
        P(),
    )
    return jax.shard_map(
        shards,
        mesh=mesh,
        in_specs=placed,
        out_specs=(
            P("fsdp", "seq", None),
            P("fsdp", "seq", None),
            P(("seq", "fsdp"), None),
            P(("seq", "fsdp"), None),
            P(("seq", "fsdp"), None),
            P(None, ("seq", "fsdp")),
            P(("seq", "fsdp")),
            P(("seq", "fsdp")),
            P(),
        ),
        check_vma=False,
    )
```

```python
import functools

import jax
import jax.numpy as jnp
from jax import lax
from jax.experimental import pallas as pl
from jax.experimental.pallas import tpu as pltpu
from jax.sharding import PartitionSpec as P

HEADS = 16
LINE = 4
LANES = 128
EPS = 1e-05
THETA = 160000.0
F32 = jnp.float32
BF16 = jnp.bfloat16
MESH = pl.DeviceIdType.MESH


def up_to(size, unit):
    return -(-size // unit) * unit


class Place:
    def __init__(self, seq_size, fsdp_size):
        self.seq_size, self.fsdp_size = seq_size, fsdp_size
        self.rest = seq_size // (2 * LINE)
        self.swap = self.rest == fsdp_size
        self.nf, self.ng = self.rest, fsdp_size
        self.blocks = LINE * self.nf * self.ng
        self.seq = lax.axis_index("seq")
        self.y = lax.axis_index("fsdp")
        self.core = self.seq % 2
        self.r = (self.seq // 2) % self.rest
        self.z = self.seq // (2 * self.rest)
        self.f, self.g = self.split(self.r, self.y, self.core)

    def split(self, r, y, core):
        if not self.swap:
            return r, y
        return (1 - core) * r + core * y, (1 - core) * y + core * r

    def device(self, z, f, g, core=None):
        core = self.core if core is None else core
        r, y = self.split(f, g, core)
        return (z * self.rest + r) * 2 + core, y

    def row_block(self, z, f, g, core=None):
        seq, y = self.device(z, f, g, core)
        return seq * self.fsdp_size + y

    def index(self, z, f, g):
        return (z * self.nf + f) * self.ng + g

    def partner(self):
        return self.seq + 1 - 2 * self.core, self.y


def both(first, second):
    if first is True:
        return second
    if second is True:
        return first
    return jnp.logical_and(first, second)


def when(condition, body):
    if condition is True:
        body()
    else:
        pl.when(condition)(body)


def meet(peers, awaited):
    barrier = pltpu.get_barrier_semaphore()
    for condition, device in peers:
        when(
            condition,
            functools.partial(
                pl.semaphore_signal, barrier, inc=1, device_id=device, device_id_type=MESH
            ),
        )
    pl.semaphore_wait(barrier, awaited)


def plane_peers(at):
    below, above = at.z > 0, at.z < LINE - 1
    peers = [
        (below, at.device(at.z - 1, at.f, at.g)),
        (above, at.device(at.z + 1, at.f, at.g)),
        (True, at.partner()),
    ]
    for step in range(1, at.nf):
        peers.append((True, at.device(at.z, (at.f + step) % at.nf, at.g)))
    for step in range(1, at.ng):
        peers.append((True, at.device(at.z, at.f, (at.g + step) % at.ng)))
    count = 1 + (at.nf - 1) + (at.ng - 1)
    count = count + jnp.where(below, 1, 0) + jnp.where(above, 1, 0)
    return peers, count


def slot_peers(at, slots):
    group = at.seq_size // slots
    own_slot, own_part = at.seq // group, at.seq % group
    same = at.seq // slots == own_part
    peers = []
    for step in range(slots):
        wide = ((own_slot + step) % slots) * group + at.seq // slots
        narrow = own_part * slots + (at.seq + step) % slots
        condition = True if step else jnp.logical_not(same)
        peers.append((condition, (wide, at.y)))
        peers.append((condition, (narrow, at.y)))
    return peers, 2 * slots - 2 * jnp.where(same, 1, 0)


def steps_of(at):
    out = []
    for dz in (0, -1, 1, -2, 2, -3, 3):
        for df in range(at.nf):
            for dg in range(at.ng):
                out.append((abs(dz) + (df > 0) + (dg > 0), dz, df, dg))
    out.sort(key=lambda item: item[0])
    return [item[1:] for item in out]


def present(at, dz):
    if dz == 0:
        return True
    return at.z + dz >= 0 if dz < 0 else at.z + dz < LINE


class Gather:
    def __init__(self, at, sections, sems, phase):
        self.at, self.sections, self.phase = at, sections, phase
        self.send_sems, self.plane_sems, self.pair_sems = sems

    @staticmethod
    def scratch(count, nf, ng):
        dma = pltpu.SemaphoreType.DMA
        blocks, kinds = LINE * nf * ng, 3 + (nf - 1) + (ng - 1)
        return [dma((count, blocks, kinds)), dma((count, blocks)), dma((count, blocks + 1))]

    def own(self, number):
        source, _, columns, _ = self.sections[number]
        return source.at[:, columns]

    def block(self, number, z, f, g):
        source, whole, columns, _ = self.sections[number]
        rows = source.shape[0]
        start = pl.multiple_of(self.at.row_block(z, f, g) * rows, rows)
        return whole.at[pl.ds(start, rows), columns]

    def forward(self, number, condition, source, dz, df, dg):
        at, order = self.at, self.sections[number][3]
        z, f, g = at.z + dz, (at.f + df) % at.nf, (at.g + dg) % at.ng
        place, target = at.index(z, f, g), self.block(number, z, f, g)
        moved = {"z": dz, "f": df, "g": dg}
        last = max([i for i, axis in enumerate(order) if moved[axis]], default=-1)

        def send(allowed, kind, device, pair=False):
            sem = (self.pair_sems if pair else self.plane_sems).at[number, place]
            start_copy(
                self.phase,
                both(condition, allowed),
                source,
                target,
                self.send_sems.at[number, place, kind],
                sem,
                device,
            )

        for i, axis in enumerate(order):
            if axis == "z" and i >= last:
                rising, sinking = dz <= 0, dz >= 0
                if rising:
                    send(at.z < LINE - 1, 0, at.device(at.z + 1, at.f, at.g))
                if sinking:
                    send(at.z > 0, 1, at.device(at.z - 1, at.f, at.g))
            if axis == "f" and i > last:
                for step in range(1, at.nf):
                    send(True, 1 + step, at.device(at.z, (at.f + step) % at.nf, at.g))
            if axis == "g" and i > last:
                for step in range(1, at.ng):
                    send(True, at.nf + step, at.device(at.z, at.f, (at.g + step) % at.ng))
        send(True, at.nf + at.ng, at.partner(), pair=True)

    def begin(self):
        at = self.at
        for number in range(len(self.sections)):
            self.forward(number, True, self.own(number), 0, 0, 0)
            own = pltpu.make_async_copy(
                self.own(number),
                self.block(number, at.z, at.f, at.g),
                self.pair_sems.at[number, at.blocks],
            )
            if self.phase.ending:
                own.wait()
            else:
                own.start()

    def arrival(self, number, dz, df, dg):
        at = self.at
        z, f, g = at.z + dz, (at.f + df) % at.nf, (at.g + dg) % at.ng
        condition = present(at, dz)
        block = self.block(number, z, f, g)
        sem = self.plane_sems.at[number, at.index(z, f, g)]
        if not self.phase.ending:
            when(condition, functools.partial(await_block, block, sem))
        self.forward(number, condition, block, dz, df, dg)

    def events(self):
        return [
            functools.partial(self.arrival, number, *item)
            for item in steps_of(self.at)[1:]
            for number in range(len(self.sections))
        ]

    def finish(self):
        for number in range(len(self.sections)):
            for place in range(self.at.blocks):
                await_block(self.block(number, 0, 0, 0), self.pair_sems.at[number, place])


def trade_in(at, source_ref, target_ref, send_sems, recv_sems, phase):
    slots, positions = source_ref.shape[0], source_ref.shape[1]
    group = at.seq_size // slots
    own_slot, own_part = at.seq // group, at.seq % group
    same = at.seq // slots == own_part
    lane = at.seq % slots
    target = target_ref.at[pl.ds(pl.multiple_of(lane * positions, positions), positions), :]
    for step in range(slots):
        slot = (own_slot + step) % slots
        if step == 0 and not phase.ending:
            local = pltpu.make_async_copy(source_ref.at[slot], target, recv_sems.at[lane])
            when(same, local.start)
        start_copy(
            phase,
            True if step else jnp.logical_not(same),
            source_ref.at[slot],
            target,
            send_sems.at[step],
            recv_sems.at[lane],
            (slot * group + at.seq // slots, at.y),
        )
        if phase.ending:
            await_block(target_ref.at[pl.ds(step * positions, positions), :], recv_sems.at[step])


def trade_out(at, source_ref, target_ref, send_sems, recv_sems, phase):
    slots, positions = target_ref.shape[0], target_ref.shape[1]
    group = at.seq_size // slots
    own_slot, own_part = at.seq // group, at.seq % group
    same = at.seq // slots == own_part
    target = target_ref.at[own_slot]
    for step in range(slots):
        lane = (at.seq + step) % slots
        source = source_ref.at[pl.ds(pl.multiple_of(lane * positions, positions), positions), :]
        if step == 0 and not phase.ending:
            local = pltpu.make_async_copy(source, target, recv_sems.at[own_slot])
            when(same, local.start)
        start_copy(
            phase,
            True if step else jnp.logical_not(same),
            source,
            target,
            send_sems.at[step],
            recv_sems.at[own_slot],
            (own_part * slots + lane, at.y),
        )
        if phase.ending:
            await_block(target_ref.at[step], recv_sems.at[step])


def first_kernel(sizes, *refs):
    at = Place(*sizes)
    weight_ref, gains_ref, hidden_ref, whole_ref, all_gains_ref, rows_ref = refs[:6]
    sems, (trade_send, trade_recv) = refs[6:9], refs[9:]
    peers, count = plane_peers(at)
    more, extra = slot_peers(at, hidden_ref.shape[0])
    meet(peers + more, count + extra)
    phase = Phase()
    sections = [
        (weight_ref, whole_ref, pl.ds(0, weight_ref.shape[1]), "zfg"),
        (gains_ref, all_gains_ref, pl.ds(0, gains_ref.shape[1]), "zfg"),
    ]
    gather = Gather(at, sections, sems, phase)
    events = gather.events()
    for phase.ending in (False, True):
        gather.begin()
        trade_in(at, hidden_ref, rows_ref, trade_send, trade_recv, phase)
        run_all(events)
    gather.finish()


def gather_first(weight, gains, hidden, seq_size, fsdp_size):
    slots, positions, model = hidden.shape
    nf, ng = seq_size // (2 * LINE), fsdp_size
    devices = seq_size * fsdp_size
    dma = pltpu.SemaphoreType.DMA
    return pl.pallas_call(
        functools.partial(first_kernel, (seq_size, fsdp_size)),
        out_shape=(
            jax.ShapeDtypeStruct((weight.shape[0] * devices, weight.shape[1]), BF16),
            jax.ShapeDtypeStruct((gains.shape[0] * devices, gains.shape[1]), BF16),
            jax.ShapeDtypeStruct((slots * positions, model), BF16),
        ),
        in_specs=[pl.BlockSpec(memory_space=pltpu.VMEM)] * 3,
        out_specs=[pl.BlockSpec(memory_space=pl.ANY)] * 3,
        scratch_shapes=Gather.scratch(2, nf, ng) + [dma((slots,)), dma((slots,))],
        compiler_params=pltpu.CompilerParams(collective_id=0, has_side_effects=True),
        name="gather_first",
    )(weight, gains, hidden)


def add_blocks(target, others):
    width = target.shape[1]
    piece = next(size for size in (512, 384, 256, LANES) if width % size == 0)

    def body(number, carry):
        columns = pl.ds(pl.multiple_of(number * piece, LANES), piece)
        total = target[:, columns].astype(F32)
        for other in others:
            total = total + other[:, columns].astype(F32)
        target[:, columns] = total.astype(target.dtype)
        return carry

    lax.fori_loop(0, width // piece, body, 0)


def line_targets(at):
    order = []
    for dz in (-3, 3, -2, 2, -1, 1, 0):
        for df in list(range(1, at.nf)) + [0]:
            for dg in list(range(1, at.ng)) + [0]:
                order.append((dg == 0, df == 0, -abs(dz), dz, df, dg))
    order.sort(key=lambda item: item[:3])
    return [item[3:] for item in order]


class Phase:
    def __init__(self):
        self.ending = False


def start_copy(phase, condition, source, target, send_sem, recv_sem, device):
    copy = pltpu.make_async_remote_copy(
        src_ref=source,
        dst_ref=target,
        send_sem=send_sem,
        recv_sem=recv_sem,
        device_id=device,
        device_id_type=MESH,
    )
    when(condition, copy.wait_send if phase.ending else copy.start)


def run_all(events):
    for event in events:
        event()


def await_block(buffer, sem):
    pltpu.make_async_copy(buffer, buffer, sem).wait()


class Scatter:
    PARTS = 17

    @staticmethod
    def scratch(order, rows, width, nf, ng):
        dma = pltpu.SemaphoreType.DMA
        plane, beyond_g = LINE * nf * ng, (ng - 1) * LINE * nf
        beyond_f = (nf - 1) * (LINE if order == "fz" else 1)
        line = LINE * (1 if order == "fz" else nf)
        counts = (plane, plane, beyond_g, beyond_f, line, line)
        buffers = [pltpu.VMEM((count, rows, width), BF16) for count in counts]
        sems = (plane, plane, plane, beyond_g, beyond_g, beyond_f, beyond_f, line, line, line, line)
        return buffers + [dma((count,)) for count in sems]

    def __init__(self, at, source, columns, order, scratch, phase):
        self.at, self.source, self.columns, self.order = at, source, columns, order
        self.phase = phase
        self.acc, self.from_pair, self.from_g, self.from_f = scratch[:4]
        self.from_below, self.from_above = scratch[4:6]
        self.load_sems, self.pair_send, self.pair_recv = scratch[6:9]
        self.g_send, self.g_recv, self.f_send, self.f_recv = scratch[9:13]
        self.up_send, self.up_recv, self.down_send, self.down_recv = scratch[13:]
        self.rows = self.acc.shape[1]

    def where_is(self, dz, df, dg):
        at = self.at
        return at.z + dz, (at.f + df) % at.nf, (at.g + dg) % at.ng

    def rows_of(self, z, f, g, core=None):
        start = pl.multiple_of(self.at.row_block(z, f, g, core) * self.rows, self.rows)
        return self.source.at[pl.ds(start, self.rows), self.columns]

    def begin(self, dz, df, dg):
        at = self.at
        z, f, g = self.where_is(dz, df, dg)
        place, other = at.index(z, f, g), 1 - at.core
        pf, pg = at.split(*at.split(f, g, at.core), other)
        there = at.index(z, pf, pg)

        def body():
            if self.phase.ending:
                await_block(self.from_pair.at[there], self.pair_send.at[there])
                return
            pltpu.make_async_copy(
                self.rows_of(z, f, g), self.acc.at[place], self.load_sems.at[place]
            ).start()
            pltpu.make_async_remote_copy(
                src_ref=self.rows_of(z, pf, pg, other),
                dst_ref=self.from_pair.at[there],
                send_sem=self.pair_send.at[there],
                recv_sem=self.pair_recv.at[there],
                device_id=at.partner(),
                device_id_type=MESH,
            ).start()

        when(present(at, dz), body)

    def join(self, condition, place, parts):
        if self.phase.ending:
            return

        def body():
            ready = [(buffer, sem) for allowed, buffer, sem in parts if allowed is True]
            for buffer, sem in ready:
                await_block(buffer, sem)
            if ready:
                add_blocks(self.acc.at[place], [buffer for buffer, _ in ready])
            for allowed, buffer, sem in parts:
                if allowed is not True:

                    def more(buffer=buffer, sem=sem):
                        await_block(buffer, sem)
                        add_blocks(self.acc.at[place], [buffer])

                    pl.when(allowed)(more)

        when(condition, body)

    def over_pair(self, dz, df, dg):
        at = self.at
        z, f, g = self.where_is(dz, df, dg)
        condition = present(at, dz)
        place = at.index(z, f, g)
        if not self.phase.ending:
            when(
                condition,
                functools.partial(await_block, self.acc.at[place], self.load_sems.at[place]),
            )
        self.join(condition, place, [(True, self.from_pair.at[place], self.pair_recv.at[place])])
        if dg:
            slot = (dg - 1) * LINE * at.nf + z * at.nf + f
            start_copy(
                self.phase,
                condition,
                self.acc.at[place],
                self.from_g.at[slot],
                self.g_send.at[slot],
                self.g_recv.at[slot],
                at.device(at.z, at.f, g),
            )

    def g_parts(self, z, f):
        slots = [(step - 1) * LINE * self.at.nf + z * self.at.nf + f for step in range(1, self.at.ng)]
        return [(True, self.from_g.at[slot], self.g_recv.at[slot]) for slot in slots]

    def f_slot(self, z, step):
        return (step - 1) * LINE + z if self.order == "fz" else step - 1

    def f_parts(self, z):
        slots = [self.f_slot(z, step) for step in range(1, self.at.nf)]
        return [(True, self.from_f.at[slot], self.f_recv.at[slot]) for slot in slots]

    def line_slot(self, z, f):
        return z if self.order == "fz" else z * self.at.nf + f

    def line_parts(self, dz, z, f):
        slot, parts = self.line_slot(z, f), []
        if 0 <= dz < LINE - 1:
            parts.append((self.at.z > 0, self.from_below.at[slot], self.up_recv.at[slot]))
        if 1 - LINE < dz <= 0:
            parts.append((self.at.z < LINE - 1, self.from_above.at[slot], self.down_recv.at[slot]))
        return parts

    def send_f(self, condition, df, z, f, place):
        slot = self.f_slot(z, df)
        start_copy(
            self.phase,
            condition,
            self.acc.at[place],
            self.from_f.at[slot],
            self.f_send.at[slot],
            self.f_recv.at[slot],
            self.at.device(self.at.z, f, self.at.g),
        )

    def send_line(self, condition, dz, z, f, place):
        slot = self.line_slot(z, f)
        rising = dz > 0
        start_copy(
            self.phase,
            condition,
            self.acc.at[place],
            (self.from_below if rising else self.from_above).at[slot],
            (self.up_send if rising else self.down_send).at[slot],
            (self.up_recv if rising else self.down_recv).at[slot],
            self.at.device(self.at.z + (1 if rising else -1), self.at.f, self.at.g),
        )

    def second(self, dz, df):
        z, f, _ = self.where_is(dz, df, 0)
        condition = present(self.at, dz)
        place = self.at.index(z, f, self.at.g)
        parts = self.g_parts(z, f)
        if self.order == "zf":
            parts = parts + self.line_parts(dz, z, f)
        self.join(condition, place, parts)
        if self.order == "zf" and dz:
            self.send_line(condition, dz, z, f, place)
        elif df:
            self.send_f(condition, df, z, f, place)

    def third(self, dz):
        z, f = self.at.z + dz, self.at.f
        condition = present(self.at, dz)
        place = self.at.index(z, f, self.at.g)
        parts = self.f_parts(z)
        if self.order == "fz":
            parts = parts + self.line_parts(dz, z, f)
        self.join(condition, place, parts)
        if dz:
            self.send_line(condition, dz, z, f, place)

    def stages(self):
        order = line_targets(self.at)
        part = functools.partial
        begins = [part(self.begin, *item) for item in order]
        pairs = [part(self.over_pair, *item) for item in order]
        if self.order == "fz":
            seconds = [part(self.second, *item[:2]) for item in order if item[2] == 0]
            thirds = [part(self.third, dz) for dz in (-3, 3, -2, 2, -1, 1, 0)]
        else:
            dfs = list(range(1, self.at.nf)) + [0]
            seconds = [part(self.second, dz, df) for dz in (-3, 3, -2, 2, -1, 1, 0) for df in dfs]
            thirds = [part(self.third, 0)]
        return begins, pairs, seconds, thirds

    def store(self, target, start):
        place = self.at.index(self.at.z, self.at.f, self.at.g)
        target[:, pl.ds(start, self.acc.shape[2])] = self.acc[place].astype(F32)


def mixed(first, second):
    marked = [((i + 0.5) / len(steps), kind, step) for kind, steps in enumerate((first, second)) for i, step in enumerate(steps)]
    return [step for _, _, step in sorted(marked, key=lambda item: item[:2])]


def pipelined(scatters):
    stages = [scatter.stages() for scatter in scatters]
    begins = [step for stage in stages for step in stage[0]]
    events = []
    for slot in range(len(scatters) + 2):
        turn_steps = []
        for kind in (3, 2, 1):
            number = slot - (kind - 1)
            if 0 <= number < len(scatters):
                turn_steps = mixed(turn_steps, stages[number][kind]) if turn_steps else stages[number][kind]
        events += turn_steps
    return begins, events


def split_scratch(refs, count):
    size = Scatter.PARTS
    return [refs[i * size : (i + 1) * size] for i in range(count)], refs[count * size :]


def scatter_sections(at, sources, spans, scratches, phase):
    scatters, places = [], []
    for number, parts in enumerate(spans):
        start = 0
        for size, order in parts:
            scratch = scratches[len(scatters)]
            scatters.append(Scatter(at, sources[number], pl.ds(start, size), order, scratch, phase))
            places.append((number, start))
            start += size
    return scatters, places


def scatter_kernel(sizes, spans, *refs):
    at = Place(*sizes)
    count, sections = len(spans), sum(len(parts) for parts in spans)
    sources, refs = refs[:count], refs[count:]
    input_ref, vector_ref, grad_ref, total_ref = refs[:4]
    owned, refs = refs[4 : 4 + count], refs[4 + count :]
    scratches, refs = split_scratch(refs, sections)
    sq_g, sq_f, sq_z, sq_c, trade_send, trade_recv, sq_send, sq_recv = refs
    slots = grad_ref.shape[0]
    peers, number = plane_peers(at)
    more, extra = slot_peers(at, slots)
    meet(peers + more, number + extra)
    phase = Phase()
    send = functools.partial(start_copy, phase)
    scatters, places = scatter_sections(at, sources, spans, scratches, phase)
    begins, events = pipelined(scatters)
    other = 1 - at.core

    def vectors_g():
        for step in range(1, at.ng):
            device = at.device(at.z, at.f, (at.g + step) % at.ng)
            send(True, sq_g.at[at.g], sq_g.at[at.g], sq_send.at[0, step], sq_recv.at[0, at.g], device)

    def vectors_f():
        for step in range(1, at.nf):
            device = at.device(at.z, (at.f + step) % at.nf, at.g)
            send(True, sq_f.at[at.f], sq_f.at[at.f], sq_send.at[1, step], sq_recv.at[1, at.f], device)

    def line_send(condition, held, kind):
        device = at.device(at.z - 1 if kind else at.z + 1, at.f, at.g)
        send(condition, sq_z.at[held], sq_z.at[held], sq_send.at[2 + kind, held], sq_recv.at[2, held], device)

    def vectors_line(distance):
        for kind, held in enumerate((at.z - distance, at.z + distance)):
            there = held < LINE if kind else held >= 0
            onward = at.z > 0 if kind else at.z < LINE - 1
            if distance and not phase.ending:
                when(
                    there,
                    functools.partial(await_block, sq_z.at[held], sq_recv.at[2, held]),
                )
            line_send(both(there, onward), held, kind)

    def vectors_pair():
        send(
            True,
            sq_c.at[at.core],
            sq_c.at[at.core],
            sq_send.at[4, 0],
            sq_recv.at[3, at.core],
            at.partner(),
        )

    def sums():
        def g():
            for step in range(1, at.ng):
                peer = (at.g + step) % at.ng
                await_block(sq_g.at[peer], sq_recv.at[0, peer])
            total = sq_g[0]
            for number in range(1, at.ng):
                total = total + sq_g[number]
            sq_f[at.f] = total
            vectors_f()

        def f():
            for step in range(1, at.nf):
                peer = (at.f + step) % at.nf
                await_block(sq_f.at[peer], sq_recv.at[1, peer])
            total = sq_f[0]
            for number in range(1, at.nf):
                total = total + sq_f[number]
            sq_z[at.z] = total
            vectors_line(0)

        def pair():
            total = sq_z[0]
            for number in range(1, LINE):
                total = total + sq_z[number]
            sq_c[at.core] = total
            vectors_pair()

        return [g, f] + [functools.partial(vectors_line, d) for d in range(1, LINE)] + [pair]

    sq_g[at.g] = vector_ref[...]
    run_all(begins)
    vectors_g()
    trade_out(at, input_ref, grad_ref, trade_send, trade_recv, phase)
    run_all(mixed(events, sums()))
    for scatter, (number, start) in zip(scatters, places):
        scatter.store(owned[number], start)
    await_block(sq_c.at[other], sq_recv.at[3, other])
    total_ref[...] = sq_c[0] + sq_c[1]

    phase.ending = True
    run_all(begins + events)
    trade_out(at, input_ref, grad_ref, trade_send, trade_recv, phase)
    vectors_g()
    vectors_f()
    for distance in range(LINE):
        vectors_line(distance)
    vectors_pair()


def scatter_last(sources, spans, input_grad, vectors, slots, seq_size, fsdp_size):
    rows = sources[0].shape[0] // (seq_size * fsdp_size)
    own_rows, model = input_grad.shape
    positions = own_rows // slots
    nf, ng = seq_size // (2 * LINE), fsdp_size
    dma = pltpu.SemaphoreType.DMA
    widest = max(nf, ng, LINE)
    vmem = pl.BlockSpec(memory_space=pltpu.VMEM)
    scratch = []
    for parts in spans:
        for size, order in parts:
            scratch += Scatter.scratch(order, rows, size, nf, ng)
    return pl.pallas_call(
        functools.partial(scatter_kernel, (seq_size, fsdp_size), spans),
        out_shape=tuple(
            [
                jax.ShapeDtypeStruct((slots, positions, model), BF16),
                jax.ShapeDtypeStruct(vectors.shape, F32),
            ]
            + [jax.ShapeDtypeStruct((rows, source.shape[1]), F32) for source in sources]
        ),
        in_specs=[pl.BlockSpec(memory_space=pl.ANY)] * len(sources) + [vmem] * 2,
        out_specs=[vmem] * (2 + len(sources)),
        scratch_shapes=scratch
        + [pltpu.VMEM((size, *vectors.shape), F32) for size in (ng, nf, LINE, 2)]
        + [dma((slots,)), dma((slots,)), dma((5, widest)), dma((4, widest))],
        compiler_params=pltpu.CompilerParams(
            collective_id=3, has_side_effects=True, vmem_limit_bytes=63_000_000
        ),
        name="scatter_last",
    )(*sources, input_grad, vectors)


def first_half(shape):
    lane = lax.broadcasted_iota(jnp.int32, shape, 1)
    return lane % 64 < 32


def turn(values, cosine, sine):
    half = first_half(values.shape)
    away = jnp.where(half, -pltpu.roll(values, 96, 1), pltpu.roll(values, 32, 1))
    return values * cosine + away * sine


def turn_back(grads, cosine, sine):
    half = first_half(grads.shape)
    moved = grads * sine
    away = jnp.where(half, pltpu.roll(moved, 96, 1), -pltpu.roll(moved, 32, 1))
    return grads * cosine + away


def normalize(values):
    average = jnp.mean(values, axis=-1, keepdims=True)
    centered = values - average
    variance = jnp.mean(centered * centered, axis=-1, keepdims=True)
    inverse = lax.rsqrt(variance + EPS)
    return centered * inverse, inverse


def norm_back(grad_normed, normed, inverse, gain_values):
    scaled = grad_normed * gain_values
    first_mean = jnp.mean(scaled, axis=-1, keepdims=True)
    second_mean = jnp.mean(scaled * normed, axis=-1, keepdims=True)
    return inverse * (scaled - first_mean - normed * second_mean)


def head_lanes(shape, head):
    return lax.broadcasted_iota(jnp.int32, shape, 1) // 64 == head


def scores_of(keys, queries, bias):
    scores = lax.dot_general(keys, queries, (((1,), (1,)), ((), ())), preferred_element_type=F32)
    return scores + bias


def key_bias(length, shape):
    return jnp.where(lax.broadcasted_iota(jnp.int32, shape, 0) < length, 0.0, -jnp.inf)


def attend(length, queries, keys, values):
    queries = queries * 0.125
    bias = key_bias(length, (keys.shape[0], 1))
    zero = jnp.zeros((), BF16)
    total, logs = None, []
    for head in range(2):
        only = head_lanes(queries.shape, head)
        scores = scores_of(keys, jnp.where(only, queries, zero), bias)
        largest = jnp.max(scores, axis=0, keepdims=True)
        weights = jnp.exp(scores - largest)
        summed = jnp.sum(weights, axis=0, keepdims=True)
        logs.append(largest + jnp.log(summed))
        held = jnp.where(head_lanes(values.shape, head), values, zero)
        part = lax.dot_general(
            held, weights.astype(BF16), (((0,), (0,)), ((), ())), preferred_element_type=F32
        )
        part = part / summed
        total = part if total is None else total + part
    return total.T.astype(BF16), logs


FRONT_TILE = 512


def front_kernel(sizes, group, spans, *refs):
    at = Place(*sizes)
    count = len(spans)
    length_ref, x_ref, gains_ref, cos_ref, sin_ref, w_ref, dy_ref = refs[:7]
    sources, refs = refs[7 : 7 + count], refs[7 + count :]
    act_ref, gain_ref, q_ref, shared_out, o_ref, log_ref, dy_rows_ref = refs[:7]
    wholes, refs = refs[7 : 7 + count], refs[7 + count :]
    sems, (trade_send, trade_recv, share_send, share_recv, shared_ref, out_sem) = refs[:3], refs[3:]
    step = pl.program_id(0)
    rows, model = q_ref.shape
    slots = dy_ref.shape[0]
    tile = o_ref.shape[0]
    tiles = rows // tile
    projecting = 3 * model // FRONT_TILE
    steps = projecting + model // LANES * tiles
    kept = 2 * model // FRONT_TILE
    phase = Phase()
    sections = []
    for number, parts in enumerate(spans):
        start = 0
        for size, order in parts:
            sections.append((sources[number], wholes[number], pl.ds(start, size), order))
            start += size
    gather = Gather(at, sections, sems, phase)
    base, part = (at.seq // group) * group, at.seq % group
    members = [base + (part + other) % group for other in range(1, group)]
    own_rows = pl.ds(pl.multiple_of(part * rows, rows), rows)

    @pl.when(step == 0)
    def _():
        peers, number = plane_peers(at)
        more, extra = slot_peers(at, slots)
        others = [(True, (member, at.y)) for member in members]
        meet(peers + more + others, number + extra + group - 1)

    @pl.when(step == 0)
    def _():
        gather.begin()
        trade_in(at, dy_ref, dy_rows_ref, trade_send, trade_recv, phase)

    @pl.when(step == 0)
    def _():
        normed, _ = normalize(x_ref[...].astype(F32))
        turned = gains_ref[...].astype(F32).T
        gain_ref[...] = turned[:8]
        act_ref[...] = (normed * turned[:1]).astype(BF16)

    def share(number):
        place = shared_ref.at[own_rows, pl.ds(number * FRONT_TILE, FRONT_TILE)]
        for other, member in enumerate(members):
            start_copy(
                phase,
                True,
                place,
                place,
                share_send.at[number, other],
                share_recv.at[number, part],
                (member, at.y),
            )

    def receive():
        for number in range(kept):
            for other in range(1, group):
                source = (part + other) % group
                place = shared_ref.at[
                    pl.ds(pl.multiple_of(source * rows, rows), rows),
                    pl.ds(number * FRONT_TILE, FRONT_TILE),
                ]
                await_block(place, share_recv.at[number, source])
        pltpu.make_async_copy(shared_ref, shared_out, out_sem).start()

    for number in range(kept):
        pl.when(step == number + 1)(functools.partial(share, number))
    pl.when(step == projecting)(receive)

    @pl.when(step < projecting)
    def _():
        mixed = jnp.dot(act_ref[...], w_ref[...], preferred_element_type=F32)

        def turned():
            cosine, sine = cos_ref[...], sin_ref[...]
            pieces = [
                turn(mixed[:, start : start + LANES], cosine, sine).astype(BF16)
                for start in range(0, FRONT_TILE, LANES)
            ]
            return jnp.concatenate(pieces, axis=1)

        @pl.when(step < kept // 2)
        def _():
            columns = pl.ds(pl.multiple_of(step * FRONT_TILE, FRONT_TILE), FRONT_TILE)
            shared_ref[own_rows, columns] = turned()

        @pl.when(both(step >= kept // 2, step < kept))
        def _():
            columns = pl.ds(pl.multiple_of(step * FRONT_TILE, FRONT_TILE), FRONT_TILE)
            shared_ref[own_rows, columns] = mixed.astype(BF16)

        @pl.when(step >= kept)
        def _():
            columns = pl.ds(pl.multiple_of((step - kept) * FRONT_TILE, FRONT_TILE), FRONT_TILE)
            q_ref[:, columns] = turned()

    @pl.when(step >= projecting)
    def _():
        pair, piece = (step - projecting) // tiles, (step - projecting) % tiles
        start = pl.multiple_of(pair * LANES, LANES)
        out, logs = attend(
            length_ref[0],
            q_ref[pl.ds(pl.multiple_of(piece * tile, tile), tile), pl.ds(start, LANES)],
            shared_ref[:, pl.ds(start, LANES)],
            shared_ref[:, pl.ds(pl.multiple_of(model + start, LANES), LANES)],
        )
        o_ref[...] = out
        for head in range(2):
            log_ref[0, head : head + 1, :] = logs[head]

    events = gather.events()
    pace = FRONT_PACE
    for number in range(steps - 1):
        group_events = events[number * pace : (number + 1) * pace]
        if group_events:
            pl.when(step == number)(functools.partial(run_all, group_events))

    @pl.when(step == steps - 1)
    def _():
        run_all(events[(steps - 1) * pace :])
        phase.ending = True
        gather.begin()
        trade_in(at, dy_ref, dy_rows_ref, trade_send, trade_recv, phase)
        run_all(events)
        for number in range(kept):
            share(number)
        gather.finish()
        pltpu.make_async_copy(shared_ref, shared_out, out_sem).wait()
        phase.ending = False


FRONT_PACE = 2


def front(length, x_rows, gains, cosine, sine, weight, dy, sources, spans, group, tile, seq_size, fsdp_size):
    rows, model = x_rows.shape
    slots, positions, _ = dy.shape
    pairs, tiles = model // LANES, rows // tile
    projecting, kept = 3 * model // FRONT_TILE, 2 * model // FRONT_TILE
    nf, ng = seq_size // (2 * LINE), fsdp_size
    devices = seq_size * fsdp_size
    count = sum(len(parts) for parts in spans)
    dma = pltpu.SemaphoreType.DMA
    vmem, anywhere = pl.BlockSpec(memory_space=pltpu.VMEM), pl.BlockSpec(memory_space=pl.ANY)

    def pair_of(i):
        return jnp.maximum(i - projecting, 0) // tiles

    def tile_of(i):
        return jnp.maximum(i - projecting, 0) % tiles

    return pl.pallas_call(
        functools.partial(front_kernel, (seq_size, fsdp_size), group, spans),
        grid=(projecting + pairs * tiles,),
        out_shape=tuple(
            [
                jax.ShapeDtypeStruct((rows, model), BF16),
                jax.ShapeDtypeStruct((8, model), F32),
                jax.ShapeDtypeStruct((rows, model), BF16),
                jax.ShapeDtypeStruct((rows * group, 2 * model), BF16),
                jax.ShapeDtypeStruct((rows, model), BF16),
                jax.ShapeDtypeStruct((pairs, 8, rows), F32),
                jax.ShapeDtypeStruct((slots * positions, model), BF16),
            ]
            + [
                jax.ShapeDtypeStruct((source.shape[0] * devices, source.shape[1]), BF16)
                for source in sources
            ]
        ),
        in_specs=[pl.BlockSpec(memory_space=pltpu.SMEM), vmem, vmem, vmem, vmem]
        + [
            pl.BlockSpec(
                (model, FRONT_TILE),
                lambda i: (0, (jnp.minimum(i, projecting - 1) + projecting - kept) % projecting),
            )
        ]
        + [vmem] * (1 + len(sources)),
        out_specs=[
            vmem,
            vmem,
            vmem,
            anywhere,
            pl.BlockSpec((tile, LANES), lambda i: (tile_of(i), pair_of(i))),
            pl.BlockSpec((1, 8, tile), lambda i: (pair_of(i), 0, tile_of(i))),
        ]
        + [anywhere] * (1 + len(sources)),
        scratch_shapes=Gather.scratch(count, nf, ng)
        + [dma((slots,)), dma((slots,)), dma((kept, group)), dma((kept, group))]
        + [pltpu.VMEM((rows * group, 2 * model), BF16), dma],
        compiler_params=pltpu.CompilerParams(
            collective_id=1, has_side_effects=True, vmem_limit_bytes=63_000_000
        ),
        name="front",
    )(length, x_rows, gains, cosine, sine, weight, dy, *sources)


def attend_back(length, queries, keys, values, grads, heads_out, logs):
    queries = queries * 0.125
    bias = key_bias(length, (keys.shape[0], 1))
    zero = jnp.zeros((), BF16)
    product = (grads.astype(F32) * heads_out.astype(F32)).T
    dq = dk = dv = None
    for head in range(2):
        only = head_lanes(queries.shape, head)
        query = jnp.where(only, queries, zero)
        grad = jnp.where(only, grads, zero)
        key = jnp.where(head_lanes(keys.shape, head), keys, zero)
        delta = jnp.sum(product[64 * head : 64 * head + 64], axis=0, keepdims=True)
        scores = scores_of(keys, query, bias)
        probs = jnp.exp(scores - logs[head : head + 1])
        grad_probs = lax.dot_general(
            values, grad, (((1,), (1,)), ((), ())), preferred_element_type=F32
        )
        grad_scores = (probs * (grad_probs - delta)).astype(BF16)
        value_part = jnp.dot(probs.astype(BF16), grad, preferred_element_type=F32)
        key_part = jnp.dot(grad_scores, query, preferred_element_type=F32)
        query_part = lax.dot_general(
            key, grad_scores, (((0,), (0,)), ((), ())), preferred_element_type=F32
        )
        dq = query_part if dq is None else dq + query_part
        dk = key_part if dk is None else dk + key_part
        dv = value_part if dv is None else dv + value_part
    return dq.T * 0.125, dk, dv


def back_kernel(sizes, group, spans, *refs):
    at = Place(*sizes)
    sections = sum(len(parts) for parts in spans)
    count = len(spans)
    length_ref, q_ref, k_ref, v_ref, g_ref, o_ref, log_ref, cos_ref, sin_ref, result_ref = refs[:10]
    sources, refs = refs[10 : 10 + count], refs[10 + count :]
    mixed_ref, out_ref = refs[:2]
    owned, refs = refs[2 : 2 + count], refs[2 + count :]
    scratches, refs = split_scratch(refs, sections)
    dk_acc, dv_acc, parts_ref, arrived, sum_send, sum_recv, trade_send, trade_recv = refs
    step = pl.program_id(0)
    tile = q_ref.shape[0]
    rows, model = result_ref.shape
    tiles, pairs = rows // tile, model // LANES
    steps = pairs * tiles + 1
    slots = out_ref.shape[0]
    phase = Phase()
    scatters, places = scatter_sections(at, sources, spans, scratches, phase)
    begins, events = pipelined(scatters)
    base, part = (at.seq // group) * group, at.seq % group
    members = [base + (part + other) % group for other in range(1, group)]

    def columns_of(pair):
        return pl.ds(pl.multiple_of(pair * LANES, LANES), LANES)

    def share(pair):
        for kind in range(2):
            for other, member in enumerate(members):
                owner = (part + other + 1) % group
                start_copy(
                    phase,
                    True,
                    parts_ref.at[kind, pl.ds(pl.multiple_of(owner * rows, rows), rows), columns_of(pair)],
                    arrived.at[kind, other, :, columns_of(pair)],
                    sum_send.at[kind, other, pair],
                    sum_recv.at[kind, other, pair],
                    (member, at.y),
                )

    @pl.when(step == 0)
    def _():
        peers, number = plane_peers(at)
        more, extra = slot_peers(at, slots)
        others = [(True, (member, at.y)) for member in members]
        meet(peers + more + others, number + extra + group - 1)
        run_all(begins)
        trade_out(at, result_ref, out_ref, trade_send, trade_recv, phase)

    pl.when(both(step > 0, step % tiles == 0))(lambda: share(step // tiles - 1))

    @pl.when(step < steps - 1)
    def _():
        pair, piece = step // tiles, step % tiles
        own = pl.ds(pl.multiple_of(piece * tile, tile), tile)
        dq, dk, dv = attend_back(
            length_ref[0], q_ref[...], k_ref[...], v_ref[...], g_ref[...], o_ref[...], log_ref[0]
        )
        mixed_ref[own, columns_of(pair)] = turn_back(dq, cos_ref[own], sin_ref[own]).astype(BF16)
        if tiles == 1:
            parts_ref[0, :, columns_of(pair)] = dk.astype(BF16)
            parts_ref[1, :, columns_of(pair)] = dv.astype(BF16)
            return

        @pl.when(piece == 0)
        def _():
            dk_acc[...] = dk
            dv_acc[...] = dv

        @pl.when(piece > 0)
        def _():
            dk_acc[...] += dk
            dv_acc[...] += dv

        @pl.when(piece == tiles - 1)
        def _():
            parts_ref[0, :, columns_of(pair)] = dk_acc[...].astype(BF16)
            parts_ref[1, :, columns_of(pair)] = dv_acc[...].astype(BF16)

    def add_parts():
        own = pl.ds(pl.multiple_of(part * rows, rows), rows)

        def body(pair, carry):
            for kind in range(2):
                total = parts_ref[kind, own, columns_of(pair)].astype(F32)
                for other in range(group - 1):
                    piece = arrived.at[kind, other, :, columns_of(pair)]
                    await_block(piece, sum_recv.at[kind, other, pair])
                    total = total + piece[...].astype(F32)
                if kind == 0:
                    total = turn_back(total, cos_ref[...], sin_ref[...])
                start = pl.multiple_of((kind + 1) * model + pair * LANES, LANES)
                mixed_ref[:, pl.ds(start, LANES)] = total.astype(BF16)
            return carry

        lax.fori_loop(0, pairs, body, 0)

    for number in range(steps - 1):
        some = events[number * BACK_PACE : (number + 1) * BACK_PACE]
        if some:
            pl.when(step == number)(functools.partial(run_all, some))

    @pl.when(step == steps - 1)
    def _():
        add_parts()
        run_all(events[(steps - 1) * BACK_PACE :])
        for scatter, (number, start) in zip(scatters, places):
            scatter.store(owned[number], start)
        phase.ending = True
        run_all(begins + events)
        trade_out(at, result_ref, out_ref, trade_send, trade_recv, phase)

        def body(pair, carry):
            share(pair)
            return carry

        lax.fori_loop(0, pairs, body, 0)
        phase.ending = False


BACK_PACE = 5


def back(length, queries, shared, grads, heads_out, logs, cosine, sine, result, sources, spans, tile, slots, seq_size, fsdp_size):
    rows, keys, model = queries.shape[0], shared.shape[0], queries.shape[1]
    group, positions = keys // rows, rows // slots
    pairs, tiles = model // LANES, rows // tile
    nf, ng = seq_size // (2 * LINE), fsdp_size
    devices = seq_size * fsdp_size
    shard = sources[0].shape[0] // devices
    vmem, anywhere = pl.BlockSpec(memory_space=pltpu.VMEM), pl.BlockSpec(memory_space=pl.ANY)
    dma = pltpu.SemaphoreType.DMA

    def pair_of(i):
        return jnp.minimum(i, pairs * tiles - 1) // tiles

    def tile_of(i):
        return jnp.minimum(i, pairs * tiles - 1) % tiles

    by_row = pl.BlockSpec((tile, LANES), lambda i: (tile_of(i), pair_of(i)))
    scratch = []
    for parts in spans:
        for size, order in parts:
            scratch += Scatter.scratch(order, shard, size, nf, ng)
    return pl.pallas_call(
        functools.partial(back_kernel, (seq_size, fsdp_size), group, spans),
        grid=(pairs * tiles + 1,),
        out_shape=tuple(
            [
                jax.ShapeDtypeStruct((rows, 3 * model), BF16),
                jax.ShapeDtypeStruct((slots, positions, model), BF16),
            ]
            + [jax.ShapeDtypeStruct((shard, source.shape[1]), F32) for source in sources]
        ),
        in_specs=[
            pl.BlockSpec(memory_space=pltpu.SMEM),
            by_row,
            pl.BlockSpec((keys, LANES), lambda i: (0, pair_of(i))),
            pl.BlockSpec((keys, LANES), lambda i: (0, pairs + pair_of(i))),
            by_row,
            by_row,
            pl.BlockSpec((1, 8, tile), lambda i: (pair_of(i), 0, tile_of(i))),
            vmem,
            vmem,
            vmem,
        ]
        + [anywhere] * len(sources),
        out_specs=[vmem, anywhere] + [vmem] * len(sources),
        scratch_shapes=scratch
        + [
            pltpu.VMEM((keys, LANES), F32),
            pltpu.VMEM((keys, LANES), F32),
            pltpu.VMEM((2, keys, model), BF16),
            pltpu.VMEM((2, group - 1, rows, model), BF16),
            dma((2, group - 1, pairs)),
            dma((2, group - 1, pairs)),
            dma((slots,)),
            dma((slots,)),
        ],
        compiler_params=pltpu.CompilerParams(
            collective_id=2, has_side_effects=True, vmem_limit_bytes=67_000_000
        ),
        name="back",
    )(length, queries, shared, shared, grads, heads_out, logs, cosine, sine, result, *sources)


def rotary_tables(places, head_size):
    halfway = head_size // 2
    ladder = jnp.arange(halfway, dtype=F32) * (2.0 / head_size)
    inverse = 1.0 / THETA**ladder
    angles = places.astype(F32)[:, None] * inverse[None, :]
    angles = jnp.concatenate([angles] * 4, axis=-1)
    return jnp.cos(angles), jnp.sin(angles)


def gelu_exact(values):
    return jax.nn.gelu(values, approximate=False)


def mm(left, right):
    return jnp.dot(left, right, preferred_element_type=F32)


def mm_right_t(left, right):
    return lax.dot_general(left, right, (((1,), (1,)), ((), ())), preferred_element_type=F32)


def mm_left_t(left, right):
    return lax.dot_general(left, right, (((0,), (0,)), ((), ())), preferred_element_type=F32)


def shards(
    hidden_in,
    out_grad,
    qkv_weight,
    attn_out_weight,
    in_weight,
    down_weight,
    attn_gain,
    mlp_gain,
    seq_lengths,
    slot_order,
):
    seq_size, fsdp_size = lax.axis_size("seq"), lax.axis_size("fsdp")
    seq_place, fsdp_place = lax.axis_index("seq"), lax.axis_index("fsdp")
    slots, positions, model = hidden_in.shape
    shard = qkv_weight.shape[0]
    ff = down_weight.shape[0]
    wide = up_to(ff, LANES)
    spare = wide - ff
    group = seq_size // slots
    rows = slots * positions
    head_size = model // HEADS

    lead = jnp.zeros((shard, spare), BF16)
    gains = jnp.concatenate(
        [attn_gain[:, None], mlp_gain[:, None], jnp.zeros((shard, LANES - 2), BF16)], axis=1
    )
    in_pack = jnp.concatenate([in_weight[:, :ff], lead, in_weight[:, ff:], lead], axis=1)
    down_pack = jnp.concatenate([down_weight.T, lead], axis=1)
    w_qkv, all_gains, x_rows = gather_first(qkv_weight, gains, hidden_in, seq_size, fsdp_size)

    slot = fsdp_place * slots + seq_place // group
    order = jnp.sum(jnp.where(jnp.arange(slot_order.shape[0]) == slot, slot_order, 0))
    length = jnp.sum(jnp.where(jnp.arange(seq_lengths.shape[0]) == order, seq_lengths, 0))
    lengths = length.astype(jnp.int32)[None]
    places = (seq_place % group) * rows + jnp.arange(rows, dtype=jnp.int32)
    valid = (places < length).astype(F32)[:, None]
    cosine, sine = rotary_tables(places, head_size)

    tile = 512 if rows % 512 == 0 and rows * group <= 1024 else 128
    act_one, gain_rows, queries, shared, heads_out, logs, dy_rows, w_attn, w_input, w_down = front(
        lengths,
        x_rows,
        all_gains,
        cosine,
        sine,
        w_qkv,
        out_grad,
        (attn_out_weight, in_pack, down_pack),
        (((model, "fzg"),), ((wide, "zfg"), (wide, "zfg")), ((wide, "fzg"),)),
        group,
        tile,
        seq_size,
        fsdp_size,
    )
    gain_attn, gain_mlp = gain_rows[0:1], gain_rows[1:2]

    x_wide = x_rows.astype(F32)
    attn = mm(heads_out, w_attn)
    middle = x_wide + attn
    normed_two, inverse_two = normalize(middle)
    act_two = (normed_two * gain_mlp).astype(BF16)
    joined = mm(act_two, w_input)
    input_half = joined[:, :wide]
    gate_half = joined[:, wide:]
    active, active_pull = jax.vjp(gelu_exact, input_half)
    product = (active * gate_half).astype(BF16)
    branch = mm_right_t(product, w_down)
    result = (middle + branch) * valid
    squares = [
        jnp.sum(valid * tensor * tensor, axis=0) for tensor in (x_wide, middle, result, attn, branch)
    ]

    grad_y = dy_rows.astype(F32) * valid
    grad_branch = grad_y.astype(BF16)
    down_part = mm_left_t(grad_branch, product).astype(BF16)
    grad_product = mm(grad_branch, w_down)
    grad_joined = jnp.concatenate(
        [active_pull(grad_product * gate_half)[0], grad_product * active], axis=1
    ).astype(BF16)
    input_part = mm_left_t(act_two, grad_joined).astype(BF16)
    grad_act_two = mm_right_t(grad_joined, w_input)
    mlp_gain_part = jnp.sum(grad_act_two * normed_two, axis=0)
    grad_middle = grad_y + norm_back(grad_act_two, normed_two, inverse_two, gain_mlp)
    grad_attn = grad_middle.astype(BF16)
    attn_part = mm_left_t(heads_out, grad_attn).astype(BF16)
    grad_heads = mm_right_t(grad_attn, w_attn).astype(BF16)

    second = "zf" if seq_size == 4 * LINE else "fz"
    early = [(attn_part, ((model, second),)), (down_part, ((wide, second),))]
    wide_part = (input_part, ((wide, "fz"), (wide, "fz")))
    if rows * group <= 1024:
        early, late = [early[0], wide_part, early[1]], []
    else:
        late = [wide_part]
    grad_mixed, out_rows, *owned = back(
        lengths,
        queries,
        shared,
        grad_heads,
        heads_out,
        logs,
        cosine,
        sine,
        result.astype(BF16),
        [part for part, _ in early],
        tuple(parts for _, parts in early),
        tile,
        slots,
        seq_size,
        fsdp_size,
    )
    qkv_part = mm_left_t(act_one, grad_mixed).astype(BF16)
    grad_act_one = mm_right_t(grad_mixed, w_qkv)
    normed_one, inverse_one = normalize(x_wide)
    attn_gain_part = jnp.sum(grad_act_one * normed_one, axis=0)
    grad_x = grad_middle + norm_back(grad_act_one, normed_one, inverse_one, gain_attn)

    vectors = jnp.stack(squares + [attn_gain_part, mlp_gain_part, jnp.zeros((model,), F32)])
    half = 3 * model // 2
    late.append((qkv_part, ((half, "fz"), (half, second))))
    grad_rows, totals, *more = scatter_last(
        [part for part, _ in late],
        tuple(parts for _, parts in late),
        grad_x.astype(BF16),
        vectors,
        slots,
        seq_size,
        fsdp_size,
    )
    own_attn, own_down, own_qkv = owned[0], owned[-1], more[-1]
    own_in = more[0] if len(more) == 2 else owned[1]
    tokens_valid = jnp.sum(seq_lengths).astype(F32)
    root_squares = jnp.sqrt(jnp.sum(totals[:5], axis=1) / (tokens_valid * model))
    own_gains = lax.dynamic_slice_in_dim(totals, (seq_place * fsdp_size + fsdp_place) * shard, shard, 1)
    return (
        out_rows,
        grad_rows,
        own_qkv,
        own_attn,
        jnp.concatenate([own_in[:, :ff], own_in[:, wide : wide + ff]], axis=1),
        own_down[:, :ff].T,
        own_gains[5],
        own_gains[6],
        root_squares,
    )


def solution(mesh):
    placed = (
        P("fsdp", "seq", None),
        P("fsdp", "seq", None),
        P(("seq", "fsdp"), None),
        P(("seq", "fsdp"), None),
        P(("seq", "fsdp"), None),
        P(None, ("seq", "fsdp")),
        P(("seq", "fsdp")),
        P(("seq", "fsdp")),
        P(),
        P(),
    )
    return jax.shard_map(
        shards,
        mesh=mesh,
        in_specs=placed,
        out_specs=(
            P("fsdp", "seq", None),
            P("fsdp", "seq", None),
            P(("seq", "fsdp"), None),
            P(("seq", "fsdp"), None),
            P(("seq", "fsdp"), None),
            P(None, ("seq", "fsdp")),
            P(("seq", "fsdp")),
            P(("seq", "fsdp")),
            P(),
        ),
        check_vma=False,
    )
```

```python
import functools

import jax
import jax.numpy as jnp
from jax import lax
from jax.experimental import pallas as pl
from jax.experimental.pallas import tpu as pltpu
from jax.sharding import PartitionSpec as P

HEADS = 16
LINE = 4
LANES = 128
EPS = 1e-05
THETA = 160000.0
F32 = jnp.float32
BF16 = jnp.bfloat16
MESH = pl.DeviceIdType.MESH


def up_to(size, unit):
    return -(-size // unit) * unit


class Place:
    def __init__(self, seq_size, fsdp_size, swap=True):
        self.seq_size, self.fsdp_size = seq_size, fsdp_size
        self.rest = seq_size // (2 * LINE)
        self.swap = swap and self.rest == fsdp_size
        self.nf, self.ng = self.rest, fsdp_size
        self.blocks = LINE * self.nf * self.ng
        self.seq = lax.axis_index("seq")
        self.y = lax.axis_index("fsdp")
        self.core = self.seq % 2
        self.r = (self.seq // 2) % self.rest
        self.z = self.seq // (2 * self.rest)
        self.f, self.g = self.split(self.r, self.y, self.core)

    def split(self, r, y, core):
        if not self.swap:
            return r, y
        return (1 - core) * r + core * y, (1 - core) * y + core * r

    def device(self, z, f, g, core=None):
        core = self.core if core is None else core
        r, y = self.split(f, g, core)
        return (z * self.rest + r) * 2 + core, y

    def row_block(self, z, f, g, core=None):
        seq, y = self.device(z, f, g, core)
        return seq * self.fsdp_size + y

    def index(self, z, f, g):
        return (z * self.nf + f) * self.ng + g

    def partner(self):
        return self.seq + 1 - 2 * self.core, self.y


def both(first, second):
    if first is True:
        return second
    if second is True:
        return first
    return jnp.logical_and(first, second)


def when(condition, body):
    if condition is True:
        body()
    else:
        pl.when(condition)(body)


def meet(peers, awaited):
    barrier = pltpu.get_barrier_semaphore()
    for condition, device in peers:
        when(
            condition,
            functools.partial(
                pl.semaphore_signal, barrier, inc=1, device_id=device, device_id_type=MESH
            ),
        )
    pl.semaphore_wait(barrier, awaited)


def plane_peers(at):
    below, above = at.z > 0, at.z < LINE - 1
    peers = [
        (below, at.device(at.z - 1, at.f, at.g)),
        (above, at.device(at.z + 1, at.f, at.g)),
        (True, at.partner()),
    ]
    for step in range(1, at.nf):
        peers.append((True, at.device(at.z, (at.f + step) % at.nf, at.g)))
    for step in range(1, at.ng):
        peers.append((True, at.device(at.z, at.f, (at.g + step) % at.ng)))
    count = 1 + (at.nf - 1) + (at.ng - 1)
    count = count + jnp.where(below, 1, 0) + jnp.where(above, 1, 0)
    return peers, count


def slot_peers(at, slots):
    group = at.seq_size // slots
    own_slot, own_part = at.seq // group, at.seq % group
    same = at.seq // slots == own_part
    peers = []
    for step in range(slots):
        wide = ((own_slot + step) % slots) * group + at.seq // slots
        narrow = own_part * slots + (at.seq + step) % slots
        condition = True if step else jnp.logical_not(same)
        peers.append((condition, (wide, at.y)))
        peers.append((condition, (narrow, at.y)))
    return peers, 2 * slots - 2 * jnp.where(same, 1, 0)


def steps_of(at):
    out = []
    for dz in (0, -1, 1, -2, 2, -3, 3):
        for df in range(at.nf):
            for dg in range(at.ng):
                out.append((abs(dz) + (df > 0) + (dg > 0), dz, df, dg))
    out.sort(key=lambda item: item[0])
    return out


def present(at, dz):
    if dz == 0:
        return True
    return at.z + dz >= 0 if dz < 0 else at.z + dz < LINE


class Gather:
    def __init__(self, at, sections, sems, phase):
        self.at, self.sections, self.phase = at, sections, phase
        plain = Place(at.seq_size, at.fsdp_size, swap=False)
        self.places = [plain if section[3][-1] == "-" else at for section in sections]
        self.send_sems, self.plane_sems, self.pair_sems = sems

    @staticmethod
    def scratch(count, nf, ng):
        dma = pltpu.SemaphoreType.DMA
        blocks, kinds = LINE * nf * ng, 3 + (nf - 1) + (ng - 1)
        return [dma((count, blocks, kinds)), dma((count, blocks)), dma((count, blocks + 1))]

    def own(self, number):
        source, _, columns, _ = self.sections[number]
        return source.at[:, columns]

    def block(self, number, z, f, g):
        source, whole, columns, _ = self.sections[number]
        rows = source.shape[0]
        start = pl.multiple_of(self.places[number].row_block(z, f, g) * rows, rows)
        return whole.at[pl.ds(start, rows), columns]

    def forward(self, number, condition, source, dz, df, dg):
        at, order = self.places[number], self.sections[number][3].strip("-")
        z, f, g = at.z + dz, (at.f + df) % at.nf, (at.g + dg) % at.ng
        place, target = at.index(z, f, g), self.block(number, z, f, g)
        moved = {"z": dz, "f": df, "g": dg}
        last = max([i for i, axis in enumerate(order) if moved[axis]], default=-1)

        def send(allowed, kind, device, pair=False):
            sem = (self.pair_sems if pair else self.plane_sems).at[number, place]
            start_copy(
                self.phase,
                both(condition, allowed),
                source,
                target,
                self.send_sems.at[number, place, kind],
                sem,
                device,
            )

        for i, axis in enumerate(order):
            if axis == "z" and i >= last:
                rising, sinking = dz <= 0, dz >= 0
                if rising:
                    send(at.z < LINE - 1, 0, at.device(at.z + 1, at.f, at.g))
                if sinking:
                    send(at.z > 0, 1, at.device(at.z - 1, at.f, at.g))
            if axis == "f" and i > last:
                for step in range(1, at.nf):
                    send(True, 1 + step, at.device(at.z, (at.f + step) % at.nf, at.g))
            if axis == "g" and i > last:
                for step in range(1, at.ng):
                    send(True, at.nf + step, at.device(at.z, at.f, (at.g + step) % at.ng))
        send(True, at.nf + at.ng, at.partner(), pair=True)

    def begin(self):
        for number in range(len(self.sections)):
            at = self.places[number]
            self.forward(number, True, self.own(number), 0, 0, 0)
            own = pltpu.make_async_copy(
                self.own(number),
                self.block(number, at.z, at.f, at.g),
                self.pair_sems.at[number, at.blocks],
            )
            if self.phase.ending:
                own.wait()
            else:
                own.start()

    def arrival(self, number, dz, df, dg):
        at = self.places[number]
        z, f, g = at.z + dz, (at.f + df) % at.nf, (at.g + dg) % at.ng
        condition = present(at, dz)
        block = self.block(number, z, f, g)
        sem = self.plane_sems.at[number, at.index(z, f, g)]
        if not self.phase.ending:
            when(condition, functools.partial(await_block, block, sem))
        self.forward(number, condition, block, dz, df, dg)

    def events(self):
        marked = [
            (hops, number, place, item)
            for place, (hops, *item) in enumerate(steps_of(self.at)[1:])
            for number in range(len(self.sections))
        ]
        marked.sort(key=lambda entry: entry[:3])
        return [functools.partial(self.arrival, number, *item) for _, number, _, item in marked]

    def from_partner(self, number, dz, df, dg):
        at = self.places[number]
        f, g = at.split(*at.split(at.f, at.g, at.core), 1 - at.core)
        z, f, g = at.z + dz, (f + df) % at.nf, (g + dg) % at.ng
        sem = self.pair_sems.at[number, at.index(z, f, g)]
        when(
            present(at, dz), functools.partial(await_block, self.block(number, 0, 0, 0), sem)
        )

    def steps(self, lag):
        events = self.events()

        def close(event):
            self.phase.ending = True
            event()
            self.from_partner(*event.args)
            self.phase.ending = False

        def step(number):
            events[number]()
            if number >= lag:
                close(events[number - lag])

        def rest():
            for event in events[-lag:]:
                close(event)
            self.phase.ending = True
            self.begin()
            for number in range(len(self.sections)):
                self.from_partner(number, 0, 0, 0)
            self.phase.ending = False

        return [functools.partial(step, number) for number in range(len(events))], rest


def trade_in(at, source_ref, target_ref, send_sems, recv_sems, phase):
    slots, positions = source_ref.shape[0], source_ref.shape[1]
    group = at.seq_size // slots
    own_slot, own_part = at.seq // group, at.seq % group
    same = at.seq // slots == own_part
    lane = at.seq % slots
    target = target_ref.at[pl.ds(pl.multiple_of(lane * positions, positions), positions), :]
    for step in range(slots):
        slot = (own_slot + step) % slots
        if step == 0 and not phase.ending:
            local = pltpu.make_async_copy(source_ref.at[slot], target, recv_sems.at[lane])
            when(same, local.start)
        start_copy(
            phase,
            True if step else jnp.logical_not(same),
            source_ref.at[slot],
            target,
            send_sems.at[step],
            recv_sems.at[lane],
            (slot * group + at.seq // slots, at.y),
        )
        if phase.ending:
            await_block(target_ref.at[pl.ds(step * positions, positions), :], recv_sems.at[step])


def trade_out(at, source_ref, target_ref, send_sems, recv_sems, phase):
    slots, positions = target_ref.shape[0], target_ref.shape[1]
    group = at.seq_size // slots
    own_slot, own_part = at.seq // group, at.seq % group
    same = at.seq // slots == own_part
    target = target_ref.at[own_slot]
    for step in range(slots):
        lane = (at.seq + step) % slots
        source = source_ref.at[pl.ds(pl.multiple_of(lane * positions, positions), positions), :]
        if step == 0 and not phase.ending:
            local = pltpu.make_async_copy(source, target, recv_sems.at[own_slot])
            when(same, local.start)
        start_copy(
            phase,
            True if step else jnp.logical_not(same),
            source,
            target,
            send_sems.at[step],
            recv_sems.at[own_slot],
            (own_part * slots + lane, at.y),
        )
        if phase.ending:
            await_block(target_ref.at[step], recv_sems.at[step])


def first_kernel(sizes, spans, weight_ref, gains_ref, hidden_ref, whole_ref, rows_ref, *refs):
    at = Place(*sizes)
    sems, (trade_send, trade_recv, pack_ref, pack_sems) = refs[:3], refs[3:]
    width, extra_width = weight_ref.shape[1], gains_ref.shape[1]
    loads = [
        pltpu.make_async_copy(weight_ref, pack_ref.at[:, pl.ds(0, width)], pack_sems.at[0]),
        pltpu.make_async_copy(gains_ref, pack_ref.at[:, pl.ds(width, extra_width)], pack_sems.at[1]),
    ]
    for load in loads:
        load.start()
    peers, count = plane_peers(at)
    more, extra = slot_peers(at, hidden_ref.shape[0])
    meet(peers + more, count + extra)
    for load in loads:
        load.wait()
    phase = Phase()
    sections, start = [], 0
    for size, order in spans:
        sections.append((pack_ref, whole_ref, pl.ds(start, size), order))
        start += size
    gather = Gather(at, sections, sems, phase)
    steps, rest = gather.steps(12)
    gather.begin()
    trade_in(at, hidden_ref, rows_ref, trade_send, trade_recv, phase)
    run_all(steps)
    rest()
    phase.ending = True
    trade_in(at, hidden_ref, rows_ref, trade_send, trade_recv, phase)


def gather_first(weight, gains, hidden, seq_size, fsdp_size):
    slots, positions, model = hidden.shape
    nf, ng = seq_size // (2 * LINE), fsdp_size
    devices = seq_size * fsdp_size
    dma = pltpu.SemaphoreType.DMA
    shard, width = weight.shape[0], weight.shape[1] + gains.shape[1]
    half = weight.shape[1] // 2
    spans = ((half, "zfg"), (width - half, "zfg"))
    return pl.pallas_call(
        functools.partial(first_kernel, (seq_size, fsdp_size), spans),
        out_shape=(
            jax.ShapeDtypeStruct((shard * devices, width), BF16),
            jax.ShapeDtypeStruct((slots * positions, model), BF16),
        ),
        in_specs=[pl.BlockSpec(memory_space=pltpu.VMEM)] * 3,
        out_specs=[pl.BlockSpec(memory_space=pl.ANY)] * 2,
        scratch_shapes=Gather.scratch(len(spans), nf, ng)
        + [dma((slots,)), dma((slots,)), pltpu.VMEM((shard, width), BF16), dma((2,))],
        compiler_params=pltpu.CompilerParams(collective_id=0, has_side_effects=True),
        name="gather_first",
    )(weight, gains, hidden)


def add_blocks(target, others):
    width = target.shape[1]
    piece = max(size for size in range(LANES, 1025, LANES) if width % size == 0)

    def body(number, carry):
        columns = pl.ds(pl.multiple_of(number * piece, LANES), piece)
        total = target[:, columns].astype(F32)
        for other in others:
            total = total + other[:, columns].astype(F32)
        target[:, columns] = total.astype(target.dtype)
        return carry

    lax.fori_loop(0, width // piece, body, 0)


def line_targets(at):
    order = []
    for dz in (-3, 3, -2, 2, -1, 1, 0):
        for df in list(range(1, at.nf)) + [0]:
            for dg in list(range(1, at.ng)) + [0]:
                order.append((dg == 0, df == 0, -abs(dz), dz, df, dg))
    order.sort(key=lambda item: item[:3])
    return [item[3:] for item in order]


class Phase:
    def __init__(self):
        self.ending = False


def start_copy(phase, condition, source, target, send_sem, recv_sem, device):
    copy = pltpu.make_async_remote_copy(
        src_ref=source,
        dst_ref=target,
        send_sem=send_sem,
        recv_sem=recv_sem,
        device_id=device,
        device_id_type=MESH,
    )
    when(condition, copy.wait_send if phase.ending else copy.start)


def run_all(events):
    for event in events:
        event()


def await_block(buffer, sem):
    pltpu.make_async_copy(buffer, buffer, sem).wait()


class Scatter:
    PARTS = 17

    @staticmethod
    def scratch(order, rows, width, nf, ng):
        dma = pltpu.SemaphoreType.DMA
        plane, beyond_g = LINE * nf * ng, (ng - 1) * LINE * nf
        beyond_f = (nf - 1) * (LINE if order == "fz" else 1)
        line = LINE * (1 if order == "fz" else nf)
        counts = (plane, plane, beyond_g, beyond_f, line, line)
        buffers = [pltpu.VMEM((count, rows, width), BF16) for count in counts]
        sems = (plane, plane, plane, beyond_g, beyond_g, beyond_f, beyond_f, line, line, line, line)
        return buffers + [dma((count,)) for count in sems]

    def __init__(self, at, source, columns, order, scratch, phase):
        self.at, self.source, self.columns, self.order = at, source, columns, order
        self.phase = phase
        self.acc, self.from_pair, self.from_g, self.from_f = scratch[:4]
        self.from_below, self.from_above = scratch[4:6]
        self.load_sems, self.pair_send, self.pair_recv = scratch[6:9]
        self.g_send, self.g_recv, self.f_send, self.f_recv = scratch[9:13]
        self.up_send, self.up_recv, self.down_send, self.down_recv = scratch[13:]
        self.rows = self.acc.shape[1]

    def where_is(self, dz, df, dg):
        at = self.at
        return at.z + dz, (at.f + df) % at.nf, (at.g + dg) % at.ng

    def rows_of(self, z, f, g, core=None):
        start = pl.multiple_of(self.at.row_block(z, f, g, core) * self.rows, self.rows)
        return self.source.at[pl.ds(start, self.rows), self.columns]

    def begin(self, dz, df, dg):
        at = self.at
        z, f, g = self.where_is(dz, df, dg)
        place, other = at.index(z, f, g), 1 - at.core
        pf, pg = at.split(*at.split(f, g, at.core), other)
        there = at.index(z, pf, pg)

        def body():
            if self.phase.ending:
                await_block(self.from_pair.at[there], self.pair_send.at[there])
                return
            pltpu.make_async_copy(
                self.rows_of(z, f, g), self.acc.at[place], self.load_sems.at[place]
            ).start()
            pltpu.make_async_remote_copy(
                src_ref=self.rows_of(z, pf, pg, other),
                dst_ref=self.from_pair.at[there],
                send_sem=self.pair_send.at[there],
                recv_sem=self.pair_recv.at[there],
                device_id=at.partner(),
                device_id_type=MESH,
            ).start()

        when(present(at, dz), body)

    def join(self, condition, place, parts):
        if self.phase.ending:
            return

        def body():
            ready = [(buffer, sem) for allowed, buffer, sem in parts if allowed is True]
            for buffer, sem in ready:
                await_block(buffer, sem)
            if ready:
                add_blocks(self.acc.at[place], [buffer for buffer, _ in ready])
            for allowed, buffer, sem in parts:
                if allowed is not True:

                    def more(buffer=buffer, sem=sem):
                        await_block(buffer, sem)
                        add_blocks(self.acc.at[place], [buffer])

                    pl.when(allowed)(more)

        when(condition, body)

    def over_pair(self, dz, df, dg):
        at = self.at
        z, f, g = self.where_is(dz, df, dg)
        condition = present(at, dz)
        place = at.index(z, f, g)
        if not self.phase.ending:
            when(
                condition,
                functools.partial(await_block, self.acc.at[place], self.load_sems.at[place]),
            )
        self.join(condition, place, [(True, self.from_pair.at[place], self.pair_recv.at[place])])
        if dg:
            slot = (dg - 1) * LINE * at.nf + z * at.nf + f
            start_copy(
                self.phase,
                condition,
                self.acc.at[place],
                self.from_g.at[slot],
                self.g_send.at[slot],
                self.g_recv.at[slot],
                at.device(at.z, at.f, g),
            )

    def g_parts(self, z, f):
        slots = [(step - 1) * LINE * self.at.nf + z * self.at.nf + f for step in range(1, self.at.ng)]
        return [(True, self.from_g.at[slot], self.g_recv.at[slot]) for slot in slots]

    def f_slot(self, z, step):
        return (step - 1) * LINE + z if self.order == "fz" else step - 1

    def f_parts(self, z):
        slots = [self.f_slot(z, step) for step in range(1, self.at.nf)]
        return [(True, self.from_f.at[slot], self.f_recv.at[slot]) for slot in slots]

    def line_slot(self, z, f):
        return z if self.order == "fz" else z * self.at.nf + f

    def line_parts(self, dz, z, f):
        slot, parts = self.line_slot(z, f), []
        if 0 <= dz < LINE - 1:
            parts.append((self.at.z > 0, self.from_below.at[slot], self.up_recv.at[slot]))
        if 1 - LINE < dz <= 0:
            parts.append((self.at.z < LINE - 1, self.from_above.at[slot], self.down_recv.at[slot]))
        return parts

    def send_f(self, condition, df, z, f, place):
        slot = self.f_slot(z, df)
        start_copy(
            self.phase,
            condition,
            self.acc.at[place],
            self.from_f.at[slot],
            self.f_send.at[slot],
            self.f_recv.at[slot],
            self.at.device(self.at.z, f, self.at.g),
        )

    def send_line(self, condition, dz, z, f, place):
        slot = self.line_slot(z, f)
        rising = dz > 0
        start_copy(
            self.phase,
            condition,
            self.acc.at[place],
            (self.from_below if rising else self.from_above).at[slot],
            (self.up_send if rising else self.down_send).at[slot],
            (self.up_recv if rising else self.down_recv).at[slot],
            self.at.device(self.at.z + (1 if rising else -1), self.at.f, self.at.g),
        )

    def second(self, dz, df):
        z, f, _ = self.where_is(dz, df, 0)
        condition = present(self.at, dz)
        place = self.at.index(z, f, self.at.g)
        parts = self.g_parts(z, f)
        if self.order == "zf":
            parts = parts + self.line_parts(dz, z, f)
        self.join(condition, place, parts)
        if self.order == "zf" and dz:
            self.send_line(condition, dz, z, f, place)
        elif df:
            self.send_f(condition, df, z, f, place)

    def third(self, dz):
        z, f = self.at.z + dz, self.at.f
        condition = present(self.at, dz)
        place = self.at.index(z, f, self.at.g)
        parts = self.f_parts(z)
        if self.order == "fz":
            parts = parts + self.line_parts(dz, z, f)
        self.join(condition, place, parts)
        if dz:
            self.send_line(condition, dz, z, f, place)

    def stages(self):
        order = line_targets(self.at)
        part = functools.partial
        begins = [part(self.begin, *item) for item in order]
        pairs = [part(self.over_pair, *item) for item in order]
        if self.order == "fz":
            seconds = [part(self.second, *item[:2]) for item in order if item[2] == 0]
            thirds = [part(self.third, dz) for dz in (-3, 3, -2, 2, -1, 1, 0)]
        else:
            dfs = list(range(1, self.at.nf)) + [0]
            seconds = [part(self.second, dz, df) for dz in (-3, 3, -2, 2, -1, 1, 0) for df in dfs]
            thirds = [part(self.third, 0)]
        return begins, pairs, seconds, thirds

    def store(self, target, start):
        place = self.at.index(self.at.z, self.at.f, self.at.g)
        target[:, pl.ds(start, self.acc.shape[2])] = self.acc[place].astype(F32)


def mixed(first, second):
    marked = []
    for kind, steps in enumerate((first, second)):
        marked += [((i + 0.5) / len(steps), kind, step) for i, step in enumerate(steps)]
    return [step for _, _, step in sorted(marked, key=lambda item: item[:2])]


def pipelined(scatters):
    begins, first, mids, lasts = [], [], [], []
    for scatter in scatters:
        starts, pairs, seconds, thirds = scatter.stages()
        begins += starts
        first += [step for step in pairs if step.args[2]]
        mid = []
        for second in seconds:
            mid += [step for step in pairs if step.args == (*second.args, 0)] + [second]
        mids.append(mid)
        lasts.append(thirds)
    events = list(first)
    for slot in range(len(scatters) + 1):
        some = lasts[slot - 1] if slot else []
        if slot < len(scatters):
            some = mixed(some, mids[slot]) if some else mids[slot]
        events += some
    return begins, events, len(first)


def lagged(events, lag, phase):
    def close(event):
        phase.ending = True
        event()
        phase.ending = False

    def step(number):
        events[number]()
        if number >= lag:
            close(events[number - lag])

    def rest():
        for event in events[-lag:]:
            close(event)

    return [functools.partial(step, number) for number in range(len(events))], rest


def split_scratch(refs, count):
    size = Scatter.PARTS
    return [refs[i * size : (i + 1) * size] for i in range(count)], refs[count * size :]


def scatter_sections(at, sources, spans, scratches, phase):
    scatters, places = [], []
    for number, parts in enumerate(spans):
        start = 0
        for size, order in parts:
            scratch = scratches[len(scatters)]
            scatters.append(Scatter(at, sources[number], pl.ds(start, size), order, scratch, phase))
            places.append((number, start))
            start += size
    return scatters, places


def scatter_kernel(sizes, spans, *refs):
    at = Place(*sizes)
    count, sections = len(spans), sum(len(parts) for parts in spans)
    sources, refs = refs[:count], refs[count:]
    input_ref, vector_ref, grad_ref, total_ref = refs[:4]
    owned, refs = refs[4 : 4 + count], refs[4 + count :]
    scratches, refs = split_scratch(refs, sections)
    sq_g, sq_f, sq_z, sq_c, trade_send, trade_recv, sq_send, sq_recv = refs
    slots = grad_ref.shape[0]
    peers, number = plane_peers(at)
    more, extra = slot_peers(at, slots)
    meet(peers + more, number + extra)
    phase = Phase()
    send = functools.partial(start_copy, phase)
    scatters, places = scatter_sections(at, sources, spans, scratches, phase)
    begins, events, _ = pipelined(scatters)
    steps, rest = lagged(events, 24, phase)
    other = 1 - at.core

    def vectors_g():
        for step in range(1, at.ng):
            device = at.device(at.z, at.f, (at.g + step) % at.ng)
            send(True, sq_g.at[at.g], sq_g.at[at.g], sq_send.at[0, step], sq_recv.at[0, at.g], device)

    def vectors_f():
        for step in range(1, at.nf):
            device = at.device(at.z, (at.f + step) % at.nf, at.g)
            send(True, sq_f.at[at.f], sq_f.at[at.f], sq_send.at[1, step], sq_recv.at[1, at.f], device)

    def line_send(condition, held, kind):
        device = at.device(at.z - 1 if kind else at.z + 1, at.f, at.g)
        send(condition, sq_z.at[held], sq_z.at[held], sq_send.at[2 + kind, held], sq_recv.at[2, held], device)

    def vectors_line(distance):
        for kind, held in enumerate((at.z - distance, at.z + distance)):
            there = held < LINE if kind else held >= 0
            onward = at.z > 0 if kind else at.z < LINE - 1
            if distance and not phase.ending:
                when(
                    there,
                    functools.partial(await_block, sq_z.at[held], sq_recv.at[2, held]),
                )
            line_send(both(there, onward), held, kind)

    def vectors_pair():
        send(
            True,
            sq_c.at[at.core],
            sq_c.at[at.core],
            sq_send.at[4, 0],
            sq_recv.at[3, at.core],
            at.partner(),
        )

    def sums():
        def g():
            for step in range(1, at.ng):
                peer = (at.g + step) % at.ng
                await_block(sq_g.at[peer], sq_recv.at[0, peer])
            total = sq_g[0]
            for number in range(1, at.ng):
                total = total + sq_g[number]
            sq_f[at.f] = total
            vectors_f()

        def f():
            for step in range(1, at.nf):
                peer = (at.f + step) % at.nf
                await_block(sq_f.at[peer], sq_recv.at[1, peer])
            total = sq_f[0]
            for number in range(1, at.nf):
                total = total + sq_f[number]
            sq_z[at.z] = total
            vectors_line(0)

        def pair():
            total = sq_z[0]
            for number in range(1, LINE):
                total = total + sq_z[number]
            sq_c[at.core] = total
            vectors_pair()

        return [g, f] + [functools.partial(vectors_line, d) for d in range(1, LINE)] + [pair]

    sq_g[at.g] = vector_ref[...]
    run_all(begins)
    vectors_g()
    trade_out(at, input_ref, grad_ref, trade_send, trade_recv, phase)
    run_all(mixed(steps, sums()))
    for scatter, (number, start) in zip(scatters, places):
        scatter.store(owned[number], start)
    await_block(sq_c.at[other], sq_recv.at[3, other])
    total_ref[...] = sq_c[0] + sq_c[1]

    rest()
    phase.ending = True
    run_all(begins)
    trade_out(at, input_ref, grad_ref, trade_send, trade_recv, phase)
    vectors_g()
    vectors_f()
    for distance in range(LINE):
        vectors_line(distance)
    vectors_pair()


def scatter_last(sources, spans, input_grad, vectors, slots, seq_size, fsdp_size):
    rows = sources[0].shape[0] // (seq_size * fsdp_size)
    own_rows, model = input_grad.shape
    positions = own_rows // slots
    nf, ng = seq_size // (2 * LINE), fsdp_size
    dma = pltpu.SemaphoreType.DMA
    widest = max(nf, ng, LINE)
    vmem = pl.BlockSpec(memory_space=pltpu.VMEM)
    scratch = []
    for parts in spans:
        for size, order in parts:
            scratch += Scatter.scratch(order, rows, size, nf, ng)
    return pl.pallas_call(
        functools.partial(scatter_kernel, (seq_size, fsdp_size), spans),
        out_shape=tuple(
            [
                jax.ShapeDtypeStruct((slots, positions, model), BF16),
                jax.ShapeDtypeStruct(vectors.shape, F32),
            ]
            + [jax.ShapeDtypeStruct((rows, source.shape[1]), F32) for source in sources]
        ),
        in_specs=[pl.BlockSpec(memory_space=pl.ANY)] * len(sources) + [vmem] * 2,
        out_specs=[vmem] * (2 + len(sources)),
        scratch_shapes=scratch
        + [pltpu.VMEM((size, *vectors.shape), F32) for size in (ng, nf, LINE, 2)]
        + [dma((slots,)), dma((slots,)), dma((5, widest)), dma((4, widest))],
        compiler_params=pltpu.CompilerParams(
            collective_id=3, has_side_effects=True, vmem_limit_bytes=63_000_000
        ),
        name="scatter_last",
    )(*sources, input_grad, vectors)


def first_half(shape):
    lane = lax.broadcasted_iota(jnp.int32, shape, 1)
    return lane % 64 < 32


def turn(values, cosine, sine):
    half = first_half(values.shape)
    away = jnp.where(half, -pltpu.roll(values, 96, 1), pltpu.roll(values, 32, 1))
    return values * cosine + away * sine


def turn_back(grads, cosine, sine):
    half = first_half(grads.shape)
    moved = grads * sine
    away = jnp.where(half, pltpu.roll(moved, 96, 1), -pltpu.roll(moved, 32, 1))
    return grads * cosine + away


def normalize(values):
    average = jnp.mean(values, axis=-1, keepdims=True)
    centered = values - average
    variance = jnp.mean(centered * centered, axis=-1, keepdims=True)
    inverse = lax.rsqrt(variance + EPS)
    return centered * inverse, inverse


def norm_back(grad_normed, normed, inverse, gain_values):
    scaled = grad_normed * gain_values
    first_mean = jnp.mean(scaled, axis=-1, keepdims=True)
    second_mean = jnp.mean(scaled * normed, axis=-1, keepdims=True)
    return inverse * (scaled - first_mean - normed * second_mean)


def head_lanes(shape, head):
    return lax.broadcasted_iota(jnp.int32, shape, 1) // 64 == head


def scores_of(keys, queries, bias):
    scores = lax.dot_general(keys, queries, (((1,), (1,)), ((), ())), preferred_element_type=F32)
    return scores + bias


def key_bias(length, shape):
    return jnp.where(lax.broadcasted_iota(jnp.int32, shape, 0) < length, 0.0, -jnp.inf)


def attend(length, queries, keys, values):
    queries = queries * 0.125
    bias = key_bias(length, (keys.shape[0], 1))
    zero = jnp.zeros((), BF16)
    total, logs = None, []
    for head in range(2):
        only = head_lanes(queries.shape, head)
        scores = scores_of(keys, jnp.where(only, queries, zero), bias)
        largest = jnp.max(scores, axis=0, keepdims=True)
        weights = jnp.exp(scores - largest)
        summed = jnp.sum(weights, axis=0, keepdims=True)
        logs.append(largest + jnp.log(summed))
        held = jnp.where(head_lanes(values.shape, head), values, zero)
        part = lax.dot_general(
            held, weights.astype(BF16), (((0,), (0,)), ((), ())), preferred_element_type=F32
        )
        part = part / summed
        total = part if total is None else total + part
    return total.T.astype(BF16), logs


FRONT_TILE = 512


def front_kernel(sizes, group, spans, *refs):
    at = Place(*sizes)
    count = len(spans)
    length_ref, x_ref, gains_ref, cos_ref, sin_ref, w_ref, dy_ref = refs[:7]
    sources, refs = refs[7 : 7 + count], refs[7 + count :]
    act_ref, gain_ref, q_ref, shared_out, o_ref, log_ref, dy_rows_ref = refs[:7]
    wholes, refs = refs[7 : 7 + count], refs[7 + count :]
    sems, (trade_send, trade_recv, share_send, share_recv, shared_ref, out_sem) = refs[:3], refs[3:]
    step = pl.program_id(0)
    rows, model = q_ref.shape
    slots = dy_ref.shape[0]
    tile = o_ref.shape[0]
    tiles = rows // tile
    projecting = 3 * model // FRONT_TILE
    steps = projecting + model // LANES * tiles
    kept = 2 * model // FRONT_TILE
    phase = Phase()
    sections = []
    for number, parts in enumerate(spans):
        start = 0
        for size, order in parts:
            sections.append((sources[number], wholes[number], pl.ds(start, size), order))
            start += size
    gather = Gather(at, sections, sems, phase)
    base, part = (at.seq // group) * group, at.seq % group
    members = [base + (part + other) % group for other in range(1, group)]
    own_rows = pl.ds(pl.multiple_of(part * rows, rows), rows)

    @pl.when(step == 0)
    def _():
        peers, number = plane_peers(at)
        more, extra = slot_peers(at, slots)
        others = [(True, (member, at.y)) for member in members]
        meet(peers + more + others, number + extra + group - 1)

    @pl.when(step == 0)
    def _():
        gather.begin()
        trade_in(at, dy_ref, dy_rows_ref, trade_send, trade_recv, phase)

    @pl.when(step == 0)
    def _():
        normed, _ = normalize(x_ref[...].astype(F32))
        turned = gains_ref[...].astype(F32).T
        gain_ref[...] = turned[:8]
        act_ref[...] = (normed * turned[:1]).astype(BF16)

    def share(number):
        place = shared_ref.at[own_rows, pl.ds(number * FRONT_TILE, FRONT_TILE)]
        for other, member in enumerate(members):
            start_copy(
                phase,
                True,
                place,
                place,
                share_send.at[number, other],
                share_recv.at[number, part],
                (member, at.y),
            )

    def receive():
        for number in range(kept):
            for other in range(1, group):
                source = (part + other) % group
                place = shared_ref.at[
                    pl.ds(pl.multiple_of(source * rows, rows), rows),
                    pl.ds(number * FRONT_TILE, FRONT_TILE),
                ]
                await_block(place, share_recv.at[number, source])
        pltpu.make_async_copy(shared_ref, shared_out, out_sem).start()

    for number in range(kept):
        pl.when(step == number + 1)(functools.partial(share, number))
    pl.when(step == projecting)(receive)

    @pl.when(step < projecting)
    def _():
        mixed = jnp.dot(act_ref[...], w_ref[...], preferred_element_type=F32)

        def turned():
            cosine, sine = cos_ref[...], sin_ref[...]
            pieces = [
                turn(mixed[:, start : start + LANES], cosine, sine).astype(BF16)
                for start in range(0, FRONT_TILE, LANES)
            ]
            return jnp.concatenate(pieces, axis=1)

        @pl.when(step < kept // 2)
        def _():
            columns = pl.ds(pl.multiple_of(step * FRONT_TILE, FRONT_TILE), FRONT_TILE)
            shared_ref[own_rows, columns] = turned()

        @pl.when(both(step >= kept // 2, step < kept))
        def _():
            columns = pl.ds(pl.multiple_of(step * FRONT_TILE, FRONT_TILE), FRONT_TILE)
            shared_ref[own_rows, columns] = mixed.astype(BF16)

        @pl.when(step >= kept)
        def _():
            columns = pl.ds(pl.multiple_of((step - kept) * FRONT_TILE, FRONT_TILE), FRONT_TILE)
            q_ref[:, columns] = turned()

    @pl.when(step >= projecting)
    def _():
        pair, piece = (step - projecting) // tiles, (step - projecting) % tiles
        start = pl.multiple_of(pair * LANES, LANES)
        out, logs = attend(
            length_ref[0],
            q_ref[pl.ds(pl.multiple_of(piece * tile, tile), tile), pl.ds(start, LANES)],
            shared_ref[:, pl.ds(start, LANES)],
            shared_ref[:, pl.ds(pl.multiple_of(model + start, LANES), LANES)],
        )
        o_ref[...] = out
        for head in range(2):
            log_ref[0, head : head + 1, :] = logs[head]

    events, rest = gather.steps(24)
    pace = FRONT_PACE
    for number in range(steps - 1):
        group_events = events[number * pace : (number + 1) * pace]
        if group_events:
            pl.when(step == number)(functools.partial(run_all, group_events))

    @pl.when(step == steps - 1)
    def _():
        run_all(events[(steps - 1) * pace :])
        rest()
        phase.ending = True
        trade_in(at, dy_ref, dy_rows_ref, trade_send, trade_recv, phase)
        for number in range(kept):
            share(number)
        pltpu.make_async_copy(shared_ref, shared_out, out_sem).wait()
        phase.ending = False


FRONT_PACE = 4


def front(length, x_rows, cosine, sine, weight, dy, sources, spans, group, tile, seq_size, fsdp_size):
    rows, model = x_rows.shape
    slots, positions, _ = dy.shape
    pairs, tiles = model // LANES, rows // tile
    projecting, kept = 3 * model // FRONT_TILE, 2 * model // FRONT_TILE
    nf, ng = seq_size // (2 * LINE), fsdp_size
    devices = seq_size * fsdp_size
    count = sum(len(parts) for parts in spans)
    dma = pltpu.SemaphoreType.DMA
    vmem, anywhere = pl.BlockSpec(memory_space=pltpu.VMEM), pl.BlockSpec(memory_space=pl.ANY)

    def pair_of(i):
        return jnp.maximum(i - projecting, 0) // tiles

    def tile_of(i):
        return jnp.maximum(i - projecting, 0) % tiles

    return pl.pallas_call(
        functools.partial(front_kernel, (seq_size, fsdp_size), group, spans),
        grid=(projecting + pairs * tiles,),
        out_shape=tuple(
            [
                jax.ShapeDtypeStruct((rows, model), BF16),
                jax.ShapeDtypeStruct((8, model), F32),
                jax.ShapeDtypeStruct((rows, model), BF16),
                jax.ShapeDtypeStruct((rows * group, 2 * model), BF16),
                jax.ShapeDtypeStruct((rows, model), BF16),
                jax.ShapeDtypeStruct((pairs, 8, rows), F32),
                jax.ShapeDtypeStruct((slots * positions, model), BF16),
            ]
            + [
                jax.ShapeDtypeStruct((source.shape[0] * devices, source.shape[1]), BF16)
                for source in sources
            ]
        ),
        in_specs=[pl.BlockSpec(memory_space=pltpu.SMEM), vmem]
        + [pl.BlockSpec((model, LANES), lambda i: (0, 3 * model // LANES)), vmem, vmem]
        + [
            pl.BlockSpec(
                (model, FRONT_TILE),
                lambda i: (0, (jnp.minimum(i, projecting - 1) + projecting - kept) % projecting),
            )
        ]
        + [vmem] * (1 + len(sources)),
        out_specs=[
            vmem,
            vmem,
            vmem,
            anywhere,
            pl.BlockSpec((tile, LANES), lambda i: (tile_of(i), pair_of(i))),
            pl.BlockSpec((1, 8, tile), lambda i: (pair_of(i), 0, tile_of(i))),
        ]
        + [anywhere] * (1 + len(sources)),
        scratch_shapes=Gather.scratch(count, nf, ng)
        + [dma((slots,)), dma((slots,)), dma((kept, group)), dma((kept, group))]
        + [pltpu.VMEM((rows * group, 2 * model), BF16), dma],
        compiler_params=pltpu.CompilerParams(
            collective_id=1, has_side_effects=True, vmem_limit_bytes=63_000_000
        ),
        name="front",
    )(length, x_rows, weight, cosine, sine, weight, dy, *sources)


def attend_back(length, queries, keys, values, grads, heads_out, logs):
    queries = queries * 0.125
    bias = key_bias(length, (keys.shape[0], 1))
    zero = jnp.zeros((), BF16)
    product = (grads.astype(F32) * heads_out.astype(F32)).T
    dq = dk = dv = None
    for head in range(2):
        only = head_lanes(queries.shape, head)
        query = jnp.where(only, queries, zero)
        grad = jnp.where(only, grads, zero)
        key = jnp.where(head_lanes(keys.shape, head), keys, zero)
        delta = jnp.sum(product[64 * head : 64 * head + 64], axis=0, keepdims=True)
        scores = scores_of(keys, query, bias)
        probs = jnp.exp(scores - logs[head : head + 1])
        grad_probs = lax.dot_general(
            values, grad, (((1,), (1,)), ((), ())), preferred_element_type=F32
        )
        grad_scores = (probs * (grad_probs - delta)).astype(BF16)
        value_part = jnp.dot(probs.astype(BF16), grad, preferred_element_type=F32)
        key_part = jnp.dot(grad_scores, query, preferred_element_type=F32)
        query_part = lax.dot_general(
            key, grad_scores, (((0,), (0,)), ((), ())), preferred_element_type=F32
        )
        dq = query_part if dq is None else dq + query_part
        dk = key_part if dk is None else dk + key_part
        dv = value_part if dv is None else dv + value_part
    return dq.T * 0.125, dk, dv


def back_kernel(sizes, group, spans, *refs):
    at = Place(*sizes)
    sections = sum(len(parts) for parts in spans)
    count = len(spans)
    length_ref, q_ref, k_ref, v_ref, g_ref, o_ref, log_ref, cos_ref, sin_ref, result_ref = refs[:10]
    sources, refs = refs[10 : 10 + count], refs[10 + count :]
    mixed_ref, out_ref = refs[:2]
    owned, refs = refs[2 : 2 + count], refs[2 + count :]
    scratches, refs = split_scratch(refs, sections)
    dk_acc, dv_acc, parts_ref, arrived, sum_send, sum_recv, trade_send, trade_recv = refs
    step = pl.program_id(0)
    tile = q_ref.shape[0]
    rows, model = result_ref.shape
    tiles, pairs = rows // tile, model // LANES
    steps = pairs * tiles + 1
    slots = out_ref.shape[0]
    phase = Phase()
    scatters, places = scatter_sections(at, sources, spans, scratches, phase)
    begins, events, ahead = pipelined(scatters)
    events, rest = lagged(events, 40, phase)
    base, part = (at.seq // group) * group, at.seq % group
    members = [base + (part + other) % group for other in range(1, group)]

    def columns_of(pair):
        return pl.ds(pl.multiple_of(pair * LANES, LANES), LANES)

    def share(pair):
        for kind in range(2):
            for other, member in enumerate(members):
                owner = (part + other + 1) % group
                start_copy(
                    phase,
                    True,
                    parts_ref.at[kind, pl.ds(pl.multiple_of(owner * rows, rows), rows), columns_of(pair)],
                    arrived.at[kind, other, :, columns_of(pair)],
                    sum_send.at[kind, other, pair],
                    sum_recv.at[kind, other, pair],
                    (member, at.y),
                )

    @pl.when(step == 0)
    def _():
        peers, number = plane_peers(at)
        more, extra = slot_peers(at, slots)
        others = [(True, (member, at.y)) for member in members]
        meet(peers + more + others, number + extra + group - 1)
        run_all(begins)
        trade_out(at, result_ref, out_ref, trade_send, trade_recv, phase)
        run_all(events[:ahead])

    for number in range(1, steps):
        some = events[ahead + (number - 1) * BACK_PACE : ahead + number * BACK_PACE]
        if some:
            pl.when(step == number)(functools.partial(run_all, some))

    pl.when(both(step > 0, step % tiles == 0))(lambda: share(step // tiles - 1))

    @pl.when(step < steps - 1)
    def _():
        pair, piece = step // tiles, step % tiles
        own = pl.ds(pl.multiple_of(piece * tile, tile), tile)
        dq, dk, dv = attend_back(
            length_ref[0], q_ref[...], k_ref[...], v_ref[...], g_ref[...], o_ref[...], log_ref[0]
        )
        mixed_ref[own, columns_of(pair)] = turn_back(dq, cos_ref[own], sin_ref[own]).astype(BF16)
        if tiles == 1:
            parts_ref[0, :, columns_of(pair)] = dk.astype(BF16)
            parts_ref[1, :, columns_of(pair)] = dv.astype(BF16)
            return

        @pl.when(piece == 0)
        def _():
            dk_acc[...] = dk
            dv_acc[...] = dv

        @pl.when(piece > 0)
        def _():
            dk_acc[...] += dk
            dv_acc[...] += dv

        @pl.when(piece == tiles - 1)
        def _():
            parts_ref[0, :, columns_of(pair)] = dk_acc[...].astype(BF16)
            parts_ref[1, :, columns_of(pair)] = dv_acc[...].astype(BF16)

    def add_parts():
        own = pl.ds(pl.multiple_of(part * rows, rows), rows)

        def body(pair, carry):
            for kind in range(2):
                total = parts_ref[kind, own, columns_of(pair)].astype(F32)
                for other in range(group - 1):
                    piece = arrived.at[kind, other, :, columns_of(pair)]
                    await_block(piece, sum_recv.at[kind, other, pair])
                    total = total + piece[...].astype(F32)
                if kind == 0:
                    total = turn_back(total, cos_ref[...], sin_ref[...])
                start = pl.multiple_of((kind + 1) * model + pair * LANES, LANES)
                mixed_ref[:, pl.ds(start, LANES)] = total.astype(BF16)
            return carry

        lax.fori_loop(0, pairs, body, 0)

    @pl.when(step == steps - 1)
    def _():
        add_parts()
        run_all(events[ahead + (steps - 1) * BACK_PACE :])
        for scatter, (number, start) in zip(scatters, places):
            scatter.store(owned[number], start)
        rest()
        phase.ending = True
        run_all(begins)
        trade_out(at, result_ref, out_ref, trade_send, trade_recv, phase)

        def body(pair, carry):
            share(pair)
            return carry

        lax.fori_loop(0, pairs, body, 0)
        phase.ending = False


BACK_PACE = 3


def back(length, queries, shared, grads, heads_out, logs, cosine, sine, result, sources, spans, tile, slots, seq_size, fsdp_size):
    rows, keys, model = queries.shape[0], shared.shape[0], queries.shape[1]
    group, positions = keys // rows, rows // slots
    pairs, tiles = model // LANES, rows // tile
    nf, ng = seq_size // (2 * LINE), fsdp_size
    devices = seq_size * fsdp_size
    shard = sources[0].shape[0] // devices
    vmem, anywhere = pl.BlockSpec(memory_space=pltpu.VMEM), pl.BlockSpec(memory_space=pl.ANY)
    dma = pltpu.SemaphoreType.DMA

    def pair_of(i):
        return jnp.minimum(i, pairs * tiles - 1) // tiles

    def tile_of(i):
        return jnp.minimum(i, pairs * tiles - 1) % tiles

    by_row = pl.BlockSpec((tile, LANES), lambda i: (tile_of(i), pair_of(i)))
    scratch = []
    for parts in spans:
        for size, order in parts:
            scratch += Scatter.scratch(order, shard, size, nf, ng)
    return pl.pallas_call(
        functools.partial(back_kernel, (seq_size, fsdp_size), group, spans),
        grid=(pairs * tiles + 1,),
        out_shape=tuple(
            [
                jax.ShapeDtypeStruct((rows, 3 * model), BF16),
                jax.ShapeDtypeStruct((slots, positions, model), BF16),
            ]
            + [jax.ShapeDtypeStruct((shard, source.shape[1]), F32) for source in sources]
        ),
        in_specs=[
            pl.BlockSpec(memory_space=pltpu.SMEM),
            by_row,
            pl.BlockSpec((keys, LANES), lambda i: (0, pair_of(i))),
            pl.BlockSpec((keys, LANES), lambda i: (0, pairs + pair_of(i))),
            by_row,
            by_row,
            pl.BlockSpec((1, 8, tile), lambda i: (pair_of(i), 0, tile_of(i))),
            vmem,
            vmem,
            vmem,
        ]
        + [anywhere] * len(sources),
        out_specs=[vmem, anywhere] + [vmem] * len(sources),
        scratch_shapes=scratch
        + [
            pltpu.VMEM((keys, LANES), F32),
            pltpu.VMEM((keys, LANES), F32),
            pltpu.VMEM((2, keys, model), BF16),
            pltpu.VMEM((2, group - 1, rows, model), BF16),
            dma((2, group - 1, pairs)),
            dma((2, group - 1, pairs)),
            dma((slots,)),
            dma((slots,)),
        ],
        compiler_params=pltpu.CompilerParams(
            collective_id=2, has_side_effects=True, vmem_limit_bytes=67_000_000
        ),
        name="back",
    )(length, queries, shared, shared, grads, heads_out, logs, cosine, sine, result, *sources)


def rotary_tables(places, head_size):
    halfway = head_size // 2
    ladder = jnp.arange(halfway, dtype=F32) * (2.0 / head_size)
    inverse = 1.0 / THETA**ladder
    angles = places.astype(F32)[:, None] * inverse[None, :]
    angles = jnp.concatenate([angles] * 4, axis=-1)
    return jnp.cos(angles), jnp.sin(angles)


def gelu_exact(values):
    return jax.nn.gelu(values, approximate=False)


def mm(left, right):
    return jnp.dot(left, right, preferred_element_type=F32)


def mm_right_t(left, right):
    return lax.dot_general(left, right, (((1,), (1,)), ((), ())), preferred_element_type=F32)


def mm_left_t(left, right):
    return lax.dot_general(left, right, (((0,), (0,)), ((), ())), preferred_element_type=F32)


def shards(
    hidden_in,
    out_grad,
    qkv_weight,
    attn_out_weight,
    in_weight,
    down_weight,
    attn_gain,
    mlp_gain,
    seq_lengths,
    slot_order,
):
    seq_size, fsdp_size = lax.axis_size("seq"), lax.axis_size("fsdp")
    seq_place, fsdp_place = lax.axis_index("seq"), lax.axis_index("fsdp")
    slots, positions, model = hidden_in.shape
    shard = qkv_weight.shape[0]
    ff = down_weight.shape[0]
    wide = up_to(ff, LANES)
    spare = wide - ff
    group = seq_size // slots
    rows = slots * positions
    head_size = model // HEADS

    lead = jnp.zeros((shard, spare), BF16)
    gains = jnp.concatenate(
        [attn_gain[:, None], mlp_gain[:, None], jnp.zeros((shard, LANES - 2), BF16)], axis=1
    )
    in_pack = jnp.concatenate([in_weight[:, :ff], lead, in_weight[:, ff:], lead], axis=1)
    down_pack = jnp.concatenate([down_weight.T, lead], axis=1)
    w_qkv, x_rows = gather_first(qkv_weight, gains, hidden_in, seq_size, fsdp_size)

    slot = fsdp_place * slots + seq_place // group
    order = jnp.sum(jnp.where(jnp.arange(slot_order.shape[0]) == slot, slot_order, 0))
    length = jnp.sum(jnp.where(jnp.arange(seq_lengths.shape[0]) == order, seq_lengths, 0))
    lengths = length.astype(jnp.int32)[None]
    places = (seq_place % group) * rows + jnp.arange(rows, dtype=jnp.int32)
    valid = (places < length).astype(F32)[:, None]
    cosine, sine = rotary_tables(places, head_size)

    tile = 512 if rows % 512 == 0 and rows * group <= 1024 else 128
    act_one, gain_rows, queries, shared, heads_out, logs, dy_rows, w_attn, w_input, w_down = front(
        lengths,
        x_rows,
        cosine,
        sine,
        w_qkv,
        out_grad,
        (attn_out_weight, in_pack, down_pack),
        (((model, "fzg-"),), ((wide, "zfg"), (wide, "zfg")), ((wide, "fzg"),)),
        group,
        tile,
        seq_size,
        fsdp_size,
    )
    gain_attn, gain_mlp = gain_rows[0:1], gain_rows[1:2]

    x_wide = x_rows.astype(F32)
    attn = mm(heads_out, w_attn)
    middle = x_wide + attn
    normed_two, inverse_two = normalize(middle)
    act_two = (normed_two * gain_mlp).astype(BF16)
    joined = mm(act_two, w_input)
    input_half = joined[:, :wide]
    gate_half = joined[:, wide:]
    active, active_pull = jax.vjp(gelu_exact, input_half)
    product = (active * gate_half).astype(BF16)
    branch = mm_right_t(product, w_down)
    result = (middle + branch) * valid
    squares = [
        jnp.sum(valid * tensor * tensor, axis=0) for tensor in (x_wide, middle, result, attn, branch)
    ]

    grad_y = dy_rows.astype(F32) * valid
    grad_branch = grad_y.astype(BF16)
    down_part = mm_left_t(grad_branch, product).astype(BF16)
    grad_product = mm(grad_branch, w_down)
    grad_joined = jnp.concatenate(
        [active_pull(grad_product * gate_half)[0], grad_product * active], axis=1
    ).astype(BF16)
    input_part = mm_left_t(act_two, grad_joined).astype(BF16)
    grad_act_two = mm_right_t(grad_joined, w_input)
    mlp_gain_part = jnp.sum(grad_act_two * normed_two, axis=0)
    grad_middle = grad_y + norm_back(grad_act_two, normed_two, inverse_two, gain_mlp)
    grad_attn = grad_middle.astype(BF16)
    attn_part = mm_left_t(heads_out, grad_attn).astype(BF16)
    grad_heads = mm_right_t(grad_attn, w_attn).astype(BF16)

    second = "zf" if seq_size == 4 * LINE else "fz"
    early = [(attn_part, ((model, second),)), (down_part, ((wide, second),))]
    wide_part = (input_part, ((wide, "fz"), (wide, "fz")))
    if rows * group <= 1024:
        early, late = [early[1], wide_part, early[0]], []
    else:
        late = [wide_part]
    grad_mixed, out_rows, *owned = back(
        lengths,
        queries,
        shared,
        grad_heads,
        heads_out,
        logs,
        cosine,
        sine,
        result.astype(BF16),
        [part for part, _ in early],
        tuple(parts for _, parts in early),
        tile,
        slots,
        seq_size,
        fsdp_size,
    )
    qkv_part = mm_left_t(act_one, grad_mixed).astype(BF16)
    grad_act_one = mm_right_t(grad_mixed, w_qkv[:, : 3 * model])
    normed_one, inverse_one = normalize(x_wide)
    attn_gain_part = jnp.sum(grad_act_one * normed_one, axis=0)
    grad_x = grad_middle + norm_back(grad_act_one, normed_one, inverse_one, gain_attn)

    vectors = jnp.stack(squares + [attn_gain_part, mlp_gain_part, jnp.zeros((model,), F32)])
    half = 3 * model // 2
    late.append((qkv_part, ((half, "fz"), (half, second))))
    grad_rows, totals, *more = scatter_last(
        [part for part, _ in late],
        tuple(parts for _, parts in late),
        grad_x.astype(BF16),
        vectors,
        slots,
        seq_size,
        fsdp_size,
    )
    own_qkv = more[-1]
    if late[0] is wide_part:
        (own_attn, own_down), own_in = owned, more[0]
    else:
        own_down, own_in, own_attn = owned
    tokens_valid = jnp.sum(seq_lengths).astype(F32)
    root_squares = jnp.sqrt(jnp.sum(totals[:5], axis=1) / (tokens_valid * model))
    own_gains = lax.dynamic_slice_in_dim(totals, (seq_place * fsdp_size + fsdp_place) * shard, shard, 1)
    return (
        out_rows,
        grad_rows,
        own_qkv,
        own_attn,
        jnp.concatenate([own_in[:, :ff], own_in[:, wide : wide + ff]], axis=1),
        own_down[:, :ff].T,
        own_gains[5],
        own_gains[6],
        root_squares,
    )


def solution(mesh):
    placed = (
        P("fsdp", "seq", None),
        P("fsdp", "seq", None),
        P(("seq", "fsdp"), None),
        P(("seq", "fsdp"), None),
        P(("seq", "fsdp"), None),
        P(None, ("seq", "fsdp")),
        P(("seq", "fsdp")),
        P(("seq", "fsdp")),
        P(),
        P(),
    )
    return jax.shard_map(
        shards,
        mesh=mesh,
        in_specs=placed,
        out_specs=(
            P("fsdp", "seq", None),
            P("fsdp", "seq", None),
            P(("seq", "fsdp"), None),
            P(("seq", "fsdp"), None),
            P(("seq", "fsdp"), None),
            P(None, ("seq", "fsdp")),
            P(("seq", "fsdp")),
            P(("seq", "fsdp")),
            P(),
        ),
        check_vma=False,
    )
```

```python
import functools

import jax
import jax.numpy as jnp
from jax import lax
from jax.experimental import pallas as pl
from jax.experimental.pallas import tpu as pltpu
from jax.sharding import PartitionSpec as P

HEADS = 16
LINE = 4
LANES = 128
EPS = 1e-05
THETA = 160000.0
F32 = jnp.float32
BF16 = jnp.bfloat16
MESH = pl.DeviceIdType.MESH


def up_to(size, unit):
    return -(-size // unit) * unit


class Place:
    def __init__(self, seq_size, fsdp_size, swap=True):
        self.seq_size, self.fsdp_size = seq_size, fsdp_size
        self.rest = seq_size // (2 * LINE)
        self.swap = swap and self.rest == fsdp_size
        self.nf, self.ng = self.rest, fsdp_size
        self.blocks = LINE * self.nf * self.ng
        self.seq = lax.axis_index("seq")
        self.y = lax.axis_index("fsdp")
        self.core = self.seq % 2
        self.r = (self.seq // 2) % self.rest
        self.z = self.seq // (2 * self.rest)
        self.f, self.g = self.split(self.r, self.y, self.core)

    def split(self, r, y, core):
        if not self.swap:
            return r, y
        return (1 - core) * r + core * y, (1 - core) * y + core * r

    def device(self, z, f, g, core=None):
        core = self.core if core is None else core
        r, y = self.split(f, g, core)
        return (z * self.rest + r) * 2 + core, y

    def row_block(self, z, f, g, core=None):
        seq, y = self.device(z, f, g, core)
        return seq * self.fsdp_size + y

    def index(self, z, f, g):
        return (z * self.nf + f) * self.ng + g

    def partner(self):
        return self.seq + 1 - 2 * self.core, self.y


def both(first, second):
    if first is True:
        return second
    if second is True:
        return first
    return jnp.logical_and(first, second)


def when(condition, body):
    if condition is True:
        body()
    else:
        pl.when(condition)(body)


def meet(peers, awaited):
    barrier = pltpu.get_barrier_semaphore()
    for condition, device in peers:
        when(
            condition,
            functools.partial(
                pl.semaphore_signal, barrier, inc=1, device_id=device, device_id_type=MESH
            ),
        )
    pl.semaphore_wait(barrier, awaited)


def plane_peers(at):
    below, above = at.z > 0, at.z < LINE - 1
    peers = [
        (below, at.device(at.z - 1, at.f, at.g)),
        (above, at.device(at.z + 1, at.f, at.g)),
        (True, at.partner()),
    ]
    for step in range(1, at.nf):
        peers.append((True, at.device(at.z, (at.f + step) % at.nf, at.g)))
    for step in range(1, at.ng):
        peers.append((True, at.device(at.z, at.f, (at.g + step) % at.ng)))
    count = 1 + (at.nf - 1) + (at.ng - 1)
    count = count + jnp.where(below, 1, 0) + jnp.where(above, 1, 0)
    return peers, count


def slot_peers(at, slots):
    group = at.seq_size // slots
    own_slot, own_part = at.seq // group, at.seq % group
    same = at.seq // slots == own_part
    peers = []
    for step in range(slots):
        wide = ((own_slot + step) % slots) * group + at.seq // slots
        narrow = own_part * slots + (at.seq + step) % slots
        condition = True if step else jnp.logical_not(same)
        peers.append((condition, (wide, at.y)))
        peers.append((condition, (narrow, at.y)))
    return peers, 2 * slots - 2 * jnp.where(same, 1, 0)


def steps_of(at):
    out = []
    for dz in (0, -1, 1, -2, 2, -3, 3):
        for df in range(at.nf):
            for dg in range(at.ng):
                out.append((abs(dz) + (df > 0) + (dg > 0), dz, df, dg))
    out.sort(key=lambda item: item[0])
    return out


def present(at, dz):
    if dz == 0:
        return True
    return at.z + dz >= 0 if dz < 0 else at.z + dz < LINE


class Gather:
    def __init__(self, at, sections, sems, phase):
        self.at, self.sections, self.phase = at, sections, phase
        plain = Place(at.seq_size, at.fsdp_size, swap=False)
        self.places = [plain if section[3][-1] == "-" else at for section in sections]
        self.send_sems, self.plane_sems, self.pair_sems = sems

    @staticmethod
    def scratch(count, nf, ng):
        dma = pltpu.SemaphoreType.DMA
        blocks, kinds = LINE * nf * ng, 3 + (nf - 1) + (ng - 1)
        return [dma((count, blocks, kinds)), dma((count, blocks)), dma((count, blocks + 1))]

    def own(self, number):
        source, _, columns, _ = self.sections[number]
        return source.at[:, columns]

    def block(self, number, z, f, g):
        source, whole, columns, _ = self.sections[number]
        rows = source.shape[0]
        start = pl.multiple_of(self.places[number].row_block(z, f, g) * rows, rows)
        return whole.at[pl.ds(start, rows), columns]

    def forward(self, number, condition, source, dz, df, dg):
        at, order = self.places[number], self.sections[number][3].strip("-")
        z, f, g = at.z + dz, (at.f + df) % at.nf, (at.g + dg) % at.ng
        place, target = at.index(z, f, g), self.block(number, z, f, g)
        moved = {"z": dz, "f": df, "g": dg}
        last = max([i for i, axis in enumerate(order) if moved[axis]], default=-1)

        def send(allowed, kind, device, pair=False):
            sem = (self.pair_sems if pair else self.plane_sems).at[number, place]
            start_copy(
                self.phase,
                both(condition, allowed),
                source,
                target,
                self.send_sems.at[number, place, kind],
                sem,
                device,
            )

        for i, axis in enumerate(order):
            if axis == "z" and i >= last:
                rising, sinking = dz <= 0, dz >= 0
                if rising:
                    send(at.z < LINE - 1, 0, at.device(at.z + 1, at.f, at.g))
                if sinking:
                    send(at.z > 0, 1, at.device(at.z - 1, at.f, at.g))
            if axis == "f" and i > last:
                for step in range(1, at.nf):
                    send(True, 1 + step, at.device(at.z, (at.f + step) % at.nf, at.g))
            if axis == "g" and i > last:
                for step in range(1, at.ng):
                    send(True, at.nf + step, at.device(at.z, at.f, (at.g + step) % at.ng))
        send(True, at.nf + at.ng, at.partner(), pair=True)

    def begin(self):
        for number in range(len(self.sections)):
            at = self.places[number]
            self.forward(number, True, self.own(number), 0, 0, 0)
            own = pltpu.make_async_copy(
                self.own(number),
                self.block(number, at.z, at.f, at.g),
                self.pair_sems.at[number, at.blocks],
            )
            if self.phase.ending:
                own.wait()
            else:
                own.start()

    def arrival(self, number, dz, df, dg):
        at = self.places[number]
        z, f, g = at.z + dz, (at.f + df) % at.nf, (at.g + dg) % at.ng
        condition = present(at, dz)
        block = self.block(number, z, f, g)
        sem = self.plane_sems.at[number, at.index(z, f, g)]
        if not self.phase.ending:
            when(condition, functools.partial(await_block, block, sem))
        self.forward(number, condition, block, dz, df, dg)

    def events(self):
        marked = [
            (hops, number, place, item)
            for place, (hops, *item) in enumerate(steps_of(self.at)[1:])
            for number in range(len(self.sections))
        ]
        marked.sort(key=lambda entry: entry[:3])
        return [functools.partial(self.arrival, number, *item) for _, number, _, item in marked]

    def from_partner(self, number, dz, df, dg):
        at = self.places[number]
        f, g = at.split(*at.split(at.f, at.g, at.core), 1 - at.core)
        z, f, g = at.z + dz, (f + df) % at.nf, (g + dg) % at.ng
        sem = self.pair_sems.at[number, at.index(z, f, g)]
        when(
            present(at, dz), functools.partial(await_block, self.block(number, 0, 0, 0), sem)
        )

    def steps(self, lag):
        events = self.events()

        def close(event):
            self.phase.ending = True
            event()
            self.from_partner(*event.args)
            self.phase.ending = False

        def step(number):
            events[number]()
            if number >= lag:
                close(events[number - lag])

        def rest():
            for event in events[-lag:]:
                close(event)
            self.phase.ending = True
            self.begin()
            for number in range(len(self.sections)):
                self.from_partner(number, 0, 0, 0)
            self.phase.ending = False

        return [functools.partial(step, number) for number in range(len(events))], rest


def trade_in(at, source_ref, target_ref, send_sems, recv_sems, phase):
    slots, positions = source_ref.shape[0], source_ref.shape[1]
    group = at.seq_size // slots
    own_slot, own_part = at.seq // group, at.seq % group
    same = at.seq // slots == own_part
    lane = at.seq % slots
    target = target_ref.at[pl.ds(pl.multiple_of(lane * positions, positions), positions), :]
    for step in range(slots):
        slot = (own_slot + step) % slots
        if step == 0 and not phase.ending:
            local = pltpu.make_async_copy(source_ref.at[slot], target, recv_sems.at[lane])
            when(same, local.start)
        start_copy(
            phase,
            True if step else jnp.logical_not(same),
            source_ref.at[slot],
            target,
            send_sems.at[step],
            recv_sems.at[lane],
            (slot * group + at.seq // slots, at.y),
        )
        if phase.ending:
            await_block(target_ref.at[pl.ds(step * positions, positions), :], recv_sems.at[step])


def trade_out(at, source_ref, target_ref, send_sems, recv_sems, phase):
    slots, positions = target_ref.shape[0], target_ref.shape[1]
    group = at.seq_size // slots
    own_slot, own_part = at.seq // group, at.seq % group
    same = at.seq // slots == own_part
    target = target_ref.at[own_slot]
    for step in range(slots):
        lane = (at.seq + step) % slots
        source = source_ref.at[pl.ds(pl.multiple_of(lane * positions, positions), positions), :]
        if step == 0 and not phase.ending:
            local = pltpu.make_async_copy(source, target, recv_sems.at[own_slot])
            when(same, local.start)
        start_copy(
            phase,
            True if step else jnp.logical_not(same),
            source,
            target,
            send_sems.at[step],
            recv_sems.at[own_slot],
            (own_part * slots + lane, at.y),
        )
        if phase.ending:
            await_block(target_ref.at[step], recv_sems.at[step])


def first_kernel(sizes, spans, weight_ref, gains_ref, hidden_ref, whole_ref, rows_ref, *refs):
    at = Place(*sizes)
    sems, (trade_send, trade_recv, pack_ref, pack_sems) = refs[:3], refs[3:]
    width, extra_width = weight_ref.shape[1], gains_ref.shape[1]
    loads = [
        pltpu.make_async_copy(weight_ref, pack_ref.at[:, pl.ds(0, width)], pack_sems.at[0]),
        pltpu.make_async_copy(gains_ref, pack_ref.at[:, pl.ds(width, extra_width)], pack_sems.at[1]),
    ]
    for load in loads:
        load.start()
    peers, count = plane_peers(at)
    more, extra = slot_peers(at, hidden_ref.shape[0])
    meet(peers + more, count + extra)
    for load in loads:
        load.wait()
    phase = Phase()
    sections, start = [], 0
    for size, order in spans:
        sections.append((pack_ref, whole_ref, pl.ds(start, size), order))
        start += size
    gather = Gather(at, sections, sems, phase)
    steps, rest = gather.steps(12)
    gather.begin()
    trade_in(at, hidden_ref, rows_ref, trade_send, trade_recv, phase)
    run_all(steps)
    rest()
    phase.ending = True
    trade_in(at, hidden_ref, rows_ref, trade_send, trade_recv, phase)


def gather_first(weight, gains, hidden, seq_size, fsdp_size):
    slots, positions, model = hidden.shape
    nf, ng = seq_size // (2 * LINE), fsdp_size
    devices = seq_size * fsdp_size
    dma = pltpu.SemaphoreType.DMA
    shard, width = weight.shape[0], weight.shape[1] + gains.shape[1]
    half = weight.shape[1] // 2
    spans = ((half, "zfg"), (width - half, "zfg"))
    return pl.pallas_call(
        functools.partial(first_kernel, (seq_size, fsdp_size), spans),
        out_shape=(
            jax.ShapeDtypeStruct((shard * devices, width), BF16),
            jax.ShapeDtypeStruct((slots * positions, model), BF16),
        ),
        in_specs=[pl.BlockSpec(memory_space=pltpu.VMEM)] * 3,
        out_specs=[pl.BlockSpec(memory_space=pl.ANY)] * 2,
        scratch_shapes=Gather.scratch(len(spans), nf, ng)
        + [dma((slots,)), dma((slots,)), pltpu.VMEM((shard, width), BF16), dma((2,))],
        compiler_params=pltpu.CompilerParams(collective_id=0, has_side_effects=True),
        name="gather_first",
    )(weight, gains, hidden)


def add_blocks(target, others):
    width = target.shape[1]
    piece = max(size for size in range(LANES, 1025, LANES) if width % size == 0)

    def body(number, carry):
        columns = pl.ds(pl.multiple_of(number * piece, LANES), piece)
        total = target[:, columns].astype(F32)
        for other in others:
            total = total + other[:, columns].astype(F32)
        target[:, columns] = total.astype(target.dtype)
        return carry

    lax.fori_loop(0, width // piece, body, 0)


def line_targets(at):
    order = []
    for dz in (-3, 3, -2, 2, -1, 1, 0):
        for df in list(range(1, at.nf)) + [0]:
            for dg in list(range(1, at.ng)) + [0]:
                order.append((dg == 0, df == 0, -abs(dz), dz, df, dg))
    order.sort(key=lambda item: item[:3])
    return [item[3:] for item in order]


class Phase:
    def __init__(self):
        self.ending = False


def start_copy(phase, condition, source, target, send_sem, recv_sem, device):
    copy = pltpu.make_async_remote_copy(
        src_ref=source,
        dst_ref=target,
        send_sem=send_sem,
        recv_sem=recv_sem,
        device_id=device,
        device_id_type=MESH,
    )
    when(condition, copy.wait_send if phase.ending else copy.start)


def run_all(events):
    for event in events:
        event()


def await_block(buffer, sem):
    pltpu.make_async_copy(buffer, buffer, sem).wait()


class Scatter:
    PARTS = 17

    @staticmethod
    def scratch(order, rows, width, nf, ng):
        dma = pltpu.SemaphoreType.DMA
        plane, beyond_g = LINE * nf * ng, (ng - 1) * LINE * nf
        beyond_f = (nf - 1) * (LINE if order == "fz" else 1)
        line = LINE * (1 if order == "fz" else nf)
        counts = (plane, plane, beyond_g, beyond_f, line, line)
        buffers = [pltpu.VMEM((count, rows, width), BF16) for count in counts]
        sems = (plane, plane, plane, beyond_g, beyond_g, beyond_f, beyond_f, line, line, line, line)
        return buffers + [dma((count,)) for count in sems]

    def __init__(self, at, source, columns, order, scratch, phase):
        self.at, self.source, self.columns, self.order = at, source, columns, order
        self.phase = phase
        self.acc, self.from_pair, self.from_g, self.from_f = scratch[:4]
        self.from_below, self.from_above = scratch[4:6]
        self.load_sems, self.pair_send, self.pair_recv = scratch[6:9]
        self.g_send, self.g_recv, self.f_send, self.f_recv = scratch[9:13]
        self.up_send, self.up_recv, self.down_send, self.down_recv = scratch[13:]
        self.rows = self.acc.shape[1]

    def where_is(self, dz, df, dg):
        at = self.at
        return at.z + dz, (at.f + df) % at.nf, (at.g + dg) % at.ng

    def rows_of(self, z, f, g, core=None):
        start = pl.multiple_of(self.at.row_block(z, f, g, core) * self.rows, self.rows)
        return self.source.at[pl.ds(start, self.rows), self.columns]

    def begin(self, dz, df, dg):
        at = self.at
        z, f, g = self.where_is(dz, df, dg)
        place, other = at.index(z, f, g), 1 - at.core
        pf, pg = at.split(*at.split(f, g, at.core), other)
        there = at.index(z, pf, pg)

        def body():
            if self.phase.ending:
                await_block(self.from_pair.at[there], self.pair_send.at[there])
                return
            pltpu.make_async_copy(
                self.rows_of(z, f, g), self.acc.at[place], self.load_sems.at[place]
            ).start()
            pltpu.make_async_remote_copy(
                src_ref=self.rows_of(z, pf, pg, other),
                dst_ref=self.from_pair.at[there],
                send_sem=self.pair_send.at[there],
                recv_sem=self.pair_recv.at[there],
                device_id=at.partner(),
                device_id_type=MESH,
            ).start()

        when(present(at, dz), body)

    def join(self, condition, place, parts):
        if self.phase.ending:
            return

        def body():
            ready = [(buffer, sem) for allowed, buffer, sem in parts if allowed is True]
            for buffer, sem in ready:
                await_block(buffer, sem)
            if ready:
                add_blocks(self.acc.at[place], [buffer for buffer, _ in ready])
            for allowed, buffer, sem in parts:
                if allowed is not True:

                    def more(buffer=buffer, sem=sem):
                        await_block(buffer, sem)
                        add_blocks(self.acc.at[place], [buffer])

                    pl.when(allowed)(more)

        when(condition, body)

    def over_pair(self, dz, df, dg):
        at = self.at
        z, f, g = self.where_is(dz, df, dg)
        condition = present(at, dz)
        place = at.index(z, f, g)
        if not self.phase.ending:
            when(
                condition,
                functools.partial(await_block, self.acc.at[place], self.load_sems.at[place]),
            )
        self.join(condition, place, [(True, self.from_pair.at[place], self.pair_recv.at[place])])
        if dg:
            slot = (dg - 1) * LINE * at.nf + z * at.nf + f
            start_copy(
                self.phase,
                condition,
                self.acc.at[place],
                self.from_g.at[slot],
                self.g_send.at[slot],
                self.g_recv.at[slot],
                at.device(at.z, at.f, g),
            )

    def g_parts(self, z, f):
        slots = [(step - 1) * LINE * self.at.nf + z * self.at.nf + f for step in range(1, self.at.ng)]
        return [(True, self.from_g.at[slot], self.g_recv.at[slot]) for slot in slots]

    def f_slot(self, z, step):
        return (step - 1) * LINE + z if self.order == "fz" else step - 1

    def f_parts(self, z):
        slots = [self.f_slot(z, step) for step in range(1, self.at.nf)]
        return [(True, self.from_f.at[slot], self.f_recv.at[slot]) for slot in slots]

    def line_slot(self, z, f):
        return z if self.order == "fz" else z * self.at.nf + f

    def line_parts(self, dz, z, f):
        slot, parts = self.line_slot(z, f), []
        if 0 <= dz < LINE - 1:
            parts.append((self.at.z > 0, self.from_below.at[slot], self.up_recv.at[slot]))
        if 1 - LINE < dz <= 0:
            parts.append((self.at.z < LINE - 1, self.from_above.at[slot], self.down_recv.at[slot]))
        return parts

    def send_f(self, condition, df, z, f, place):
        slot = self.f_slot(z, df)
        start_copy(
            self.phase,
            condition,
            self.acc.at[place],
            self.from_f.at[slot],
            self.f_send.at[slot],
            self.f_recv.at[slot],
            self.at.device(self.at.z, f, self.at.g),
        )

    def send_line(self, condition, dz, z, f, place):
        slot = self.line_slot(z, f)
        rising = dz > 0
        start_copy(
            self.phase,
            condition,
            self.acc.at[place],
            (self.from_below if rising else self.from_above).at[slot],
            (self.up_send if rising else self.down_send).at[slot],
            (self.up_recv if rising else self.down_recv).at[slot],
            self.at.device(self.at.z + (1 if rising else -1), self.at.f, self.at.g),
        )

    def second(self, dz, df):
        z, f, _ = self.where_is(dz, df, 0)
        condition = present(self.at, dz)
        place = self.at.index(z, f, self.at.g)
        parts = self.g_parts(z, f)
        if self.order == "zf":
            parts = parts + self.line_parts(dz, z, f)
        self.join(condition, place, parts)
        if self.order == "zf" and dz:
            self.send_line(condition, dz, z, f, place)
        elif df:
            self.send_f(condition, df, z, f, place)

    def third(self, dz):
        z, f = self.at.z + dz, self.at.f
        condition = present(self.at, dz)
        place = self.at.index(z, f, self.at.g)
        parts = self.f_parts(z)
        if self.order == "fz":
            parts = parts + self.line_parts(dz, z, f)
        self.join(condition, place, parts)
        if dz:
            self.send_line(condition, dz, z, f, place)

    def stages(self):
        order = line_targets(self.at)
        part = functools.partial
        begins = [part(self.begin, *item) for item in order]
        pairs = [part(self.over_pair, *item) for item in order]
        if self.order == "fz":
            seconds = [part(self.second, *item[:2]) for item in order if item[2] == 0]
            thirds = [part(self.third, dz) for dz in (-3, 3, -2, 2, -1, 1, 0)]
        else:
            dfs = list(range(1, self.at.nf)) + [0]
            seconds = [part(self.second, dz, df) for dz in (-3, 3, -2, 2, -1, 1, 0) for df in dfs]
            thirds = [part(self.third, 0)]
        return begins, pairs, seconds, thirds

    def store(self, target, start):
        place = self.at.index(self.at.z, self.at.f, self.at.g)
        target[:, pl.ds(start, self.acc.shape[2])] = self.acc[place].astype(F32)


def mixed(first, second):
    marked = []
    for kind, steps in enumerate((first, second)):
        marked += [((i + 0.5) / len(steps), kind, step) for i, step in enumerate(steps)]
    return [step for _, _, step in sorted(marked, key=lambda item: item[:2])]


def pipelined(scatters):
    begins, first, mids, lasts = [], [], [], []
    for scatter in scatters:
        starts, pairs, seconds, thirds = scatter.stages()
        begins += starts
        first += [step for step in pairs if step.args[2]]
        mid = []
        for second in seconds:
            mid += [step for step in pairs if step.args == (*second.args, 0)] + [second]
        mids.append(mid)
        lasts.append(thirds)
    events = list(first)
    for slot in range(len(scatters) + 1):
        some = lasts[slot - 1] if slot else []
        if slot < len(scatters):
            some = mixed(some, mids[slot]) if some else mids[slot]
        events += some
    return begins, events, len(first)


def lagged(events, lag, phase):
    def close(event):
        phase.ending = True
        event()
        phase.ending = False

    def step(number):
        events[number]()
        if number >= lag:
            close(events[number - lag])

    def rest():
        for event in events[-lag:]:
            close(event)

    return [functools.partial(step, number) for number in range(len(events))], rest


def split_scratch(refs, count):
    size = Scatter.PARTS
    return [refs[i * size : (i + 1) * size] for i in range(count)], refs[count * size :]


def scatter_sections(at, sources, spans, scratches, phase):
    scatters, places = [], []
    for number, parts in enumerate(spans):
        start = 0
        for size, order in parts:
            scratch = scratches[len(scatters)]
            scatters.append(Scatter(at, sources[number], pl.ds(start, size), order, scratch, phase))
            places.append((number, start))
            start += size
    return scatters, places


def scatter_kernel(sizes, spans, *refs):
    at = Place(*sizes)
    count, sections = len(spans), sum(len(parts) for parts in spans)
    sources, refs = refs[:count], refs[count:]
    input_ref, vector_ref, grad_ref, total_ref = refs[:4]
    owned, refs = refs[4 : 4 + count], refs[4 + count :]
    scratches, refs = split_scratch(refs, sections)
    sq_g, sq_f, sq_z, sq_c, trade_send, trade_recv, sq_send, sq_recv = refs
    slots = grad_ref.shape[0]
    peers, number = plane_peers(at)
    more, extra = slot_peers(at, slots)
    meet(peers + more, number + extra)
    phase = Phase()
    send = functools.partial(start_copy, phase)
    scatters, places = scatter_sections(at, sources, spans, scratches, phase)
    begins, events, _ = pipelined(scatters)
    steps, rest = lagged(events, 24, phase)
    other = 1 - at.core

    def vectors_g():
        for step in range(1, at.ng):
            device = at.device(at.z, at.f, (at.g + step) % at.ng)
            send(True, sq_g.at[at.g], sq_g.at[at.g], sq_send.at[0, step], sq_recv.at[0, at.g], device)

    def vectors_f():
        for step in range(1, at.nf):
            device = at.device(at.z, (at.f + step) % at.nf, at.g)
            send(True, sq_f.at[at.f], sq_f.at[at.f], sq_send.at[1, step], sq_recv.at[1, at.f], device)

    def line_send(condition, held, kind):
        device = at.device(at.z - 1 if kind else at.z + 1, at.f, at.g)
        send(condition, sq_z.at[held], sq_z.at[held], sq_send.at[2 + kind, held], sq_recv.at[2, held], device)

    def vectors_line(distance):
        for kind, held in enumerate((at.z - distance, at.z + distance)):
            there = held < LINE if kind else held >= 0
            onward = at.z > 0 if kind else at.z < LINE - 1
            if distance and not phase.ending:
                when(
                    there,
                    functools.partial(await_block, sq_z.at[held], sq_recv.at[2, held]),
                )
            line_send(both(there, onward), held, kind)

    def vectors_pair():
        send(
            True,
            sq_c.at[at.core],
            sq_c.at[at.core],
            sq_send.at[4, 0],
            sq_recv.at[3, at.core],
            at.partner(),
        )

    def sums():
        def g():
            for step in range(1, at.ng):
                peer = (at.g + step) % at.ng
                await_block(sq_g.at[peer], sq_recv.at[0, peer])
            total = sq_g[0]
            for number in range(1, at.ng):
                total = total + sq_g[number]
            sq_f[at.f] = total
            vectors_f()

        def f():
            for step in range(1, at.nf):
                peer = (at.f + step) % at.nf
                await_block(sq_f.at[peer], sq_recv.at[1, peer])
            total = sq_f[0]
            for number in range(1, at.nf):
                total = total + sq_f[number]
            sq_z[at.z] = total
            vectors_line(0)

        def pair():
            total = sq_z[0]
            for number in range(1, LINE):
                total = total + sq_z[number]
            sq_c[at.core] = total
            vectors_pair()

        return [g, f] + [functools.partial(vectors_line, d) for d in range(1, LINE)] + [pair]

    sq_g[at.g] = vector_ref[...]
    run_all(begins)
    vectors_g()
    trade_out(at, input_ref, grad_ref, trade_send, trade_recv, phase)
    run_all(mixed(steps, sums()))
    for scatter, (number, start) in zip(scatters, places):
        scatter.store(owned[number], start)
    await_block(sq_c.at[other], sq_recv.at[3, other])
    total_ref[...] = sq_c[0] + sq_c[1]

    rest()
    phase.ending = True
    run_all(begins)
    trade_out(at, input_ref, grad_ref, trade_send, trade_recv, phase)
    vectors_g()
    vectors_f()
    for distance in range(LINE):
        vectors_line(distance)
    vectors_pair()


def scatter_last(sources, spans, input_grad, vectors, slots, seq_size, fsdp_size):
    rows = sources[0].shape[0] // (seq_size * fsdp_size)
    own_rows, model = input_grad.shape
    positions = own_rows // slots
    nf, ng = seq_size // (2 * LINE), fsdp_size
    dma = pltpu.SemaphoreType.DMA
    widest = max(nf, ng, LINE)
    vmem = pl.BlockSpec(memory_space=pltpu.VMEM)
    scratch = []
    for parts in spans:
        for size, order in parts:
            scratch += Scatter.scratch(order, rows, size, nf, ng)
    return pl.pallas_call(
        functools.partial(scatter_kernel, (seq_size, fsdp_size), spans),
        out_shape=tuple(
            [
                jax.ShapeDtypeStruct((slots, positions, model), BF16),
                jax.ShapeDtypeStruct(vectors.shape, F32),
            ]
            + [jax.ShapeDtypeStruct((rows, source.shape[1]), F32) for source in sources]
        ),
        in_specs=[pl.BlockSpec(memory_space=pl.ANY)] * len(sources) + [vmem] * 2,
        out_specs=[vmem] * (2 + len(sources)),
        scratch_shapes=scratch
        + [pltpu.VMEM((size, *vectors.shape), F32) for size in (ng, nf, LINE, 2)]
        + [dma((slots,)), dma((slots,)), dma((5, widest)), dma((4, widest))],
        compiler_params=pltpu.CompilerParams(
            collective_id=3, has_side_effects=True, vmem_limit_bytes=63_000_000
        ),
        name="scatter_last",
    )(*sources, input_grad, vectors)


def first_half(shape):
    lane = lax.broadcasted_iota(jnp.int32, shape, 1)
    return lane % 64 < 32


def turn(values, cosine, sine):
    half = first_half(values.shape)
    away = jnp.where(half, -pltpu.roll(values, 96, 1), pltpu.roll(values, 32, 1))
    return values * cosine + away * sine


def turn_back(grads, cosine, sine):
    half = first_half(grads.shape)
    moved = grads * sine
    away = jnp.where(half, pltpu.roll(moved, 96, 1), -pltpu.roll(moved, 32, 1))
    return grads * cosine + away


def normalize(values):
    average = jnp.mean(values, axis=-1, keepdims=True)
    centered = values - average
    variance = jnp.mean(centered * centered, axis=-1, keepdims=True)
    inverse = lax.rsqrt(variance + EPS)
    return centered * inverse, inverse


def norm_back(grad_normed, normed, inverse, gain_values):
    scaled = grad_normed * gain_values
    first_mean = jnp.mean(scaled, axis=-1, keepdims=True)
    second_mean = jnp.mean(scaled * normed, axis=-1, keepdims=True)
    return inverse * (scaled - first_mean - normed * second_mean)


def head_lanes(shape, head):
    return lax.broadcasted_iota(jnp.int32, shape, 1) // 64 == head


def scores_of(keys, queries, bias):
    scores = lax.dot_general(keys, queries, (((1,), (1,)), ((), ())), preferred_element_type=F32)
    return scores + bias


def key_bias(length, shape):
    return jnp.where(lax.broadcasted_iota(jnp.int32, shape, 0) < length, 0.0, -jnp.inf)


def attend(length, queries, keys, values):
    queries = queries * 0.125
    bias = key_bias(length, (keys.shape[0], 1))
    zero = jnp.zeros((), BF16)
    total, logs = None, []
    for head in range(2):
        only = head_lanes(queries.shape, head)
        scores = scores_of(keys, jnp.where(only, queries, zero), bias)
        largest = jnp.max(scores, axis=0, keepdims=True)
        weights = jnp.exp(scores - largest)
        summed = jnp.sum(weights, axis=0, keepdims=True)
        logs.append(largest + jnp.log(summed))
        held = jnp.where(head_lanes(values.shape, head), values, zero)
        part = lax.dot_general(
            held, weights.astype(BF16), (((0,), (0,)), ((), ())), preferred_element_type=F32
        )
        part = part / summed
        total = part if total is None else total + part
    return total.T.astype(BF16), logs


FRONT_TILE = 512


def front_kernel(sizes, group, spans, *refs):
    at = Place(*sizes)
    count = len(spans)
    length_ref, x_ref, gains_ref, cos_ref, sin_ref, w_ref, dy_ref = refs[:7]
    sources, refs = refs[7 : 7 + count], refs[7 + count :]
    act_ref, gain_ref, q_ref, shared_out, o_ref, log_ref, dy_rows_ref = refs[:7]
    wholes, refs = refs[7 : 7 + count], refs[7 + count :]
    sems, (trade_send, trade_recv, share_send, share_recv, shared_ref, out_sem) = refs[:3], refs[3:]
    step = pl.program_id(0)
    rows, model = q_ref.shape
    slots = dy_ref.shape[0]
    tile = o_ref.shape[0]
    tiles = rows // tile
    projecting = 3 * model // FRONT_TILE
    steps = projecting + model // LANES * tiles
    kept = 2 * model // FRONT_TILE
    phase = Phase()
    sections = []
    for number, parts in enumerate(spans):
        start = 0
        for size, order in parts:
            sections.append((sources[number], wholes[number], pl.ds(start, size), order))
            start += size
    gather = Gather(at, sections, sems, phase)
    base, part = (at.seq // group) * group, at.seq % group
    members = [base + (part + other) % group for other in range(1, group)]
    own_rows = pl.ds(pl.multiple_of(part * rows, rows), rows)

    @pl.when(step == 0)
    def _():
        peers, number = plane_peers(at)
        more, extra = slot_peers(at, slots)
        others = [(True, (member, at.y)) for member in members]
        meet(peers + more + others, number + extra + group - 1)

    @pl.when(step == 0)
    def _():
        gather.begin()
        trade_in(at, dy_ref, dy_rows_ref, trade_send, trade_recv, phase)

    @pl.when(step == 0)
    def _():
        normed, _ = normalize(x_ref[...].astype(F32))
        turned = gains_ref[...].astype(F32).T
        gain_ref[...] = turned[:8]
        act_ref[...] = (normed * turned[:1]).astype(BF16)

    def share(number):
        place = shared_ref.at[own_rows, pl.ds(number * FRONT_TILE, FRONT_TILE)]
        for other, member in enumerate(members):
            start_copy(
                phase,
                True,
                place,
                place,
                share_send.at[number, other],
                share_recv.at[number, part],
                (member, at.y),
            )

    def receive():
        for number in range(kept):
            for other in range(1, group):
                source = (part + other) % group
                place = shared_ref.at[
                    pl.ds(pl.multiple_of(source * rows, rows), rows),
                    pl.ds(number * FRONT_TILE, FRONT_TILE),
                ]
                await_block(place, share_recv.at[number, source])
        pltpu.make_async_copy(shared_ref, shared_out, out_sem).start()

    for number in range(kept):
        pl.when(step == number + 1)(functools.partial(share, number))
    pl.when(step == projecting)(receive)

    @pl.when(step < projecting)
    def _():
        mixed = jnp.dot(act_ref[...], w_ref[...], preferred_element_type=F32)

        def turned():
            cosine, sine = cos_ref[...], sin_ref[...]
            pieces = [
                turn(mixed[:, start : start + LANES], cosine, sine).astype(BF16)
                for start in range(0, FRONT_TILE, LANES)
            ]
            return jnp.concatenate(pieces, axis=1)

        @pl.when(step < kept // 2)
        def _():
            columns = pl.ds(pl.multiple_of(step * FRONT_TILE, FRONT_TILE), FRONT_TILE)
            shared_ref[own_rows, columns] = turned()

        @pl.when(both(step >= kept // 2, step < kept))
        def _():
            columns = pl.ds(pl.multiple_of(step * FRONT_TILE, FRONT_TILE), FRONT_TILE)
            shared_ref[own_rows, columns] = mixed.astype(BF16)

        @pl.when(step >= kept)
        def _():
            columns = pl.ds(pl.multiple_of((step - kept) * FRONT_TILE, FRONT_TILE), FRONT_TILE)
            q_ref[:, columns] = turned()

    @pl.when(step >= projecting)
    def _():
        pair, piece = (step - projecting) // tiles, (step - projecting) % tiles
        start = pl.multiple_of(pair * LANES, LANES)
        out, logs = attend(
            length_ref[0],
            q_ref[pl.ds(pl.multiple_of(piece * tile, tile), tile), pl.ds(start, LANES)],
            shared_ref[:, pl.ds(start, LANES)],
            shared_ref[:, pl.ds(pl.multiple_of(model + start, LANES), LANES)],
        )
        o_ref[...] = out
        for head in range(2):
            log_ref[0, head : head + 1, :] = logs[head]

    events, rest = gather.steps(24)
    pace = FRONT_PACE
    for number in range(steps - 1):
        group_events = events[number * pace : (number + 1) * pace]
        if group_events:
            pl.when(step == number)(functools.partial(run_all, group_events))

    @pl.when(step == steps - 1)
    def _():
        run_all(events[(steps - 1) * pace :])
        rest()
        phase.ending = True
        trade_in(at, dy_ref, dy_rows_ref, trade_send, trade_recv, phase)
        for number in range(kept):
            share(number)
        pltpu.make_async_copy(shared_ref, shared_out, out_sem).wait()
        phase.ending = False


FRONT_PACE = 4


def front(length, x_rows, cosine, sine, weight, dy, sources, spans, group, tile, seq_size, fsdp_size):
    rows, model = x_rows.shape
    slots, positions, _ = dy.shape
    pairs, tiles = model // LANES, rows // tile
    projecting, kept = 3 * model // FRONT_TILE, 2 * model // FRONT_TILE
    nf, ng = seq_size // (2 * LINE), fsdp_size
    devices = seq_size * fsdp_size
    count = sum(len(parts) for parts in spans)
    dma = pltpu.SemaphoreType.DMA
    vmem, anywhere = pl.BlockSpec(memory_space=pltpu.VMEM), pl.BlockSpec(memory_space=pl.ANY)

    def pair_of(i):
        return jnp.maximum(i - projecting, 0) // tiles

    def tile_of(i):
        return jnp.maximum(i - projecting, 0) % tiles

    return pl.pallas_call(
        functools.partial(front_kernel, (seq_size, fsdp_size), group, spans),
        grid=(projecting + pairs * tiles,),
        out_shape=tuple(
            [
                jax.ShapeDtypeStruct((rows, model), BF16),
                jax.ShapeDtypeStruct((8, model), F32),
                jax.ShapeDtypeStruct((rows, model), BF16),
                jax.ShapeDtypeStruct((rows * group, 2 * model), BF16),
                jax.ShapeDtypeStruct((rows, model), BF16),
                jax.ShapeDtypeStruct((pairs, 8, rows), F32),
                jax.ShapeDtypeStruct((slots * positions, model), BF16),
            ]
            + [
                jax.ShapeDtypeStruct((source.shape[0] * devices, source.shape[1]), BF16)
                for source in sources
            ]
        ),
        in_specs=[pl.BlockSpec(memory_space=pltpu.SMEM), vmem]
        + [pl.BlockSpec((model, LANES), lambda i: (0, 3 * model // LANES)), vmem, vmem]
        + [
            pl.BlockSpec(
                (model, FRONT_TILE),
                lambda i: (0, (jnp.minimum(i, projecting - 1) + projecting - kept) % projecting),
            )
        ]
        + [vmem] * (1 + len(sources)),
        out_specs=[
            vmem,
            vmem,
            vmem,
            anywhere,
            pl.BlockSpec((tile, LANES), lambda i: (tile_of(i), pair_of(i))),
            pl.BlockSpec((1, 8, tile), lambda i: (pair_of(i), 0, tile_of(i))),
        ]
        + [anywhere] * (1 + len(sources)),
        scratch_shapes=Gather.scratch(count, nf, ng)
        + [dma((slots,)), dma((slots,)), dma((kept, group)), dma((kept, group))]
        + [pltpu.VMEM((rows * group, 2 * model), BF16), dma],
        compiler_params=pltpu.CompilerParams(
            collective_id=1, has_side_effects=True, vmem_limit_bytes=63_000_000
        ),
        name="front",
    )(length, x_rows, weight, cosine, sine, weight, dy, *sources)


def attend_back(length, queries, keys, values, grads, heads_out, logs):
    queries = queries * 0.125
    bias = key_bias(length, (keys.shape[0], 1))
    zero = jnp.zeros((), BF16)
    product = (grads.astype(F32) * heads_out.astype(F32)).T
    dq = dk = dv = None
    for head in range(2):
        only = head_lanes(queries.shape, head)
        query = jnp.where(only, queries, zero)
        grad = jnp.where(only, grads, zero)
        key = jnp.where(head_lanes(keys.shape, head), keys, zero)
        delta = jnp.sum(product[64 * head : 64 * head + 64], axis=0, keepdims=True)
        scores = scores_of(keys, query, bias)
        probs = jnp.exp(scores - logs[head : head + 1])
        grad_probs = lax.dot_general(
            values, grad, (((1,), (1,)), ((), ())), preferred_element_type=F32
        )
        grad_scores = (probs * (grad_probs - delta)).astype(BF16)
        value_part = jnp.dot(probs.astype(BF16), grad, preferred_element_type=F32)
        key_part = jnp.dot(grad_scores, query, preferred_element_type=F32)
        query_part = lax.dot_general(
            key, grad_scores, (((0,), (0,)), ((), ())), preferred_element_type=F32
        )
        dq = query_part if dq is None else dq + query_part
        dk = key_part if dk is None else dk + key_part
        dv = value_part if dv is None else dv + value_part
    return dq.T * 0.125, dk, dv


def back_kernel(sizes, group, spans, *refs):
    at = Place(*sizes)
    sections = sum(len(parts) for parts in spans)
    count = len(spans)
    length_ref, q_ref, k_ref, v_ref, g_ref, o_ref, log_ref, cos_ref, sin_ref, result_ref = refs[:10]
    sources, refs = refs[10 : 10 + count], refs[10 + count :]
    mixed_ref, out_ref = refs[:2]
    owned, refs = refs[2 : 2 + count], refs[2 + count :]
    scratches, refs = split_scratch(refs, sections)
    dk_acc, dv_acc, parts_ref, arrived, sum_send, sum_recv, trade_send, trade_recv = refs
    step = pl.program_id(0)
    tile = q_ref.shape[0]
    rows, model = result_ref.shape
    tiles, pairs = rows // tile, model // LANES
    steps = pairs * tiles + 1
    slots = out_ref.shape[0]
    phase = Phase()
    scatters, places = scatter_sections(at, sources, spans, scratches, phase)
    begins, events, ahead = pipelined(scatters)
    events, rest = lagged(events, 40, phase)
    base, part = (at.seq // group) * group, at.seq % group
    members = [base + (part + other) % group for other in range(1, group)]

    def columns_of(pair):
        return pl.ds(pl.multiple_of(pair * LANES, LANES), LANES)

    def share(pair):
        for kind in range(2):
            for other, member in enumerate(members):
                owner = (part + other + 1) % group
                start_copy(
                    phase,
                    True,
                    parts_ref.at[kind, pl.ds(pl.multiple_of(owner * rows, rows), rows), columns_of(pair)],
                    arrived.at[kind, other, :, columns_of(pair)],
                    sum_send.at[kind, other, pair],
                    sum_recv.at[kind, other, pair],
                    (member, at.y),
                )

    @pl.when(step == 0)
    def _():
        peers, number = plane_peers(at)
        more, extra = slot_peers(at, slots)
        others = [(True, (member, at.y)) for member in members]
        meet(peers + more + others, number + extra + group - 1)
        run_all(begins)
        trade_out(at, result_ref, out_ref, trade_send, trade_recv, phase)
        run_all(events[:ahead])

    for number in range(1, steps):
        some = events[ahead + (number - 1) * BACK_PACE : ahead + number * BACK_PACE]
        if some:
            pl.when(step == number)(functools.partial(run_all, some))

    pl.when(both(step > 0, step % tiles == 0))(lambda: share(step // tiles - 1))

    @pl.when(step < steps - 1)
    def _():
        pair, piece = step // tiles, step % tiles
        own = pl.ds(pl.multiple_of(piece * tile, tile), tile)
        dq, dk, dv = attend_back(
            length_ref[0], q_ref[...], k_ref[...], v_ref[...], g_ref[...], o_ref[...], log_ref[0]
        )
        mixed_ref[own, columns_of(pair)] = turn_back(dq, cos_ref[own], sin_ref[own]).astype(BF16)
        if tiles == 1:
            parts_ref[0, :, columns_of(pair)] = dk.astype(BF16)
            parts_ref[1, :, columns_of(pair)] = dv.astype(BF16)
            return

        @pl.when(piece == 0)
        def _():
            dk_acc[...] = dk
            dv_acc[...] = dv

        @pl.when(piece > 0)
        def _():
            dk_acc[...] += dk
            dv_acc[...] += dv

        @pl.when(piece == tiles - 1)
        def _():
            parts_ref[0, :, columns_of(pair)] = dk_acc[...].astype(BF16)
            parts_ref[1, :, columns_of(pair)] = dv_acc[...].astype(BF16)

    def add_parts():
        own = pl.ds(pl.multiple_of(part * rows, rows), rows)

        def body(pair, carry):
            for kind in range(2):
                total = parts_ref[kind, own, columns_of(pair)].astype(F32)
                for other in range(group - 1):
                    piece = arrived.at[kind, other, :, columns_of(pair)]
                    await_block(piece, sum_recv.at[kind, other, pair])
                    total = total + piece[...].astype(F32)
                if kind == 0:
                    total = turn_back(total, cos_ref[...], sin_ref[...])
                start = pl.multiple_of((kind + 1) * model + pair * LANES, LANES)
                mixed_ref[:, pl.ds(start, LANES)] = total.astype(BF16)
            return carry

        lax.fori_loop(0, pairs, body, 0)

    @pl.when(step == steps - 1)
    def _():
        add_parts()
        run_all(events[ahead + (steps - 1) * BACK_PACE :])
        for scatter, (number, start) in zip(scatters, places):
            scatter.store(owned[number], start)
        rest()
        phase.ending = True
        run_all(begins)
        trade_out(at, result_ref, out_ref, trade_send, trade_recv, phase)

        def body(pair, carry):
            share(pair)
            return carry

        lax.fori_loop(0, pairs, body, 0)
        phase.ending = False


BACK_PACE = 3


def back(length, queries, shared, grads, heads_out, logs, cosine, sine, result, sources, spans, tile, slots, seq_size, fsdp_size):
    rows, keys, model = queries.shape[0], shared.shape[0], queries.shape[1]
    group, positions = keys // rows, rows // slots
    pairs, tiles = model // LANES, rows // tile
    nf, ng = seq_size // (2 * LINE), fsdp_size
    devices = seq_size * fsdp_size
    shard = sources[0].shape[0] // devices
    vmem, anywhere = pl.BlockSpec(memory_space=pltpu.VMEM), pl.BlockSpec(memory_space=pl.ANY)
    dma = pltpu.SemaphoreType.DMA

    def pair_of(i):
        return jnp.minimum(i, pairs * tiles - 1) // tiles

    def tile_of(i):
        return jnp.minimum(i, pairs * tiles - 1) % tiles

    by_row = pl.BlockSpec((tile, LANES), lambda i: (tile_of(i), pair_of(i)))
    scratch = []
    for parts in spans:
        for size, order in parts:
            scratch += Scatter.scratch(order, shard, size, nf, ng)
    return pl.pallas_call(
        functools.partial(back_kernel, (seq_size, fsdp_size), group, spans),
        grid=(pairs * tiles + 1,),
        out_shape=tuple(
            [
                jax.ShapeDtypeStruct((rows, 3 * model), BF16),
                jax.ShapeDtypeStruct((slots, positions, model), BF16),
            ]
            + [jax.ShapeDtypeStruct((shard, source.shape[1]), F32) for source in sources]
        ),
        in_specs=[
            pl.BlockSpec(memory_space=pltpu.SMEM),
            by_row,
            pl.BlockSpec((keys, LANES), lambda i: (0, pair_of(i))),
            pl.BlockSpec((keys, LANES), lambda i: (0, pairs + pair_of(i))),
            by_row,
            by_row,
            pl.BlockSpec((1, 8, tile), lambda i: (pair_of(i), 0, tile_of(i))),
            vmem,
            vmem,
            vmem,
        ]
        + [anywhere] * len(sources),
        out_specs=[vmem, anywhere] + [vmem] * len(sources),
        scratch_shapes=scratch
        + [
            pltpu.VMEM((keys, LANES), F32),
            pltpu.VMEM((keys, LANES), F32),
            pltpu.VMEM((2, keys, model), BF16),
            pltpu.VMEM((2, group - 1, rows, model), BF16),
            dma((2, group - 1, pairs)),
            dma((2, group - 1, pairs)),
            dma((slots,)),
            dma((slots,)),
        ],
        compiler_params=pltpu.CompilerParams(
            collective_id=2, has_side_effects=True, vmem_limit_bytes=67_000_000
        ),
        name="back",
    )(length, queries, shared, shared, grads, heads_out, logs, cosine, sine, result, *sources)


def rotary_tables(places, head_size):
    halfway = head_size // 2
    ladder = jnp.arange(halfway, dtype=F32) * (2.0 / head_size)
    inverse = 1.0 / THETA**ladder
    angles = places.astype(F32)[:, None] * inverse[None, :]
    angles = jnp.concatenate([angles] * 4, axis=-1)
    return jnp.cos(angles), jnp.sin(angles)


def mm(left, right):
    return jnp.dot(left, right, preferred_element_type=F32)


def mm_right_t(left, right):
    return lax.dot_general(left, right, (((1,), (1,)), ((), ())), preferred_element_type=F32)


def mm_left_t(left, right):
    return lax.dot_general(left, right, (((0,), (0,)), ((), ())), preferred_element_type=F32)


SQRT_HALF = 0.7071067811865476
INV_SQRT_TAU = 0.3989422804014327


def gelu_and_slope(values):
    share = 0.5 + 0.5 * lax.erf(values * SQRT_HALF)
    density = INV_SQRT_TAU * jnp.exp(-0.5 * values * values)
    return values * share, share + values * density


def mlp_kernel(
    bounds_ref,
    x_ref,
    heads_ref,
    dy_ref,
    w_attn_ref,
    gain_ref,
    w_in_ref,
    w_gate_ref,
    w_down_ref,
    result_ref,
    vectors_ref,
    grad_middle_ref,
    grad_heads_ref,
    attn_part_ref,
    in_part_ref,
    gate_part_ref,
    down_part_ref,
    act,
    act_turned,
    grad_branch,
    grad_turned,
    middle,
    branch,
    grad_act,
):
    step = pl.program_id(0)
    rows = x_ref.shape[0]
    gain = gain_ref[...]
    position = bounds_ref[1] + lax.broadcasted_iota(jnp.int32, (rows, 1), 0)
    valid = jnp.where(position < bounds_ref[0], 1.0, 0.0).astype(F32)

    def squares(row, values):
        vectors_ref[row : row + 1, :] = jnp.sum(valid * values * values, axis=0, keepdims=True)

    @pl.when(step == 0)
    def _():
        x_wide = x_ref[...].astype(F32)
        attn = mm(heads_ref[...], w_attn_ref[...])
        total = x_wide + attn
        middle[...] = total
        vectors_ref[...] = jnp.zeros_like(vectors_ref)
        squares(0, x_wide)
        squares(1, total)
        squares(3, attn)
        scaled = normalize(total)[0] * gain
        act[...] = scaled.astype(BF16)
        act_turned[...] = scaled.T.astype(BF16)
        grad_y = dy_ref[...].astype(F32) * valid
        grad_branch[...] = grad_y.astype(BF16)
        grad_turned[...] = grad_y.T.astype(BF16)
        branch[...] = jnp.zeros_like(branch)
        grad_act[...] = jnp.zeros_like(grad_act)

    input_half = mm(act[...], w_in_ref[...])
    gate_half = mm(act[...], w_gate_ref[...])
    grad_product = mm(grad_branch[...], w_down_ref[...])
    active, slope = gelu_and_slope(input_half)
    product = (active * gate_half).astype(BF16)
    grad_input = (grad_product * gate_half * slope).astype(BF16)
    grad_gate = (grad_product * active).astype(BF16)
    branch[...] += mm_right_t(product, w_down_ref[...])
    grad_act[...] += mm_right_t(grad_input, w_in_ref[...]) + mm_right_t(grad_gate, w_gate_ref[...])
    in_part_ref[...] = mm(act_turned[...], grad_input).astype(BF16)
    gate_part_ref[...] = mm(act_turned[...], grad_gate).astype(BF16)
    down_part_ref[...] = mm(grad_turned[...], product).astype(BF16)

    @pl.when(step == pl.num_programs(0) - 1)
    def _():
        result = (middle[...] + branch[...]) * valid
        squares(2, result)
        squares(4, branch[...])
        result_ref[...] = result.astype(BF16)
        normed, inverse = normalize(middle[...])
        vectors_ref[6:7, :] = jnp.sum(grad_act[...] * normed, axis=0, keepdims=True)
        grad_y = dy_ref[...].astype(F32) * valid
        grad_middle = grad_y + norm_back(grad_act[...], normed, inverse, gain)
        grad_middle_ref[...] = grad_middle
        grad_attn = grad_middle.astype(BF16)
        grad_heads_ref[...] = mm_right_t(grad_attn, w_attn_ref[...]).astype(BF16)
        attn_part_ref[...] = mm_left_t(heads_ref[...], grad_attn).astype(BF16)


MLP_TILE = 896


def mlp(bounds, x_rows, heads_out, dy_rows, w_attn, gain, w_input, w_down):
    rows, model = x_rows.shape
    wide = w_down.shape[1]
    tile = MLP_TILE if wide % MLP_TILE == 0 else LANES
    steps = wide // tile
    vmem = pl.BlockSpec(memory_space=pltpu.VMEM)
    by_column = pl.BlockSpec((model, tile), lambda i: (0, i))
    part = jax.ShapeDtypeStruct((model, wide), BF16)
    return pl.pallas_call(
        mlp_kernel,
        grid=(steps,),
        out_shape=(
            jax.ShapeDtypeStruct((rows, model), BF16),
            jax.ShapeDtypeStruct((8, model), F32),
            jax.ShapeDtypeStruct((rows, model), F32),
            jax.ShapeDtypeStruct((rows, model), BF16),
            jax.ShapeDtypeStruct((model, model), BF16),
            part,
            part,
            part,
        ),
        in_specs=[pl.BlockSpec(memory_space=pltpu.SMEM)]
        + [vmem] * 5
        + [by_column, pl.BlockSpec((model, tile), lambda i: (0, steps + i)), by_column],
        out_specs=[vmem] * 5 + [by_column] * 3,
        scratch_shapes=[
            pltpu.VMEM((rows, model), BF16),
            pltpu.VMEM((model, rows), BF16),
            pltpu.VMEM((rows, model), BF16),
            pltpu.VMEM((model, rows), BF16),
            pltpu.VMEM((rows, model), F32),
            pltpu.VMEM((rows, model), F32),
            pltpu.VMEM((rows, model), F32),
        ],
        compiler_params=pltpu.CompilerParams(vmem_limit_bytes=63_000_000),
        name="mlp",
    )(bounds, x_rows, heads_out, dy_rows, w_attn, gain, w_input, w_input, w_down)


def shards(
    hidden_in,
    out_grad,
    qkv_weight,
    attn_out_weight,
    in_weight,
    down_weight,
    attn_gain,
    mlp_gain,
    seq_lengths,
    slot_order,
):
    seq_size, fsdp_size = lax.axis_size("seq"), lax.axis_size("fsdp")
    seq_place, fsdp_place = lax.axis_index("seq"), lax.axis_index("fsdp")
    slots, positions, model = hidden_in.shape
    shard = qkv_weight.shape[0]
    ff = down_weight.shape[0]
    wide = up_to(ff, LANES)
    spare = wide - ff
    group = seq_size // slots
    rows = slots * positions
    head_size = model // HEADS

    lead = jnp.zeros((shard, spare), BF16)
    gains = jnp.concatenate(
        [attn_gain[:, None], mlp_gain[:, None], jnp.zeros((shard, LANES - 2), BF16)], axis=1
    )
    in_pack = jnp.concatenate([in_weight[:, :ff], lead, in_weight[:, ff:], lead], axis=1)
    down_pack = jnp.concatenate([down_weight.T, lead], axis=1)
    w_qkv, x_rows = gather_first(qkv_weight, gains, hidden_in, seq_size, fsdp_size)

    slot = fsdp_place * slots + seq_place // group
    order = jnp.sum(jnp.where(jnp.arange(slot_order.shape[0]) == slot, slot_order, 0))
    length = jnp.sum(jnp.where(jnp.arange(seq_lengths.shape[0]) == order, seq_lengths, 0))
    lengths = length.astype(jnp.int32)[None]
    places = (seq_place % group) * rows + jnp.arange(rows, dtype=jnp.int32)
    cosine, sine = rotary_tables(places, head_size)

    tile = 512 if rows % 512 == 0 and rows * group <= 1024 else 128
    act_one, gain_rows, queries, shared, heads_out, logs, dy_rows, w_attn, w_input, w_down = front(
        lengths,
        x_rows,
        cosine,
        sine,
        w_qkv,
        out_grad,
        (attn_out_weight, in_pack, down_pack),
        (((model, "fzg-"),), ((wide, "zfg"), (wide, "zfg")), ((wide, "fzg"),)),
        group,
        tile,
        seq_size,
        fsdp_size,
    )
    gain_attn, gain_mlp = gain_rows[0:1], gain_rows[1:2]

    bounds = jnp.stack([lengths[0], places[0]])
    result, vectors, grad_middle, grad_heads, attn_part, in_part, gate_part, down_part = mlp(
        bounds, x_rows, heads_out, dy_rows, w_attn, gain_mlp, w_input, w_down
    )

    second = "zf" if seq_size == 4 * LINE else "fz"
    early = [(attn_part, ((model, second),)), (down_part, ((wide, second),))]
    wide_parts = [(in_part, ((wide, "fz"),)), (gate_part, ((wide, "fz"),))]
    fits = rows * group <= 1024
    if fits:
        early, late = [early[1], *wide_parts, early[0]], []
    else:
        late = wide_parts
    grad_mixed, out_rows, *owned = back(
        lengths,
        queries,
        shared,
        grad_heads,
        heads_out,
        logs,
        cosine,
        sine,
        result,
        [part for part, _ in early],
        tuple(parts for _, parts in early),
        tile,
        slots,
        seq_size,
        fsdp_size,
    )
    qkv_part = mm_left_t(act_one, grad_mixed).astype(BF16)
    grad_act_one = mm_right_t(grad_mixed, w_qkv[:, : 3 * model])
    normed_one, inverse_one = normalize(x_rows.astype(F32))
    attn_gain_part = jnp.sum(grad_act_one * normed_one, axis=0)
    grad_x = grad_middle + norm_back(grad_act_one, normed_one, inverse_one, gain_attn)

    vectors = vectors.at[5].set(attn_gain_part)
    half = 3 * model // 2
    late.append((qkv_part, ((half, "fz"), (half, second))))
    grad_rows, totals, *more = scatter_last(
        [part for part, _ in late],
        tuple(parts for _, parts in late),
        grad_x.astype(BF16),
        vectors,
        slots,
        seq_size,
        fsdp_size,
    )
    own_qkv = more[-1]
    if fits:
        own_down, own_in, own_gate, own_attn = owned
    else:
        own_attn, own_down = owned
        own_in, own_gate = more[:2]
    tokens_valid = jnp.sum(seq_lengths).astype(F32)
    root_squares = jnp.sqrt(jnp.sum(totals[:5], axis=1) / (tokens_valid * model))
    own_gains = lax.dynamic_slice_in_dim(totals, (seq_place * fsdp_size + fsdp_place) * shard, shard, 1)
    return (
        out_rows,
        grad_rows,
        own_qkv,
        own_attn,
        jnp.concatenate([own_in[:, :ff], own_gate[:, :ff]], axis=1),
        own_down[:, :ff].T,
        own_gains[5],
        own_gains[6],
        root_squares,
    )


def solution(mesh):
    placed = (
        P("fsdp", "seq", None),
        P("fsdp", "seq", None),
        P(("seq", "fsdp"), None),
        P(("seq", "fsdp"), None),
        P(("seq", "fsdp"), None),
        P(None, ("seq", "fsdp")),
        P(("seq", "fsdp")),
        P(("seq", "fsdp")),
        P(),
        P(),
    )
    return jax.shard_map(
        shards,
        mesh=mesh,
        in_specs=placed,
        out_specs=(
            P("fsdp", "seq", None),
            P("fsdp", "seq", None),
            P(("seq", "fsdp"), None),
            P(("seq", "fsdp"), None),
            P(("seq", "fsdp"), None),
            P(None, ("seq", "fsdp")),
            P(("seq", "fsdp")),
            P(("seq", "fsdp")),
            P(),
        ),
        check_vma=False,
    )
```

```python
import functools

import jax
import jax.numpy as jnp
from jax import lax
from jax.experimental import pallas as pl
from jax.experimental.pallas import tpu as pltpu
from jax.sharding import PartitionSpec as P

HEADS = 16
LINE = 4
LANES = 128
EPS = 1e-05
THETA = 160000.0
F32 = jnp.float32
BF16 = jnp.bfloat16
MESH = pl.DeviceIdType.MESH


def up_to(size, unit):
    return -(-size // unit) * unit


class Place:
    def __init__(self, seq_size, fsdp_size, swap=True):
        self.seq_size, self.fsdp_size = seq_size, fsdp_size
        self.rest = seq_size // (2 * LINE)
        self.swap = swap and self.rest == fsdp_size
        self.nf, self.ng = self.rest, fsdp_size
        self.blocks = LINE * self.nf * self.ng
        self.seq = lax.axis_index("seq")
        self.y = lax.axis_index("fsdp")
        self.core = self.seq % 2
        self.r = (self.seq // 2) % self.rest
        self.z = self.seq // (2 * self.rest)
        self.f, self.g = self.split(self.r, self.y, self.core)

    def split(self, r, y, core):
        if not self.swap:
            return r, y
        return (1 - core) * r + core * y, (1 - core) * y + core * r

    def device(self, z, f, g, core=None):
        core = self.core if core is None else core
        r, y = self.split(f, g, core)
        return (z * self.rest + r) * 2 + core, y

    def row_block(self, z, f, g, core=None):
        seq, y = self.device(z, f, g, core)
        return seq * self.fsdp_size + y

    def index(self, z, f, g):
        return (z * self.nf + f) * self.ng + g

    def partner(self):
        return self.seq + 1 - 2 * self.core, self.y


def both(first, second):
    if first is True:
        return second
    if second is True:
        return first
    return jnp.logical_and(first, second)


def when(condition, body):
    if condition is True:
        body()
    else:
        pl.when(condition)(body)


def meet(peers, awaited):
    barrier = pltpu.get_barrier_semaphore()
    for condition, device in peers:
        when(
            condition,
            functools.partial(
                pl.semaphore_signal, barrier, inc=1, device_id=device, device_id_type=MESH
            ),
        )
    pl.semaphore_wait(barrier, awaited)


def plane_peers(at):
    below, above = at.z > 0, at.z < LINE - 1
    peers = [
        (below, at.device(at.z - 1, at.f, at.g)),
        (above, at.device(at.z + 1, at.f, at.g)),
        (True, at.partner()),
    ]
    for step in range(1, at.nf):
        peers.append((True, at.device(at.z, (at.f + step) % at.nf, at.g)))
    for step in range(1, at.ng):
        peers.append((True, at.device(at.z, at.f, (at.g + step) % at.ng)))
    count = 1 + (at.nf - 1) + (at.ng - 1)
    count = count + jnp.where(below, 1, 0) + jnp.where(above, 1, 0)
    return peers, count


def slot_peers(at, slots):
    group = at.seq_size // slots
    own_slot, own_part = at.seq // group, at.seq % group
    same = at.seq // slots == own_part
    peers = []
    for step in range(slots):
        wide = ((own_slot + step) % slots) * group + at.seq // slots
        narrow = own_part * slots + (at.seq + step) % slots
        condition = True if step else jnp.logical_not(same)
        peers.append((condition, (wide, at.y)))
        peers.append((condition, (narrow, at.y)))
    return peers, 2 * slots - 2 * jnp.where(same, 1, 0)


def steps_of(at):
    out = []
    for dz in (0, -1, 1, -2, 2, -3, 3):
        for df in range(at.nf):
            for dg in range(at.ng):
                out.append((abs(dz) + (df > 0) + (dg > 0), dz, df, dg))
    out.sort(key=lambda item: item[0])
    return out


def present(at, dz):
    if dz == 0:
        return True
    return at.z + dz >= 0 if dz < 0 else at.z + dz < LINE


class Gather:
    def __init__(self, at, sections, sems, phase):
        self.at, self.sections, self.phase = at, sections, phase
        plain = Place(at.seq_size, at.fsdp_size, swap=False)
        self.places = [plain if section[3][-1] == "-" else at for section in sections]
        self.send_sems, self.plane_sems, self.pair_sems = sems

    @staticmethod
    def scratch(count, nf, ng):
        dma = pltpu.SemaphoreType.DMA
        blocks, kinds = LINE * nf * ng, 3 + (nf - 1) + (ng - 1)
        return [dma((count, blocks, kinds)), dma((count, blocks)), dma((count, blocks + 1))]

    def own(self, number):
        source, _, columns, _ = self.sections[number]
        return source.at[:, columns]

    def block(self, number, z, f, g):
        source, whole, columns, _ = self.sections[number]
        rows = source.shape[0]
        start = pl.multiple_of(self.places[number].row_block(z, f, g) * rows, rows)
        return whole.at[pl.ds(start, rows), columns]

    def forward(self, number, condition, source, dz, df, dg):
        at, order = self.places[number], self.sections[number][3].strip("-")
        z, f, g = at.z + dz, (at.f + df) % at.nf, (at.g + dg) % at.ng
        place, target = at.index(z, f, g), self.block(number, z, f, g)
        moved = {"z": dz, "f": df, "g": dg}
        last = max([i for i, axis in enumerate(order) if moved[axis]], default=-1)

        def send(allowed, kind, device, pair=False):
            sem = (self.pair_sems if pair else self.plane_sems).at[number, place]
            start_copy(
                self.phase,
                both(condition, allowed),
                source,
                target,
                self.send_sems.at[number, place, kind],
                sem,
                device,
            )

        for i, axis in enumerate(order):
            if axis == "z" and i >= last:
                rising, sinking = dz <= 0, dz >= 0
                if rising:
                    send(at.z < LINE - 1, 0, at.device(at.z + 1, at.f, at.g))
                if sinking:
                    send(at.z > 0, 1, at.device(at.z - 1, at.f, at.g))
            if axis == "f" and i > last:
                for step in range(1, at.nf):
                    send(True, 1 + step, at.device(at.z, (at.f + step) % at.nf, at.g))
            if axis == "g" and i > last:
                for step in range(1, at.ng):
                    send(True, at.nf + step, at.device(at.z, at.f, (at.g + step) % at.ng))
        send(True, at.nf + at.ng, at.partner(), pair=True)

    def begin(self):
        for number in range(len(self.sections)):
            at = self.places[number]
            self.forward(number, True, self.own(number), 0, 0, 0)
            own = pltpu.make_async_copy(
                self.own(number),
                self.block(number, at.z, at.f, at.g),
                self.pair_sems.at[number, at.blocks],
            )
            if self.phase.ending:
                own.wait()
            else:
                own.start()

    def arrival(self, number, dz, df, dg):
        at = self.places[number]
        z, f, g = at.z + dz, (at.f + df) % at.nf, (at.g + dg) % at.ng
        condition = present(at, dz)
        block = self.block(number, z, f, g)
        sem = self.plane_sems.at[number, at.index(z, f, g)]
        if not self.phase.ending:
            when(condition, functools.partial(await_block, block, sem))
        self.forward(number, condition, block, dz, df, dg)

    def events(self):
        marked = [
            (hops, number, place, item)
            for place, (hops, *item) in enumerate(steps_of(self.at)[1:])
            for number in range(len(self.sections))
        ]
        marked.sort(key=lambda entry: entry[:3])
        return [functools.partial(self.arrival, number, *item) for _, number, _, item in marked]

    def from_partner(self, number, dz, df, dg):
        at = self.places[number]
        f, g = at.split(*at.split(at.f, at.g, at.core), 1 - at.core)
        z, f, g = at.z + dz, (f + df) % at.nf, (g + dg) % at.ng
        sem = self.pair_sems.at[number, at.index(z, f, g)]
        when(
            present(at, dz), functools.partial(await_block, self.block(number, 0, 0, 0), sem)
        )

    def steps(self, lag):
        events = self.events()

        def close(event):
            self.phase.ending = True
            event()
            self.from_partner(*event.args)
            self.phase.ending = False

        def step(number):
            events[number]()
            if number >= lag:
                close(events[number - lag])

        def rest():
            for event in events[-lag:]:
                close(event)
            self.phase.ending = True
            self.begin()
            for number in range(len(self.sections)):
                self.from_partner(number, 0, 0, 0)
            self.phase.ending = False

        return [functools.partial(step, number) for number in range(len(events))], rest


def trade_in(at, source_ref, target_ref, send_sems, recv_sems, phase):
    slots, positions = source_ref.shape[0], source_ref.shape[1]
    group = at.seq_size // slots
    own_slot, own_part = at.seq // group, at.seq % group
    same = at.seq // slots == own_part
    lane = at.seq % slots
    target = target_ref.at[pl.ds(pl.multiple_of(lane * positions, positions), positions), :]
    for step in range(slots):
        slot = (own_slot + step) % slots
        if step == 0 and not phase.ending:
            local = pltpu.make_async_copy(source_ref.at[slot], target, recv_sems.at[lane])
            when(same, local.start)
        start_copy(
            phase,
            True if step else jnp.logical_not(same),
            source_ref.at[slot],
            target,
            send_sems.at[step],
            recv_sems.at[lane],
            (slot * group + at.seq // slots, at.y),
        )
        if phase.ending:
            await_block(target_ref.at[pl.ds(step * positions, positions), :], recv_sems.at[step])


def trade_out(at, source_ref, target_ref, send_sems, recv_sems, phase):
    slots, positions = target_ref.shape[0], target_ref.shape[1]
    group = at.seq_size // slots
    own_slot, own_part = at.seq // group, at.seq % group
    same = at.seq // slots == own_part
    target = target_ref.at[own_slot]
    for step in range(slots):
        lane = (at.seq + step) % slots
        source = source_ref.at[pl.ds(pl.multiple_of(lane * positions, positions), positions), :]
        if step == 0 and not phase.ending:
            local = pltpu.make_async_copy(source, target, recv_sems.at[own_slot])
            when(same, local.start)
        start_copy(
            phase,
            True if step else jnp.logical_not(same),
            source,
            target,
            send_sems.at[step],
            recv_sems.at[own_slot],
            (own_part * slots + lane, at.y),
        )
        if phase.ending:
            await_block(target_ref.at[step], recv_sems.at[step])


def first_kernel(sizes, spans, weight_ref, gains_ref, hidden_ref, whole_ref, rows_ref, *refs):
    at = Place(*sizes)
    sems, (trade_send, trade_recv, pack_ref, pack_sems) = refs[:3], refs[3:]
    width, extra_width = weight_ref.shape[1], gains_ref.shape[1]
    loads = [
        pltpu.make_async_copy(weight_ref, pack_ref.at[:, pl.ds(0, width)], pack_sems.at[0]),
        pltpu.make_async_copy(gains_ref, pack_ref.at[:, pl.ds(width, extra_width)], pack_sems.at[1]),
    ]
    for load in loads:
        load.start()
    peers, count = plane_peers(at)
    more, extra = slot_peers(at, hidden_ref.shape[0])
    meet(peers + more, count + extra)
    for load in loads:
        load.wait()
    phase = Phase()
    sections, start = [], 0
    for size, order in spans:
        sections.append((pack_ref, whole_ref, pl.ds(start, size), order))
        start += size
    gather = Gather(at, sections, sems, phase)
    steps, rest = gather.steps(12)
    gather.begin()
    trade_in(at, hidden_ref, rows_ref, trade_send, trade_recv, phase)
    run_all(steps)
    rest()
    phase.ending = True
    trade_in(at, hidden_ref, rows_ref, trade_send, trade_recv, phase)


def gather_first(weight, gains, hidden, seq_size, fsdp_size):
    slots, positions, model = hidden.shape
    nf, ng = seq_size // (2 * LINE), fsdp_size
    devices = seq_size * fsdp_size
    dma = pltpu.SemaphoreType.DMA
    shard, width = weight.shape[0], weight.shape[1] + gains.shape[1]
    half = weight.shape[1] // 2
    spans = ((half, "zfg"), (width - half, "zfg"))
    return pl.pallas_call(
        functools.partial(first_kernel, (seq_size, fsdp_size), spans),
        out_shape=(
            jax.ShapeDtypeStruct((shard * devices, width), BF16),
            jax.ShapeDtypeStruct((slots * positions, model), BF16),
        ),
        in_specs=[pl.BlockSpec(memory_space=pltpu.VMEM)] * 3,
        out_specs=[pl.BlockSpec(memory_space=pl.ANY)] * 2,
        scratch_shapes=Gather.scratch(len(spans), nf, ng)
        + [dma((slots,)), dma((slots,)), pltpu.VMEM((shard, width), BF16), dma((2,))],
        compiler_params=pltpu.CompilerParams(collective_id=0, has_side_effects=True),
        name="gather_first",
    )(weight, gains, hidden)


def add_blocks(target, others):
    width = target.shape[1]
    piece = max(size for size in range(LANES, 1025, LANES) if width % size == 0)

    def body(number, carry):
        columns = pl.ds(pl.multiple_of(number * piece, LANES), piece)
        total = target[:, columns].astype(F32)
        for other in others:
            total = total + other[:, columns].astype(F32)
        target[:, columns] = total.astype(target.dtype)
        return carry

    lax.fori_loop(0, width // piece, body, 0)


def line_targets(at):
    order = []
    for dz in (-3, 3, -2, 2, -1, 1, 0):
        for df in list(range(1, at.nf)) + [0]:
            for dg in list(range(1, at.ng)) + [0]:
                order.append((dg == 0, df == 0, -abs(dz), dz, df, dg))
    order.sort(key=lambda item: item[:3])
    return [item[3:] for item in order]


class Phase:
    def __init__(self):
        self.ending = False


def start_copy(phase, condition, source, target, send_sem, recv_sem, device):
    copy = pltpu.make_async_remote_copy(
        src_ref=source,
        dst_ref=target,
        send_sem=send_sem,
        recv_sem=recv_sem,
        device_id=device,
        device_id_type=MESH,
    )
    when(condition, copy.wait_send if phase.ending else copy.start)


def run_all(events):
    for event in events:
        event()


def await_block(buffer, sem):
    pltpu.make_async_copy(buffer, buffer, sem).wait()


class Scatter:
    PARTS = 17

    @staticmethod
    def scratch(order, rows, width, nf, ng):
        dma = pltpu.SemaphoreType.DMA
        plane, beyond_g = LINE * nf * ng, (ng - 1) * LINE * nf
        beyond_f = (nf - 1) * (LINE if order == "fz" else 1)
        line = LINE * (1 if order == "fz" else nf)
        counts = (plane, plane, beyond_g, beyond_f, line, line)
        buffers = [pltpu.VMEM((count, rows, width), BF16) for count in counts]
        sems = (plane, plane, plane, beyond_g, beyond_g, beyond_f, beyond_f, line, line, line, line)
        return buffers + [dma((count,)) for count in sems]

    def __init__(self, at, source, columns, order, scratch, phase):
        self.at, self.source, self.columns, self.order = at, source, columns, order
        self.phase = phase
        self.acc, self.from_pair, self.from_g, self.from_f = scratch[:4]
        self.from_below, self.from_above = scratch[4:6]
        self.load_sems, self.pair_send, self.pair_recv = scratch[6:9]
        self.g_send, self.g_recv, self.f_send, self.f_recv = scratch[9:13]
        self.up_send, self.up_recv, self.down_send, self.down_recv = scratch[13:]
        self.rows = self.acc.shape[1]

    def where_is(self, dz, df, dg):
        at = self.at
        return at.z + dz, (at.f + df) % at.nf, (at.g + dg) % at.ng

    def rows_of(self, z, f, g, core=None):
        start = pl.multiple_of(self.at.row_block(z, f, g, core) * self.rows, self.rows)
        return self.source.at[pl.ds(start, self.rows), self.columns]

    def begin(self, dz, df, dg):
        at = self.at
        z, f, g = self.where_is(dz, df, dg)
        place, other = at.index(z, f, g), 1 - at.core
        pf, pg = at.split(*at.split(at.f, at.g, at.core), other)
        pf, pg = (pf + df) % at.nf, (pg + dg) % at.ng
        there = at.index(z, pf, pg)

        def body():
            if self.phase.ending:
                await_block(self.from_pair.at[there], self.pair_send.at[there])
                return
            pltpu.make_async_copy(
                self.rows_of(z, f, g), self.acc.at[place], self.load_sems.at[place]
            ).start()
            pltpu.make_async_remote_copy(
                src_ref=self.rows_of(z, pf, pg, other),
                dst_ref=self.from_pair.at[there],
                send_sem=self.pair_send.at[there],
                recv_sem=self.pair_recv.at[there],
                device_id=at.partner(),
                device_id_type=MESH,
            ).start()

        when(present(at, dz), body)

    def join(self, condition, place, parts):
        if self.phase.ending:
            return

        def body():
            ready = [(buffer, sem) for allowed, buffer, sem in parts if allowed is True]
            for buffer, sem in ready:
                await_block(buffer, sem)
            if ready:
                add_blocks(self.acc.at[place], [buffer for buffer, _ in ready])
            for allowed, buffer, sem in parts:
                if allowed is not True:

                    def more(buffer=buffer, sem=sem):
                        await_block(buffer, sem)
                        add_blocks(self.acc.at[place], [buffer])

                    pl.when(allowed)(more)

        when(condition, body)

    def over_pair(self, dz, df, dg):
        at = self.at
        z, f, g = self.where_is(dz, df, dg)
        condition = present(at, dz)
        place = at.index(z, f, g)
        if not self.phase.ending:
            when(
                condition,
                functools.partial(await_block, self.acc.at[place], self.load_sems.at[place]),
            )
        self.join(condition, place, [(True, self.from_pair.at[place], self.pair_recv.at[place])])
        if dg:
            slot = (dg - 1) * LINE * at.nf + z * at.nf + f
            start_copy(
                self.phase,
                condition,
                self.acc.at[place],
                self.from_g.at[slot],
                self.g_send.at[slot],
                self.g_recv.at[slot],
                at.device(at.z, at.f, g),
            )

    def g_parts(self, z, f):
        slots = [(step - 1) * LINE * self.at.nf + z * self.at.nf + f for step in range(1, self.at.ng)]
        return [(True, self.from_g.at[slot], self.g_recv.at[slot]) for slot in slots]

    def f_slot(self, z, step):
        return (step - 1) * LINE + z if self.order == "fz" else step - 1

    def f_parts(self, z):
        slots = [self.f_slot(z, step) for step in range(1, self.at.nf)]
        return [(True, self.from_f.at[slot], self.f_recv.at[slot]) for slot in slots]

    def line_slot(self, z, f):
        return z if self.order == "fz" else z * self.at.nf + f

    def line_parts(self, dz, z, f):
        slot, parts = self.line_slot(z, f), []
        if 0 <= dz < LINE - 1:
            parts.append((self.at.z > 0, self.from_below.at[slot], self.up_recv.at[slot]))
        if 1 - LINE < dz <= 0:
            parts.append((self.at.z < LINE - 1, self.from_above.at[slot], self.down_recv.at[slot]))
        return parts

    def send_f(self, condition, df, z, f, place):
        slot = self.f_slot(z, df)
        start_copy(
            self.phase,
            condition,
            self.acc.at[place],
            self.from_f.at[slot],
            self.f_send.at[slot],
            self.f_recv.at[slot],
            self.at.device(self.at.z, f, self.at.g),
        )

    def send_line(self, condition, dz, z, f, place):
        slot = self.line_slot(z, f)
        rising = dz > 0
        start_copy(
            self.phase,
            condition,
            self.acc.at[place],
            (self.from_below if rising else self.from_above).at[slot],
            (self.up_send if rising else self.down_send).at[slot],
            (self.up_recv if rising else self.down_recv).at[slot],
            self.at.device(self.at.z + (1 if rising else -1), self.at.f, self.at.g),
        )

    def second(self, dz, df):
        z, f, _ = self.where_is(dz, df, 0)
        condition = present(self.at, dz)
        place = self.at.index(z, f, self.at.g)
        parts = self.g_parts(z, f)
        if self.order == "zf":
            parts = parts + self.line_parts(dz, z, f)
        self.join(condition, place, parts)
        if self.order == "zf" and dz:
            self.send_line(condition, dz, z, f, place)
        elif df:
            self.send_f(condition, df, z, f, place)

    def third(self, dz):
        z, f = self.at.z + dz, self.at.f
        condition = present(self.at, dz)
        place = self.at.index(z, f, self.at.g)
        parts = self.f_parts(z)
        if self.order == "fz":
            parts = parts + self.line_parts(dz, z, f)
        self.join(condition, place, parts)
        if dz:
            self.send_line(condition, dz, z, f, place)

    def stages(self):
        order = line_targets(self.at)
        part = functools.partial
        begins = [part(self.begin, *item) for item in order]
        pairs = [part(self.over_pair, *item) for item in order]
        if self.order == "fz":
            seconds = [part(self.second, *item[:2]) for item in order if item[2] == 0]
            thirds = [part(self.third, dz) for dz in (-3, 3, -2, 2, -1, 1, 0)]
        else:
            dfs = list(range(1, self.at.nf)) + [0]
            seconds = [part(self.second, dz, df) for dz in (-3, 3, -2, 2, -1, 1, 0) for df in dfs]
            thirds = [part(self.third, 0)]
        return begins, pairs, seconds, thirds

    def store(self, target, start):
        place = self.at.index(self.at.z, self.at.f, self.at.g)
        target[:, pl.ds(start, self.acc.shape[2])] = self.acc[place].astype(F32)


def mixed(first, second):
    marked = []
    for kind, steps in enumerate((first, second)):
        marked += [((i + 0.5) / len(steps), kind, step) for i, step in enumerate(steps)]
    return [step for _, _, step in sorted(marked, key=lambda item: item[:2])]


def pipelined(scatters):
    first, mids, lasts, starts = [], [], [], {}
    for scatter in scatters:
        begins, pairs, seconds, thirds = scatter.stages()
        starts.update(zip(pairs, begins))
        first += [step for step in pairs if step.args[2]]
        mid = []
        for second in seconds:
            mid += [step for step in pairs if step.args == (*second.args, 0)] + [second]
        mids.append(mid)
        lasts.append(thirds)
    events = list(first)
    for slot in range(len(scatters) + 1):
        some = lasts[slot - 1] if slot else []
        if slot < len(scatters):
            some = mixed(some, mids[slot]) if some else mids[slot]
        events += some
    begins = [starts[event] for event in events if event in starts]
    later = iter(begins[AHEAD:])

    def with_begin(event):
        begin = next(later, None) if event in starts else None
        return event if begin is None else functools.partial(run_all, [event, begin])

    return begins[:AHEAD], [with_begin(event) for event in events], len(first)


AHEAD = 64


def lagged(events, lag, phase):
    def close(event):
        phase.ending = True
        event()
        phase.ending = False

    def step(number):
        events[number]()
        if number >= lag:
            close(events[number - lag])

    def rest():
        for event in events[-lag:]:
            close(event)

    return [functools.partial(step, number) for number in range(len(events))], rest


def split_scratch(refs, count):
    size = Scatter.PARTS
    return [refs[i * size : (i + 1) * size] for i in range(count)], refs[count * size :]


def scatter_sections(at, sources, spans, scratches, phase):
    scatters, places = [], []
    for number, parts in enumerate(spans):
        start = 0
        for size, order in parts:
            scratch = scratches[len(scatters)]
            scatters.append(Scatter(at, sources[number], pl.ds(start, size), order, scratch, phase))
            places.append((number, start))
            start += size
    return scatters, places


def scatter_kernel(sizes, spans, *refs):
    at = Place(*sizes)
    count, sections = len(spans), sum(len(parts) for parts in spans)
    sources, refs = refs[:count], refs[count:]
    input_ref, vector_ref, grad_ref, total_ref = refs[:4]
    owned, refs = refs[4 : 4 + count], refs[4 + count :]
    scratches, refs = split_scratch(refs, sections)
    sq_g, sq_f, sq_z, sq_c, trade_send, trade_recv, sq_send, sq_recv = refs
    slots = grad_ref.shape[0]
    peers, number = plane_peers(at)
    more, extra = slot_peers(at, slots)
    meet(peers + more, number + extra)
    phase = Phase()
    send = functools.partial(start_copy, phase)
    scatters, places = scatter_sections(at, sources, spans, scratches, phase)
    begins, events, _ = pipelined(scatters)
    steps, rest = lagged(events, 24, phase)
    other = 1 - at.core

    def vectors_g():
        for step in range(1, at.ng):
            device = at.device(at.z, at.f, (at.g + step) % at.ng)
            send(True, sq_g.at[at.g], sq_g.at[at.g], sq_send.at[0, step], sq_recv.at[0, at.g], device)

    def vectors_f():
        for step in range(1, at.nf):
            device = at.device(at.z, (at.f + step) % at.nf, at.g)
            send(True, sq_f.at[at.f], sq_f.at[at.f], sq_send.at[1, step], sq_recv.at[1, at.f], device)

    def line_send(condition, held, kind):
        device = at.device(at.z - 1 if kind else at.z + 1, at.f, at.g)
        send(condition, sq_z.at[held], sq_z.at[held], sq_send.at[2 + kind, held], sq_recv.at[2, held], device)

    def vectors_line(distance):
        for kind, held in enumerate((at.z - distance, at.z + distance)):
            there = held < LINE if kind else held >= 0
            onward = at.z > 0 if kind else at.z < LINE - 1
            if distance and not phase.ending:
                when(
                    there,
                    functools.partial(await_block, sq_z.at[held], sq_recv.at[2, held]),
                )
            line_send(both(there, onward), held, kind)

    def vectors_pair():
        send(
            True,
            sq_c.at[at.core],
            sq_c.at[at.core],
            sq_send.at[4, 0],
            sq_recv.at[3, at.core],
            at.partner(),
        )

    def sums():
        def g():
            for step in range(1, at.ng):
                peer = (at.g + step) % at.ng
                await_block(sq_g.at[peer], sq_recv.at[0, peer])
            total = sq_g[0]
            for number in range(1, at.ng):
                total = total + sq_g[number]
            sq_f[at.f] = total
            vectors_f()

        def f():
            for step in range(1, at.nf):
                peer = (at.f + step) % at.nf
                await_block(sq_f.at[peer], sq_recv.at[1, peer])
            total = sq_f[0]
            for number in range(1, at.nf):
                total = total + sq_f[number]
            sq_z[at.z] = total
            vectors_line(0)

        def pair():
            total = sq_z[0]
            for number in range(1, LINE):
                total = total + sq_z[number]
            sq_c[at.core] = total
            vectors_pair()

        return [g, f] + [functools.partial(vectors_line, d) for d in range(1, LINE)] + [pair]

    sq_g[at.g] = vector_ref[...]
    run_all(begins)
    vectors_g()
    trade_out(at, input_ref, grad_ref, trade_send, trade_recv, phase)
    run_all(mixed(steps, sums()))
    for scatter, (number, start) in zip(scatters, places):
        scatter.store(owned[number], start)
    await_block(sq_c.at[other], sq_recv.at[3, other])
    total_ref[...] = sq_c[0] + sq_c[1]

    rest()
    phase.ending = True
    run_all(begins)
    trade_out(at, input_ref, grad_ref, trade_send, trade_recv, phase)
    vectors_g()
    vectors_f()
    for distance in range(LINE):
        vectors_line(distance)
    vectors_pair()


def scatter_last(sources, spans, input_grad, vectors, slots, seq_size, fsdp_size):
    rows = sources[0].shape[0] // (seq_size * fsdp_size)
    own_rows, model = input_grad.shape
    positions = own_rows // slots
    nf, ng = seq_size // (2 * LINE), fsdp_size
    dma = pltpu.SemaphoreType.DMA
    widest = max(nf, ng, LINE)
    vmem = pl.BlockSpec(memory_space=pltpu.VMEM)
    scratch = []
    for parts in spans:
        for size, order in parts:
            scratch += Scatter.scratch(order, rows, size, nf, ng)
    return pl.pallas_call(
        functools.partial(scatter_kernel, (seq_size, fsdp_size), spans),
        out_shape=tuple(
            [
                jax.ShapeDtypeStruct((slots, positions, model), BF16),
                jax.ShapeDtypeStruct(vectors.shape, F32),
            ]
            + [jax.ShapeDtypeStruct((rows, source.shape[1]), F32) for source in sources]
        ),
        in_specs=[pl.BlockSpec(memory_space=pl.ANY)] * len(sources) + [vmem] * 2,
        out_specs=[vmem] * (2 + len(sources)),
        scratch_shapes=scratch
        + [pltpu.VMEM((size, *vectors.shape), F32) for size in (ng, nf, LINE, 2)]
        + [dma((slots,)), dma((slots,)), dma((5, widest)), dma((4, widest))],
        compiler_params=pltpu.CompilerParams(
            collective_id=3, has_side_effects=True, vmem_limit_bytes=63_000_000
        ),
        name="scatter_last",
    )(*sources, input_grad, vectors)


def first_half(shape):
    lane = lax.broadcasted_iota(jnp.int32, shape, 1)
    return lane % 64 < 32


def turn(values, cosine, sine):
    half = first_half(values.shape)
    away = jnp.where(half, -pltpu.roll(values, 96, 1), pltpu.roll(values, 32, 1))
    return values * cosine + away * sine


def turn_back(grads, cosine, sine):
    half = first_half(grads.shape)
    moved = grads * sine
    away = jnp.where(half, pltpu.roll(moved, 96, 1), -pltpu.roll(moved, 32, 1))
    return grads * cosine + away


def normalize(values):
    average = jnp.mean(values, axis=-1, keepdims=True)
    centered = values - average
    variance = jnp.mean(centered * centered, axis=-1, keepdims=True)
    inverse = lax.rsqrt(variance + EPS)
    return centered * inverse, inverse


def norm_back(grad_normed, normed, inverse, gain_values):
    scaled = grad_normed * gain_values
    first_mean = jnp.mean(scaled, axis=-1, keepdims=True)
    second_mean = jnp.mean(scaled * normed, axis=-1, keepdims=True)
    return inverse * (scaled - first_mean - normed * second_mean)


def head_lanes(shape, head):
    return lax.broadcasted_iota(jnp.int32, shape, 1) // 64 == head


def scores_of(keys, queries, bias):
    scores = lax.dot_general(keys, queries, (((1,), (1,)), ((), ())), preferred_element_type=F32)
    return scores + bias


def key_bias(length, shape):
    return jnp.where(lax.broadcasted_iota(jnp.int32, shape, 0) < length, 0.0, -jnp.inf)


def attend(length, queries, keys, values):
    queries = queries * 0.125
    bias = key_bias(length, (keys.shape[0], 1))
    zero = jnp.zeros((), BF16)
    total, logs = None, []
    for head in range(2):
        only = head_lanes(queries.shape, head)
        scores = scores_of(keys, jnp.where(only, queries, zero), bias)
        largest = jnp.max(scores, axis=0, keepdims=True)
        weights = jnp.exp(scores - largest)
        summed = jnp.sum(weights, axis=0, keepdims=True)
        logs.append(largest + jnp.log(summed))
        held = jnp.where(head_lanes(values.shape, head), values, zero)
        part = lax.dot_general(
            held, weights.astype(BF16), (((0,), (0,)), ((), ())), preferred_element_type=F32
        )
        part = part / summed
        total = part if total is None else total + part
    return total.T.astype(BF16), logs


FRONT_TILE = 512


def front_kernel(sizes, group, spans, *refs):
    at = Place(*sizes)
    count = len(spans)
    length_ref, x_ref, gains_ref, cos_ref, sin_ref, w_ref, dy_ref = refs[:7]
    sources, refs = refs[7 : 7 + count], refs[7 + count :]
    act_ref, gain_ref, q_ref, shared_out, o_ref, log_ref, dy_rows_ref = refs[:7]
    wholes, refs = refs[7 : 7 + count], refs[7 + count :]
    sems, (trade_send, trade_recv, share_send, share_recv, shared_ref, out_sem) = refs[:3], refs[3:]
    step = pl.program_id(0)
    rows, model = q_ref.shape
    slots = dy_ref.shape[0]
    tile = o_ref.shape[0]
    tiles = rows // tile
    projecting = 3 * model // FRONT_TILE
    steps = projecting + model // LANES * tiles
    kept = 2 * model // FRONT_TILE
    phase = Phase()
    sections = []
    for number, parts in enumerate(spans):
        start = 0
        for size, order in parts:
            sections.append((sources[number], wholes[number], pl.ds(start, size), order))
            start += size
    gather = Gather(at, sections, sems, phase)
    base, part = (at.seq // group) * group, at.seq % group
    members = [base + (part + other) % group for other in range(1, group)]
    own_rows = pl.ds(pl.multiple_of(part * rows, rows), rows)

    @pl.when(step == 0)
    def _():
        peers, number = plane_peers(at)
        more, extra = slot_peers(at, slots)
        others = [(True, (member, at.y)) for member in members]
        meet(peers + more + others, number + extra + group - 1)

    @pl.when(step == 0)
    def _():
        gather.begin()
        trade_in(at, dy_ref, dy_rows_ref, trade_send, trade_recv, phase)

    @pl.when(step == 0)
    def _():
        normed, _ = normalize(x_ref[...].astype(F32))
        turned = gains_ref[...].astype(F32).T
        gain_ref[...] = turned[:8]
        act_ref[...] = (normed * turned[:1]).astype(BF16)

    def share(number):
        place = shared_ref.at[own_rows, pl.ds(number * FRONT_TILE, FRONT_TILE)]
        for other, member in enumerate(members):
            start_copy(
                phase,
                True,
                place,
                place,
                share_send.at[number, other],
                share_recv.at[number, part],
                (member, at.y),
            )

    def receive():
        for number in range(kept):
            for other in range(1, group):
                source = (part + other) % group
                place = shared_ref.at[
                    pl.ds(pl.multiple_of(source * rows, rows), rows),
                    pl.ds(number * FRONT_TILE, FRONT_TILE),
                ]
                await_block(place, share_recv.at[number, source])
        pltpu.make_async_copy(shared_ref, shared_out, out_sem).start()

    for number in range(kept):
        pl.when(step == number + 1)(functools.partial(share, number))
    pl.when(step == projecting)(receive)

    @pl.when(step < projecting)
    def _():
        mixed = jnp.dot(act_ref[...], w_ref[...], preferred_element_type=F32)

        def turned():
            cosine, sine = cos_ref[...], sin_ref[...]
            pieces = [
                turn(mixed[:, start : start + LANES], cosine, sine).astype(BF16)
                for start in range(0, FRONT_TILE, LANES)
            ]
            return jnp.concatenate(pieces, axis=1)

        @pl.when(step < kept // 2)
        def _():
            columns = pl.ds(pl.multiple_of(step * FRONT_TILE, FRONT_TILE), FRONT_TILE)
            shared_ref[own_rows, columns] = turned()

        @pl.when(both(step >= kept // 2, step < kept))
        def _():
            columns = pl.ds(pl.multiple_of(step * FRONT_TILE, FRONT_TILE), FRONT_TILE)
            shared_ref[own_rows, columns] = mixed.astype(BF16)

        @pl.when(step >= kept)
        def _():
            columns = pl.ds(pl.multiple_of((step - kept) * FRONT_TILE, FRONT_TILE), FRONT_TILE)
            q_ref[:, columns] = turned()

    @pl.when(step >= projecting)
    def _():
        pair, piece = (step - projecting) // tiles, (step - projecting) % tiles
        start = pl.multiple_of(pair * LANES, LANES)
        out, logs = attend(
            length_ref[0],
            q_ref[pl.ds(pl.multiple_of(piece * tile, tile), tile), pl.ds(start, LANES)],
            shared_ref[:, pl.ds(start, LANES)],
            shared_ref[:, pl.ds(pl.multiple_of(model + start, LANES), LANES)],
        )
        o_ref[...] = out
        for head in range(2):
            log_ref[0, head : head + 1, :] = logs[head]

    events, rest = gather.steps(24)
    pace = FRONT_PACE
    for number in range(steps - 1):
        group_events = events[number * pace : (number + 1) * pace]
        if group_events:
            pl.when(step == number)(functools.partial(run_all, group_events))

    @pl.when(step == steps - 1)
    def _():
        run_all(events[(steps - 1) * pace :])
        rest()
        phase.ending = True
        trade_in(at, dy_ref, dy_rows_ref, trade_send, trade_recv, phase)
        for number in range(kept):
            share(number)
        pltpu.make_async_copy(shared_ref, shared_out, out_sem).wait()
        phase.ending = False


FRONT_PACE = 4


def front(length, x_rows, cosine, sine, weight, dy, sources, spans, group, tile, seq_size, fsdp_size):
    rows, model = x_rows.shape
    slots, positions, _ = dy.shape
    pairs, tiles = model // LANES, rows // tile
    projecting, kept = 3 * model // FRONT_TILE, 2 * model // FRONT_TILE
    nf, ng = seq_size // (2 * LINE), fsdp_size
    devices = seq_size * fsdp_size
    count = sum(len(parts) for parts in spans)
    dma = pltpu.SemaphoreType.DMA
    vmem, anywhere = pl.BlockSpec(memory_space=pltpu.VMEM), pl.BlockSpec(memory_space=pl.ANY)

    def pair_of(i):
        return jnp.maximum(i - projecting, 0) // tiles

    def tile_of(i):
        return jnp.maximum(i - projecting, 0) % tiles

    return pl.pallas_call(
        functools.partial(front_kernel, (seq_size, fsdp_size), group, spans),
        grid=(projecting + pairs * tiles,),
        out_shape=tuple(
            [
                jax.ShapeDtypeStruct((rows, model), BF16),
                jax.ShapeDtypeStruct((8, model), F32),
                jax.ShapeDtypeStruct((rows, model), BF16),
                jax.ShapeDtypeStruct((rows * group, 2 * model), BF16),
                jax.ShapeDtypeStruct((rows, model), BF16),
                jax.ShapeDtypeStruct((pairs, 8, rows), F32),
                jax.ShapeDtypeStruct((slots * positions, model), BF16),
            ]
            + [
                jax.ShapeDtypeStruct((source.shape[0] * devices, source.shape[1]), BF16)
                for source in sources
            ]
        ),
        in_specs=[pl.BlockSpec(memory_space=pltpu.SMEM), vmem]
        + [pl.BlockSpec((model, LANES), lambda i: (0, 3 * model // LANES)), vmem, vmem]
        + [
            pl.BlockSpec(
                (model, FRONT_TILE),
                lambda i: (0, (jnp.minimum(i, projecting - 1) + projecting - kept) % projecting),
            )
        ]
        + [vmem] * (1 + len(sources)),
        out_specs=[
            vmem,
            vmem,
            vmem,
            anywhere,
            pl.BlockSpec((tile, LANES), lambda i: (tile_of(i), pair_of(i))),
            pl.BlockSpec((1, 8, tile), lambda i: (pair_of(i), 0, tile_of(i))),
        ]
        + [anywhere] * (1 + len(sources)),
        scratch_shapes=Gather.scratch(count, nf, ng)
        + [dma((slots,)), dma((slots,)), dma((kept, group)), dma((kept, group))]
        + [pltpu.VMEM((rows * group, 2 * model), BF16), dma],
        compiler_params=pltpu.CompilerParams(
            collective_id=1, has_side_effects=True, vmem_limit_bytes=63_000_000
        ),
        name="front",
    )(length, x_rows, weight, cosine, sine, weight, dy, *sources)


def attend_back(length, queries, keys, values, grads, heads_out, logs):
    queries = queries * 0.125
    bias = key_bias(length, (keys.shape[0], 1))
    zero = jnp.zeros((), BF16)
    product = (grads.astype(F32) * heads_out.astype(F32)).T
    dq = dk = dv = None
    for head in range(2):
        only = head_lanes(queries.shape, head)
        query = jnp.where(only, queries, zero)
        grad = jnp.where(only, grads, zero)
        key = jnp.where(head_lanes(keys.shape, head), keys, zero)
        delta = jnp.sum(product[64 * head : 64 * head + 64], axis=0, keepdims=True)
        scores = scores_of(keys, query, bias)
        probs = jnp.exp(scores - logs[head : head + 1])
        grad_probs = lax.dot_general(
            values, grad, (((1,), (1,)), ((), ())), preferred_element_type=F32
        )
        grad_scores = (probs * (grad_probs - delta)).astype(BF16)
        value_part = jnp.dot(probs.astype(BF16), grad, preferred_element_type=F32)
        key_part = jnp.dot(grad_scores, query, preferred_element_type=F32)
        query_part = lax.dot_general(
            key, grad_scores, (((0,), (0,)), ((), ())), preferred_element_type=F32
        )
        dq = query_part if dq is None else dq + query_part
        dk = key_part if dk is None else dk + key_part
        dv = value_part if dv is None else dv + value_part
    return dq.T * 0.125, dk, dv


def back_kernel(sizes, group, spans, *refs):
    at = Place(*sizes)
    sections = sum(len(parts) for parts in spans)
    count = len(spans)
    length_ref, q_ref, k_ref, v_ref, g_ref, o_ref, log_ref, cos_ref, sin_ref, result_ref = refs[:10]
    act_ref, x_ref, middle_ref, gain_ref, vectors_ref, w_ref = refs[10:16]
    sources, refs = refs[16 : 16 + count], refs[16 + count :]
    out_ref, part_ref, grad_x_ref, sums_ref = refs[:4]
    owned, refs = refs[4 : 4 + count], refs[4 + count :]
    scratches, refs = split_scratch(refs, sections)
    dk_acc, dv_acc, parts_ref, arrived, sum_send, sum_recv, trade_send, trade_recv = refs[:8]
    mixed_ref, act_turned, grad_act = refs[8:]
    step = pl.program_id(0)
    tile = q_ref.shape[0]
    rows, model = result_ref.shape
    tiles, pairs = rows // tile, model // LANES
    attending = pairs * tiles
    steps = attending + 1 + 3 * model // FRONT_TILE
    slots = out_ref.shape[0]
    phase = Phase()
    scatters, places = scatter_sections(at, sources, spans, scratches, phase)
    begins, events, ahead = pipelined(scatters)
    events, rest = lagged(events, 40, phase)
    base, part = (at.seq // group) * group, at.seq % group
    members = [base + (part + other) % group for other in range(1, group)]

    def columns_of(pair):
        return pl.ds(pl.multiple_of(pair * LANES, LANES), LANES)

    def share(pair):
        for kind in range(2):
            for other, member in enumerate(members):
                owner = (part + other + 1) % group
                start_copy(
                    phase,
                    True,
                    parts_ref.at[kind, pl.ds(pl.multiple_of(owner * rows, rows), rows), columns_of(pair)],
                    arrived.at[kind, other, :, columns_of(pair)],
                    sum_send.at[kind, other, pair],
                    sum_recv.at[kind, other, pair],
                    (member, at.y),
                )

    @pl.when(step == 0)
    def _():
        peers, number = plane_peers(at)
        more, extra = slot_peers(at, slots)
        others = [(True, (member, at.y)) for member in members]
        meet(peers + more + others, number + extra + group - 1)
        run_all(begins)
        trade_out(at, result_ref, out_ref, trade_send, trade_recv, phase)
        run_all(events[:ahead])

    for number in range(1, steps):
        some = events[ahead + (number - 1) * BACK_PACE : ahead + number * BACK_PACE]
        if some:
            pl.when(step == number)(functools.partial(run_all, some))

    shared_now = jnp.logical_and(both(step > 0, step <= attending), step % tiles == 0)
    pl.when(shared_now)(lambda: share(step // tiles - 1))

    @pl.when(step < attending)
    def _():
        pair, piece = step // tiles, step % tiles
        own = pl.ds(pl.multiple_of(piece * tile, tile), tile)
        dq, dk, dv = attend_back(
            length_ref[0], q_ref[...], k_ref[...], v_ref[...], g_ref[...], o_ref[...], log_ref[0]
        )
        mixed_ref[own, columns_of(pair)] = turn_back(dq, cos_ref[own], sin_ref[own]).astype(BF16)
        if tiles == 1:
            parts_ref[0, :, columns_of(pair)] = dk.astype(BF16)
            parts_ref[1, :, columns_of(pair)] = dv.astype(BF16)
            return

        @pl.when(piece == 0)
        def _():
            dk_acc[...] = dk
            dv_acc[...] = dv

        @pl.when(piece > 0)
        def _():
            dk_acc[...] += dk
            dv_acc[...] += dv

        @pl.when(piece == tiles - 1)
        def _():
            parts_ref[0, :, columns_of(pair)] = dk_acc[...].astype(BF16)
            parts_ref[1, :, columns_of(pair)] = dv_acc[...].astype(BF16)

    def add_parts():
        own = pl.ds(pl.multiple_of(part * rows, rows), rows)

        def body(pair, carry):
            for kind in range(2):
                total = parts_ref[kind, own, columns_of(pair)].astype(F32)
                for other in range(group - 1):
                    piece = arrived.at[kind, other, :, columns_of(pair)]
                    await_block(piece, sum_recv.at[kind, other, pair])
                    total = total + piece[...].astype(F32)
                if kind == 0:
                    total = turn_back(total, cos_ref[...], sin_ref[...])
                start = pl.multiple_of((kind + 1) * model + pair * LANES, LANES)
                mixed_ref[:, pl.ds(start, LANES)] = total.astype(BF16)
            return carry

        lax.fori_loop(0, pairs, body, 0)

    @pl.when(step == attending)
    def _():
        add_parts()
        act_turned[...] = act_ref[...].astype(F32).T.astype(BF16)
        grad_act[...] = jnp.zeros_like(grad_act)

    @pl.when(step > attending)
    def _():
        start = pl.multiple_of((step - attending - 1) * FRONT_TILE, FRONT_TILE)
        grad_mixed = mixed_ref[:, pl.ds(start, FRONT_TILE)]
        grad_act[...] += mm_right_t(grad_mixed, w_ref[...])
        part_ref[...] = mm(act_turned[...], grad_mixed).astype(BF16)

    @pl.when(step == steps - 1)
    def _():
        normed, inverse = normalize(x_ref[...].astype(F32))
        sums_ref[...] = vectors_ref[...]
        sums_ref[5:6, :] = jnp.sum(grad_act[...] * normed, axis=0, keepdims=True)
        grad_x = middle_ref[...] + norm_back(grad_act[...], normed, inverse, gain_ref[0:1, :])
        grad_x_ref[...] = grad_x.astype(BF16)
        run_all(events[ahead + (steps - 1) * BACK_PACE :])
        for scatter, (number, start) in zip(scatters, places):
            scatter.store(owned[number], start)
        rest()
        phase.ending = True
        run_all(begins)
        trade_out(at, result_ref, out_ref, trade_send, trade_recv, phase)

        def body(pair, carry):
            share(pair)
            return carry

        lax.fori_loop(0, pairs, body, 0)
        phase.ending = False


BACK_PACE = 3


def back(
    length,
    queries,
    shared,
    grads,
    heads_out,
    logs,
    cosine,
    sine,
    result,
    act,
    x_rows,
    grad_middle,
    gain,
    vectors,
    weight,
    sources,
    spans,
    tile,
    slots,
    seq_size,
    fsdp_size,
):
    rows, keys, model = queries.shape[0], shared.shape[0], queries.shape[1]
    group, positions = keys // rows, rows // slots
    pairs, tiles = model // LANES, rows // tile
    nf, ng = seq_size // (2 * LINE), fsdp_size
    devices = seq_size * fsdp_size
    shard = model // devices
    vmem, anywhere = pl.BlockSpec(memory_space=pltpu.VMEM), pl.BlockSpec(memory_space=pl.ANY)
    dma = pltpu.SemaphoreType.DMA

    def pair_of(i):
        return jnp.minimum(i, pairs * tiles - 1) // tiles

    def tile_of(i):
        return jnp.minimum(i, pairs * tiles - 1) % tiles

    by_row = pl.BlockSpec((tile, LANES), lambda i: (tile_of(i), pair_of(i)))
    last = 3 * model // FRONT_TILE - 1
    by_column = pl.BlockSpec(
        (model, FRONT_TILE), lambda i: (0, jnp.clip(i - pairs * tiles - 1, 0, last))
    )
    scratch = []
    for parts in spans:
        for size, order in parts:
            scratch += Scatter.scratch(order, shard, size, nf, ng)
    return pl.pallas_call(
        functools.partial(back_kernel, (seq_size, fsdp_size), group, spans),
        grid=(pairs * tiles + 2 + last,),
        out_shape=tuple(
            [
                jax.ShapeDtypeStruct((slots, positions, model), BF16),
                jax.ShapeDtypeStruct((model, 3 * model), BF16),
                jax.ShapeDtypeStruct((rows, model), BF16),
                jax.ShapeDtypeStruct(vectors.shape, F32),
            ]
            + [jax.ShapeDtypeStruct((shard, source.shape[1]), F32) for source in sources]
        ),
        in_specs=[
            pl.BlockSpec(memory_space=pltpu.SMEM),
            by_row,
            pl.BlockSpec((keys, LANES), lambda i: (0, pair_of(i))),
            pl.BlockSpec((keys, LANES), lambda i: (0, pairs + pair_of(i))),
            by_row,
            by_row,
            pl.BlockSpec((1, 8, tile), lambda i: (pair_of(i), 0, tile_of(i))),
            vmem,
            vmem,
            vmem,
        ]
        + [vmem] * 5
        + [by_column]
        + [anywhere] * len(sources),
        out_specs=[anywhere, by_column, vmem, vmem] + [vmem] * len(sources),
        scratch_shapes=scratch
        + [
            pltpu.VMEM((keys, LANES), F32),
            pltpu.VMEM((keys, LANES), F32),
            pltpu.VMEM((2, keys, model), BF16),
            pltpu.VMEM((2, group - 1, rows, model), BF16),
            dma((2, group - 1, pairs)),
            dma((2, group - 1, pairs)),
            dma((slots,)),
            dma((slots,)),
            pltpu.VMEM((rows, 3 * model), BF16),
            pltpu.VMEM((model, rows), BF16),
            pltpu.VMEM((rows, model), F32),
        ],
        compiler_params=pltpu.CompilerParams(
            collective_id=2, has_side_effects=True, vmem_limit_bytes=67_000_000
        ),
        name="back",
    )(
        length,
        queries,
        shared,
        shared,
        grads,
        heads_out,
        logs,
        cosine,
        sine,
        result,
        act,
        x_rows,
        grad_middle,
        gain,
        vectors,
        weight,
        *sources,
    )


def rotary_tables(places, head_size):
    halfway = head_size // 2
    ladder = jnp.arange(halfway, dtype=F32) * (2.0 / head_size)
    inverse = 1.0 / THETA**ladder
    angles = places.astype(F32)[:, None] * inverse[None, :]
    angles = jnp.concatenate([angles] * 4, axis=-1)
    return jnp.cos(angles), jnp.sin(angles)


def mm(left, right):
    return jnp.dot(left, right, preferred_element_type=F32)


def mm_right_t(left, right):
    return lax.dot_general(left, right, (((1,), (1,)), ((), ())), preferred_element_type=F32)


def mm_left_t(left, right):
    return lax.dot_general(left, right, (((0,), (0,)), ((), ())), preferred_element_type=F32)


SQRT_HALF = 0.7071067811865476
INV_SQRT_TAU = 0.3989422804014327


def gelu_and_slope(values):
    share = 0.5 + 0.5 * lax.erf(values * SQRT_HALF)
    density = INV_SQRT_TAU * jnp.exp(-0.5 * values * values)
    return values * share, share + values * density


def mlp_kernel(
    bounds_ref,
    x_ref,
    heads_ref,
    dy_ref,
    w_attn_ref,
    gain_ref,
    w_in_ref,
    w_gate_ref,
    w_down_ref,
    result_ref,
    vectors_ref,
    grad_middle_ref,
    grad_heads_ref,
    attn_part_ref,
    in_part_ref,
    gate_part_ref,
    down_part_ref,
    act,
    act_turned,
    grad_branch,
    grad_turned,
    middle,
    branch,
    grad_act,
):
    step = pl.program_id(0)
    rows = x_ref.shape[0]
    gain = gain_ref[1:2, :]
    position = bounds_ref[1] + lax.broadcasted_iota(jnp.int32, (rows, 1), 0)
    valid = jnp.where(position < bounds_ref[0], 1.0, 0.0).astype(F32)

    def squares(row, values):
        vectors_ref[row : row + 1, :] = jnp.sum(valid * values * values, axis=0, keepdims=True)

    @pl.when(step == 0)
    def _():
        x_wide = x_ref[...].astype(F32)
        attn = mm(heads_ref[...], w_attn_ref[...])
        total = x_wide + attn
        middle[...] = total
        vectors_ref[...] = jnp.zeros_like(vectors_ref)
        squares(0, x_wide)
        squares(1, total)
        squares(3, attn)
        scaled = normalize(total)[0] * gain
        act[...] = scaled.astype(BF16)
        act_turned[...] = scaled.T.astype(BF16)
        grad_y = dy_ref[...].astype(F32) * valid
        grad_branch[...] = grad_y.astype(BF16)
        grad_turned[...] = grad_y.T.astype(BF16)
        branch[...] = jnp.zeros_like(branch)
        grad_act[...] = jnp.zeros_like(grad_act)

    input_half = mm(act[...], w_in_ref[...])
    gate_half = mm(act[...], w_gate_ref[...])
    grad_product = mm(grad_branch[...], w_down_ref[...])
    active, slope = gelu_and_slope(input_half)
    product = (active * gate_half).astype(BF16)
    grad_input = (grad_product * gate_half * slope).astype(BF16)
    grad_gate = (grad_product * active).astype(BF16)
    branch[...] += mm_right_t(product, w_down_ref[...])
    grad_act[...] += mm_right_t(grad_input, w_in_ref[...]) + mm_right_t(grad_gate, w_gate_ref[...])
    in_part_ref[...] = mm(act_turned[...], grad_input).astype(BF16)
    gate_part_ref[...] = mm(act_turned[...], grad_gate).astype(BF16)
    down_part_ref[...] = mm(grad_turned[...], product).astype(BF16)

    @pl.when(step == pl.num_programs(0) - 1)
    def _():
        result = (middle[...] + branch[...]) * valid
        squares(2, result)
        squares(4, branch[...])
        result_ref[...] = result.astype(BF16)
        normed, inverse = normalize(middle[...])
        vectors_ref[6:7, :] = jnp.sum(grad_act[...] * normed, axis=0, keepdims=True)
        grad_y = dy_ref[...].astype(F32) * valid
        grad_middle = grad_y + norm_back(grad_act[...], normed, inverse, gain)
        grad_middle_ref[...] = grad_middle
        grad_attn = grad_middle.astype(BF16)
        grad_heads_ref[...] = mm_right_t(grad_attn, w_attn_ref[...]).astype(BF16)
        attn_part_ref[...] = mm_left_t(heads_ref[...], grad_attn).astype(BF16)


MLP_TILE = 896


def mlp(bounds, x_rows, heads_out, dy_rows, w_attn, gain, w_input, w_down):
    rows, model = x_rows.shape
    wide = w_down.shape[1]
    tile = MLP_TILE if wide % MLP_TILE == 0 else LANES
    steps = wide // tile
    vmem = pl.BlockSpec(memory_space=pltpu.VMEM)
    by_column = pl.BlockSpec((model, tile), lambda i: (0, i))
    part = jax.ShapeDtypeStruct((model, wide), BF16)
    return pl.pallas_call(
        mlp_kernel,
        grid=(steps,),
        out_shape=(
            jax.ShapeDtypeStruct((rows, model), BF16),
            jax.ShapeDtypeStruct((8, model), F32),
            jax.ShapeDtypeStruct((rows, model), F32),
            jax.ShapeDtypeStruct((rows, model), BF16),
            jax.ShapeDtypeStruct((model, model), BF16),
            part,
            part,
            part,
        ),
        in_specs=[pl.BlockSpec(memory_space=pltpu.SMEM)]
        + [vmem] * 5
        + [by_column, pl.BlockSpec((model, tile), lambda i: (0, steps + i)), by_column],
        out_specs=[vmem] * 5 + [by_column] * 3,
        scratch_shapes=[
            pltpu.VMEM((rows, model), BF16),
            pltpu.VMEM((model, rows), BF16),
            pltpu.VMEM((rows, model), BF16),
            pltpu.VMEM((model, rows), BF16),
            pltpu.VMEM((rows, model), F32),
            pltpu.VMEM((rows, model), F32),
            pltpu.VMEM((rows, model), F32),
        ],
        compiler_params=pltpu.CompilerParams(vmem_limit_bytes=63_000_000),
        name="mlp",
    )(bounds, x_rows, heads_out, dy_rows, w_attn, gain, w_input, w_input, w_down)


def shards(
    hidden_in,
    out_grad,
    qkv_weight,
    attn_out_weight,
    in_weight,
    down_weight,
    attn_gain,
    mlp_gain,
    seq_lengths,
    slot_order,
):
    seq_size, fsdp_size = lax.axis_size("seq"), lax.axis_size("fsdp")
    seq_place, fsdp_place = lax.axis_index("seq"), lax.axis_index("fsdp")
    slots, positions, model = hidden_in.shape
    shard = qkv_weight.shape[0]
    ff = down_weight.shape[0]
    wide = up_to(ff, LANES)
    spare = wide - ff
    group = seq_size // slots
    rows = slots * positions
    head_size = model // HEADS

    lead = jnp.zeros((shard, spare), BF16)
    gains = jnp.concatenate(
        [attn_gain[:, None], mlp_gain[:, None], jnp.zeros((shard, LANES - 2), BF16)], axis=1
    )
    in_pack = jnp.concatenate([in_weight[:, :ff], lead, in_weight[:, ff:], lead], axis=1)
    down_pack = jnp.concatenate([down_weight.T, lead], axis=1)
    w_qkv, x_rows = gather_first(qkv_weight, gains, hidden_in, seq_size, fsdp_size)

    slot = fsdp_place * slots + seq_place // group
    order = jnp.sum(jnp.where(jnp.arange(slot_order.shape[0]) == slot, slot_order, 0))
    length = jnp.sum(jnp.where(jnp.arange(seq_lengths.shape[0]) == order, seq_lengths, 0))
    base = (seq_place % group) * rows
    bounds = jnp.stack([length.astype(jnp.int32), base.astype(jnp.int32)])
    places = base + jnp.arange(rows, dtype=jnp.int32)
    cosine, sine = rotary_tables(places, head_size)

    tile = 512 if rows % 512 == 0 and rows * group <= 1024 else 128
    act_one, gain_rows, queries, shared, heads_out, logs, dy_rows, w_attn, w_input, w_down = front(
        bounds,
        x_rows,
        cosine,
        sine,
        w_qkv,
        out_grad,
        (attn_out_weight, in_pack, down_pack),
        (((model, "fzg-"),), ((wide, "zfg"), (wide, "zfg")), ((wide, "fzg"),)),
        group,
        tile,
        seq_size,
        fsdp_size,
    )

    result, vectors, grad_middle, grad_heads, attn_part, in_part, gate_part, down_part = mlp(
        bounds, x_rows, heads_out, dy_rows, w_attn, gain_rows, w_input, w_down
    )

    second = "zf" if seq_size == 4 * LINE else "fz"
    early = [
        (down_part, ((wide, second),)),
        (in_part, ((wide, "fz"),)),
        (gate_part, ((wide, "fz"),)),
        (attn_part, ((model, second),)),
    ]
    late = []
    if rows * group > 1024:
        early, late = late, early
    out_rows, qkv_part, grad_x, vectors, *owned = back(
        bounds,
        queries,
        shared,
        grad_heads,
        heads_out,
        logs,
        cosine,
        sine,
        result,
        act_one,
        x_rows,
        grad_middle,
        gain_rows,
        vectors,
        w_qkv,
        [part for part, _ in early],
        tuple(parts for _, parts in early),
        tile,
        slots,
        seq_size,
        fsdp_size,
    )
    half = 3 * model // 2
    late.append((qkv_part, ((half, "fz"), (half, second))))
    grad_rows, totals, *more = scatter_last(
        [part for part, _ in late],
        tuple(parts for _, parts in late),
        grad_x,
        vectors,
        slots,
        seq_size,
        fsdp_size,
    )
    own_down, own_in, own_gate, own_attn, own_qkv = owned + more
    tokens_valid = jnp.sum(seq_lengths).astype(F32)
    root_squares = jnp.sqrt(jnp.sum(totals[:5], axis=1) / (tokens_valid * model))
    own_gains = lax.dynamic_slice_in_dim(totals, (seq_place * fsdp_size + fsdp_place) * shard, shard, 1)
    return (
        out_rows,
        grad_rows,
        own_qkv,
        own_attn,
        jnp.concatenate([own_in[:, :ff], own_gate[:, :ff]], axis=1),
        own_down[:, :ff].T,
        own_gains[5],
        own_gains[6],
        root_squares,
    )


def solution(mesh):
    placed = (
        P("fsdp", "seq", None),
        P("fsdp", "seq", None),
        P(("seq", "fsdp"), None),
        P(("seq", "fsdp"), None),
        P(("seq", "fsdp"), None),
        P(None, ("seq", "fsdp")),
        P(("seq", "fsdp")),
        P(("seq", "fsdp")),
        P(),
        P(),
    )
    return jax.shard_map(
        shards,
        mesh=mesh,
        in_specs=placed,
        out_specs=(
            P("fsdp", "seq", None),
            P("fsdp", "seq", None),
            P(("seq", "fsdp"), None),
            P(("seq", "fsdp"), None),
            P(("seq", "fsdp"), None),
            P(None, ("seq", "fsdp")),
            P(("seq", "fsdp")),
            P(("seq", "fsdp")),
            P(),
        ),
        check_vma=False,
    )
```

```python
import functools

import jax
import jax.numpy as jnp
from jax import lax
from jax.experimental import pallas as pl
from jax.experimental.pallas import tpu as pltpu
from jax.sharding import PartitionSpec as P

HEADS = 16
LINE = 4
LANES = 128
EPS = 1e-05
THETA = 160000.0
F32 = jnp.float32
BF16 = jnp.bfloat16
MESH = pl.DeviceIdType.MESH


def up_to(size, unit):
    return -(-size // unit) * unit


class Place:
    def __init__(self, seq_size, fsdp_size, swap=True):
        self.seq_size, self.fsdp_size = seq_size, fsdp_size
        self.rest = seq_size // (2 * LINE)
        self.swap = swap and self.rest == fsdp_size
        self.nf, self.ng = self.rest, fsdp_size
        self.blocks = LINE * self.nf * self.ng
        self.seq = lax.axis_index("seq")
        self.y = lax.axis_index("fsdp")
        self.core = self.seq % 2
        self.r = (self.seq // 2) % self.rest
        self.z = self.seq // (2 * self.rest)
        self.f, self.g = self.split(self.r, self.y, self.core)

    def split(self, r, y, core):
        if not self.swap:
            return r, y
        return (1 - core) * r + core * y, (1 - core) * y + core * r

    def device(self, z, f, g, core=None):
        core = self.core if core is None else core
        r, y = self.split(f, g, core)
        return (z * self.rest + r) * 2 + core, y

    def row_block(self, z, f, g, core=None):
        seq, y = self.device(z, f, g, core)
        return seq * self.fsdp_size + y

    def index(self, z, f, g):
        return (z * self.nf + f) * self.ng + g

    def partner(self):
        return self.seq + 1 - 2 * self.core, self.y


def both(first, second):
    if first is True:
        return second
    if second is True:
        return first
    return jnp.logical_and(first, second)


def when(condition, body):
    if condition is True:
        body()
    else:
        pl.when(condition)(body)


def meet(peers, awaited):
    barrier = pltpu.get_barrier_semaphore()
    for condition, device in peers:
        when(
            condition,
            functools.partial(
                pl.semaphore_signal, barrier, inc=1, device_id=device, device_id_type=MESH
            ),
        )
    pl.semaphore_wait(barrier, awaited)


def plane_peers(at):
    below, above = at.z > 0, at.z < LINE - 1
    peers = [
        (below, at.device(at.z - 1, at.f, at.g)),
        (above, at.device(at.z + 1, at.f, at.g)),
        (True, at.partner()),
    ]
    for step in range(1, at.nf):
        peers.append((True, at.device(at.z, (at.f + step) % at.nf, at.g)))
    for step in range(1, at.ng):
        peers.append((True, at.device(at.z, at.f, (at.g + step) % at.ng)))
    count = 1 + (at.nf - 1) + (at.ng - 1)
    count = count + jnp.where(below, 1, 0) + jnp.where(above, 1, 0)
    return peers, count


def slot_peers(at, slots):
    group = at.seq_size // slots
    own_slot, own_part = at.seq // group, at.seq % group
    same = at.seq // slots == own_part
    peers = []
    for step in range(slots):
        wide = ((own_slot + step) % slots) * group + at.seq // slots
        narrow = own_part * slots + (at.seq + step) % slots
        condition = True if step else jnp.logical_not(same)
        peers.append((condition, (wide, at.y)))
        peers.append((condition, (narrow, at.y)))
    return peers, 2 * slots - 2 * jnp.where(same, 1, 0)


def steps_of(at):
    out = []
    for dz in (0, -1, 1, -2, 2, -3, 3):
        for df in range(at.nf):
            for dg in range(at.ng):
                out.append((abs(dz) + (df > 0) + (dg > 0), dz, df, dg))
    out.sort(key=lambda item: item[0])
    return out


def present(at, dz):
    if dz == 0:
        return True
    return at.z + dz >= 0 if dz < 0 else at.z + dz < LINE


class Gather:
    def __init__(self, at, sections, sems, phase):
        self.at, self.sections, self.phase = at, sections, phase
        plain = Place(at.seq_size, at.fsdp_size, swap=False)
        self.places = [plain if section[3][-1] == "-" else at for section in sections]
        self.send_sems, self.plane_sems, self.pair_sems = sems

    @staticmethod
    def scratch(count, nf, ng):
        dma = pltpu.SemaphoreType.DMA
        blocks, kinds = LINE * nf * ng, 3 + (nf - 1) + (ng - 1)
        return [dma((count, blocks, kinds)), dma((count, blocks)), dma((count, blocks + 1))]

    def own(self, number):
        source, _, columns, _ = self.sections[number]
        return source.at[:, columns]

    def block(self, number, z, f, g):
        source, whole, columns, _ = self.sections[number]
        rows = source.shape[0]
        start = pl.multiple_of(self.places[number].row_block(z, f, g) * rows, rows)
        return whole.at[pl.ds(start, rows), columns]

    def forward(self, number, condition, source, dz, df, dg):
        at, order = self.places[number], self.sections[number][3].strip("-")
        z, f, g = at.z + dz, (at.f + df) % at.nf, (at.g + dg) % at.ng
        place, target = at.index(z, f, g), self.block(number, z, f, g)
        moved = {"z": dz, "f": df, "g": dg}
        last = max([i for i, axis in enumerate(order) if moved[axis]], default=-1)

        def send(allowed, kind, device, pair=False):
            sem = (self.pair_sems if pair else self.plane_sems).at[number, place]
            start_copy(
                self.phase,
                both(condition, allowed),
                source,
                target,
                self.send_sems.at[number, place, kind],
                sem,
                device,
            )

        for i, axis in enumerate(order):
            if axis == "z" and i >= last:
                rising, sinking = dz <= 0, dz >= 0
                if rising:
                    send(at.z < LINE - 1, 0, at.device(at.z + 1, at.f, at.g))
                if sinking:
                    send(at.z > 0, 1, at.device(at.z - 1, at.f, at.g))
            if axis == "f" and i > last:
                for step in range(1, at.nf):
                    send(True, 1 + step, at.device(at.z, (at.f + step) % at.nf, at.g))
            if axis == "g" and i > last:
                for step in range(1, at.ng):
                    send(True, at.nf + step, at.device(at.z, at.f, (at.g + step) % at.ng))
        send(True, at.nf + at.ng, at.partner(), pair=True)

    def begin(self):
        for number in range(len(self.sections)):
            at = self.places[number]
            self.forward(number, True, self.own(number), 0, 0, 0)
            own = pltpu.make_async_copy(
                self.own(number),
                self.block(number, at.z, at.f, at.g),
                self.pair_sems.at[number, at.blocks],
            )
            if self.phase.ending:
                own.wait()
            else:
                own.start()

    def arrival(self, number, dz, df, dg):
        at = self.places[number]
        z, f, g = at.z + dz, (at.f + df) % at.nf, (at.g + dg) % at.ng
        condition = present(at, dz)
        block = self.block(number, z, f, g)
        sem = self.plane_sems.at[number, at.index(z, f, g)]
        if not self.phase.ending:
            when(condition, functools.partial(await_block, block, sem))
        self.forward(number, condition, block, dz, df, dg)

    def events(self):
        marked = [
            (hops, number, place, item)
            for place, (hops, *item) in enumerate(steps_of(self.at)[1:])
            for number in range(len(self.sections))
        ]
        marked.sort(key=lambda entry: entry[:3])
        return [functools.partial(self.arrival, number, *item) for _, number, _, item in marked]

    def from_partner(self, number, dz, df, dg):
        at = self.places[number]
        f, g = at.split(*at.split(at.f, at.g, at.core), 1 - at.core)
        z, f, g = at.z + dz, (f + df) % at.nf, (g + dg) % at.ng
        sem = self.pair_sems.at[number, at.index(z, f, g)]
        when(
            present(at, dz), functools.partial(await_block, self.block(number, 0, 0, 0), sem)
        )

    def steps(self, lag):
        events = self.events()

        def close(event):
            self.phase.ending = True
            event()
            self.from_partner(*event.args)
            self.phase.ending = False

        def step(number):
            events[number]()
            if number >= lag:
                close(events[number - lag])

        def rest():
            for event in events[-lag:]:
                close(event)
            self.phase.ending = True
            self.begin()
            for number in range(len(self.sections)):
                self.from_partner(number, 0, 0, 0)
            self.phase.ending = False

        return [functools.partial(step, number) for number in range(len(events))], rest


def trade_in(at, source_ref, target_ref, send_sems, recv_sems, phase):
    slots, positions = source_ref.shape[0], source_ref.shape[1]
    group = at.seq_size // slots
    own_slot, own_part = at.seq // group, at.seq % group
    same = at.seq // slots == own_part
    lane = at.seq % slots
    target = target_ref.at[pl.ds(pl.multiple_of(lane * positions, positions), positions), :]
    for step in range(slots):
        slot = (own_slot + step) % slots
        if step == 0 and not phase.ending:
            local = pltpu.make_async_copy(source_ref.at[slot], target, recv_sems.at[lane])
            when(same, local.start)
        start_copy(
            phase,
            True if step else jnp.logical_not(same),
            source_ref.at[slot],
            target,
            send_sems.at[step],
            recv_sems.at[lane],
            (slot * group + at.seq // slots, at.y),
        )
        if phase.ending:
            await_block(target_ref.at[pl.ds(step * positions, positions), :], recv_sems.at[step])


def trade_out(at, source_ref, target_ref, send_sems, recv_sems, phase):
    slots, positions = target_ref.shape[0], target_ref.shape[1]
    group = at.seq_size // slots
    own_slot, own_part = at.seq // group, at.seq % group
    same = at.seq // slots == own_part
    target = target_ref.at[own_slot]
    for step in range(slots):
        lane = (at.seq + step) % slots
        source = source_ref.at[pl.ds(pl.multiple_of(lane * positions, positions), positions), :]
        if step == 0 and not phase.ending:
            local = pltpu.make_async_copy(source, target, recv_sems.at[own_slot])
            when(same, local.start)
        start_copy(
            phase,
            True if step else jnp.logical_not(same),
            source,
            target,
            send_sems.at[step],
            recv_sems.at[own_slot],
            (own_part * slots + lane, at.y),
        )
        if phase.ending:
            await_block(target_ref.at[step], recv_sems.at[step])


def first_kernel(sizes, spans, weight_ref, gains_ref, hidden_ref, whole_ref, rows_ref, *refs):
    at = Place(*sizes)
    sems, (trade_send, trade_recv, pack_ref, pack_sems) = refs[:3], refs[3:]
    width, extra_width = weight_ref.shape[1], gains_ref.shape[1]
    loads = [
        pltpu.make_async_copy(weight_ref, pack_ref.at[:, pl.ds(0, width)], pack_sems.at[0]),
        pltpu.make_async_copy(gains_ref, pack_ref.at[:, pl.ds(width, extra_width)], pack_sems.at[1]),
    ]
    for load in loads:
        load.start()
    peers, count = plane_peers(at)
    more, extra = slot_peers(at, hidden_ref.shape[0])
    meet(peers + more, count + extra)
    for load in loads:
        load.wait()
    phase = Phase()
    sections, start = [], 0
    for size, order in spans:
        sections.append((pack_ref, whole_ref, pl.ds(start, size), order))
        start += size
    gather = Gather(at, sections, sems, phase)
    steps, rest = gather.steps(12)
    gather.begin()
    trade_in(at, hidden_ref, rows_ref, trade_send, trade_recv, phase)
    run_all(steps)
    rest()
    phase.ending = True
    trade_in(at, hidden_ref, rows_ref, trade_send, trade_recv, phase)


def gather_first(weight, gains, hidden, seq_size, fsdp_size):
    slots, positions, model = hidden.shape
    nf, ng = seq_size // (2 * LINE), fsdp_size
    devices = seq_size * fsdp_size
    dma = pltpu.SemaphoreType.DMA
    shard, width = weight.shape[0], weight.shape[1] + gains.shape[1]
    half = weight.shape[1] // 2
    spans = ((half, "zfg"), (width - half, "zfg"))
    return pl.pallas_call(
        functools.partial(first_kernel, (seq_size, fsdp_size), spans),
        out_shape=(
            jax.ShapeDtypeStruct((shard * devices, width), BF16),
            jax.ShapeDtypeStruct((slots * positions, model), BF16),
        ),
        in_specs=[pl.BlockSpec(memory_space=pltpu.VMEM)] * 3,
        out_specs=[pl.BlockSpec(memory_space=pl.ANY)] * 2,
        scratch_shapes=Gather.scratch(len(spans), nf, ng)
        + [dma((slots,)), dma((slots,)), pltpu.VMEM((shard, width), BF16), dma((2,))],
        compiler_params=pltpu.CompilerParams(collective_id=0, has_side_effects=True),
        name="gather_first",
    )(weight, gains, hidden)


def add_blocks(target, others):
    width = target.shape[1]
    piece = max(size for size in range(LANES, 1025, LANES) if width % size == 0)

    def body(number, carry):
        columns = pl.ds(pl.multiple_of(number * piece, LANES), piece)
        total = target[:, columns].astype(F32)
        for other in others:
            total = total + other[:, columns].astype(F32)
        target[:, columns] = total.astype(target.dtype)
        return carry

    lax.fori_loop(0, width // piece, body, 0)


def line_targets(at):
    order = []
    for dz in (-3, 3, -2, 2, -1, 1, 0):
        for df in list(range(1, at.nf)) + [0]:
            for dg in list(range(1, at.ng)) + [0]:
                order.append((dg == 0, df == 0, -abs(dz), dz, df, dg))
    order.sort(key=lambda item: item[:3])
    return [item[3:] for item in order]


class Phase:
    def __init__(self):
        self.ending = False


def start_copy(phase, condition, source, target, send_sem, recv_sem, device):
    copy = pltpu.make_async_remote_copy(
        src_ref=source,
        dst_ref=target,
        send_sem=send_sem,
        recv_sem=recv_sem,
        device_id=device,
        device_id_type=MESH,
    )
    when(condition, copy.wait_send if phase.ending else copy.start)


def run_all(events):
    for event in events:
        event()


def await_block(buffer, sem):
    pltpu.make_async_copy(buffer, buffer, sem).wait()


class Scatter:
    PARTS = 17

    @staticmethod
    def scratch(order, rows, width, nf, ng):
        dma = pltpu.SemaphoreType.DMA
        plane, beyond_g = LINE * nf * ng, (ng - 1) * LINE * nf
        beyond_f = (nf - 1) * (LINE if order == "fz" else 1)
        line = LINE * (1 if order == "fz" else nf)
        counts = (plane, plane, beyond_g, beyond_f, line, line)
        buffers = [pltpu.VMEM((count, rows, width), BF16) for count in counts]
        sems = (plane, plane, plane, beyond_g, beyond_g, beyond_f, beyond_f, line, line, line, line)
        return buffers + [dma((count,)) for count in sems]

    def __init__(self, at, source, columns, order, scratch, phase):
        self.at, self.source, self.columns, self.order = at, source, columns, order
        self.phase = phase
        self.acc, self.from_pair, self.from_g, self.from_f = scratch[:4]
        self.from_below, self.from_above = scratch[4:6]
        self.load_sems, self.pair_send, self.pair_recv = scratch[6:9]
        self.g_send, self.g_recv, self.f_send, self.f_recv = scratch[9:13]
        self.up_send, self.up_recv, self.down_send, self.down_recv = scratch[13:]
        self.rows = self.acc.shape[1]

    def where_is(self, dz, df, dg):
        at = self.at
        return at.z + dz, (at.f + df) % at.nf, (at.g + dg) % at.ng

    def rows_of(self, z, f, g, core=None):
        start = pl.multiple_of(self.at.row_block(z, f, g, core) * self.rows, self.rows)
        return self.source.at[pl.ds(start, self.rows), self.columns]

    def begin(self, dz, df, dg):
        at = self.at
        z, f, g = self.where_is(dz, df, dg)
        place, other = at.index(z, f, g), 1 - at.core
        pf, pg = at.split(*at.split(at.f, at.g, at.core), other)
        pf, pg = (pf + df) % at.nf, (pg + dg) % at.ng
        there = at.index(z, pf, pg)

        def body():
            if self.phase.ending:
                await_block(self.from_pair.at[there], self.pair_send.at[there])
                return
            pltpu.make_async_copy(
                self.rows_of(z, f, g), self.acc.at[place], self.load_sems.at[place]
            ).start()
            pltpu.make_async_remote_copy(
                src_ref=self.rows_of(z, pf, pg, other),
                dst_ref=self.from_pair.at[there],
                send_sem=self.pair_send.at[there],
                recv_sem=self.pair_recv.at[there],
                device_id=at.partner(),
                device_id_type=MESH,
            ).start()

        when(present(at, dz), body)

    def join(self, condition, place, parts):
        if self.phase.ending:
            return

        def body():
            ready = [(buffer, sem) for allowed, buffer, sem in parts if allowed is True]
            for buffer, sem in ready:
                await_block(buffer, sem)
            if ready:
                add_blocks(self.acc.at[place], [buffer for buffer, _ in ready])
            for allowed, buffer, sem in parts:
                if allowed is not True:

                    def more(buffer=buffer, sem=sem):
                        await_block(buffer, sem)
                        add_blocks(self.acc.at[place], [buffer])

                    pl.when(allowed)(more)

        when(condition, body)

    def over_pair(self, dz, df, dg):
        at = self.at
        z, f, g = self.where_is(dz, df, dg)
        condition = present(at, dz)
        place = at.index(z, f, g)
        if not self.phase.ending:
            when(
                condition,
                functools.partial(await_block, self.acc.at[place], self.load_sems.at[place]),
            )
        self.join(condition, place, [(True, self.from_pair.at[place], self.pair_recv.at[place])])
        if dg:
            slot = (dg - 1) * LINE * at.nf + z * at.nf + f
            start_copy(
                self.phase,
                condition,
                self.acc.at[place],
                self.from_g.at[slot],
                self.g_send.at[slot],
                self.g_recv.at[slot],
                at.device(at.z, at.f, g),
            )

    def g_parts(self, z, f):
        slots = [(step - 1) * LINE * self.at.nf + z * self.at.nf + f for step in range(1, self.at.ng)]
        return [(True, self.from_g.at[slot], self.g_recv.at[slot]) for slot in slots]

    def f_slot(self, z, step):
        return (step - 1) * LINE + z if self.order == "fz" else step - 1

    def f_parts(self, z):
        slots = [self.f_slot(z, step) for step in range(1, self.at.nf)]
        return [(True, self.from_f.at[slot], self.f_recv.at[slot]) for slot in slots]

    def line_slot(self, z, f):
        return z if self.order == "fz" else z * self.at.nf + f

    def line_parts(self, dz, z, f):
        slot, parts = self.line_slot(z, f), []
        if 0 <= dz < LINE - 1:
            parts.append((self.at.z > 0, self.from_below.at[slot], self.up_recv.at[slot]))
        if 1 - LINE < dz <= 0:
            parts.append((self.at.z < LINE - 1, self.from_above.at[slot], self.down_recv.at[slot]))
        return parts

    def send_f(self, condition, df, z, f, place):
        slot = self.f_slot(z, df)
        start_copy(
            self.phase,
            condition,
            self.acc.at[place],
            self.from_f.at[slot],
            self.f_send.at[slot],
            self.f_recv.at[slot],
            self.at.device(self.at.z, f, self.at.g),
        )

    def send_line(self, condition, dz, z, f, place):
        slot = self.line_slot(z, f)
        rising = dz > 0
        start_copy(
            self.phase,
            condition,
            self.acc.at[place],
            (self.from_below if rising else self.from_above).at[slot],
            (self.up_send if rising else self.down_send).at[slot],
            (self.up_recv if rising else self.down_recv).at[slot],
            self.at.device(self.at.z + (1 if rising else -1), self.at.f, self.at.g),
        )

    def second(self, dz, df):
        z, f, _ = self.where_is(dz, df, 0)
        condition = present(self.at, dz)
        place = self.at.index(z, f, self.at.g)
        parts = self.g_parts(z, f)
        if self.order == "zf":
            parts = parts + self.line_parts(dz, z, f)
        self.join(condition, place, parts)
        if self.order == "zf" and dz:
            self.send_line(condition, dz, z, f, place)
        elif df:
            self.send_f(condition, df, z, f, place)

    def third(self, dz):
        z, f = self.at.z + dz, self.at.f
        condition = present(self.at, dz)
        place = self.at.index(z, f, self.at.g)
        parts = self.f_parts(z)
        if self.order == "fz":
            parts = parts + self.line_parts(dz, z, f)
        self.join(condition, place, parts)
        if dz:
            self.send_line(condition, dz, z, f, place)

    def stages(self):
        order = line_targets(self.at)
        part = functools.partial
        begins = [part(self.begin, *item) for item in order]
        pairs = [part(self.over_pair, *item) for item in order]
        if self.order == "fz":
            seconds = [part(self.second, *item[:2]) for item in order if item[2] == 0]
            thirds = [part(self.third, dz) for dz in (-3, 3, -2, 2, -1, 1, 0)]
        else:
            dfs = list(range(1, self.at.nf)) + [0]
            seconds = [part(self.second, dz, df) for dz in (-3, 3, -2, 2, -1, 1, 0) for df in dfs]
            thirds = [part(self.third, 0)]
        return begins, pairs, seconds, thirds

    def store(self, target, start):
        place = self.at.index(self.at.z, self.at.f, self.at.g)
        target[:, pl.ds(start, self.acc.shape[2])] = self.acc[place].astype(F32)


def mixed(first, second):
    marked = []
    for kind, steps in enumerate((first, second)):
        marked += [((i + 0.5) / len(steps), kind, step) for i, step in enumerate(steps)]
    return [step for _, _, step in sorted(marked, key=lambda item: item[:2])]


def pipelined(scatters):
    first, mids, lasts, starts = [], [], [], {}
    for scatter in scatters:
        begins, pairs, seconds, thirds = scatter.stages()
        starts.update(zip(pairs, begins))
        first += [step for step in pairs if step.args[2]]
        mid = []
        for second in seconds:
            mid += [step for step in pairs if step.args == (*second.args, 0)] + [second]
        mids.append(mid)
        lasts.append(thirds)
    events = list(first)
    for slot in range(len(scatters) + 1):
        some = lasts[slot - 1] if slot else []
        if slot < len(scatters):
            some = mixed(some, mids[slot]) if some else mids[slot]
        events += some
    begins = [starts[event] for event in events if event in starts]
    later = iter(begins[AHEAD:])

    def with_begin(event):
        begin = next(later, None) if event in starts else None
        return event if begin is None else functools.partial(run_all, [event, begin])

    return begins[:AHEAD], [with_begin(event) for event in events], len(first)


AHEAD = 64


def lagged(events, lag, phase):
    def close(event):
        phase.ending = True
        event()
        phase.ending = False

    def step(number):
        events[number]()
        if number >= lag:
            close(events[number - lag])

    def rest():
        for event in events[-lag:]:
            close(event)

    return [functools.partial(step, number) for number in range(len(events))], rest


def split_scratch(refs, count):
    size = Scatter.PARTS
    return [refs[i * size : (i + 1) * size] for i in range(count)], refs[count * size :]


def scatter_sections(at, sources, spans, scratches, phase):
    scatters, places = [], []
    for number, parts in enumerate(spans):
        start = 0
        for size, order in parts:
            scratch = scratches[len(scatters)]
            scatters.append(Scatter(at, sources[number], pl.ds(start, size), order, scratch, phase))
            places.append((number, start))
            start += size
    return scatters, places


def scatter_kernel(sizes, spans, *refs):
    at = Place(*sizes)
    count, sections = len(spans), sum(len(parts) for parts in spans)
    sources, refs = refs[:count], refs[count:]
    input_ref, vector_ref, grad_ref, total_ref = refs[:4]
    owned, refs = refs[4 : 4 + count], refs[4 + count :]
    scratches, refs = split_scratch(refs, sections)
    sq_g, sq_f, sq_z, sq_c, trade_send, trade_recv, sq_send, sq_recv = refs
    slots = grad_ref.shape[0]
    peers, number = plane_peers(at)
    more, extra = slot_peers(at, slots)
    meet(peers + more, number + extra)
    phase = Phase()
    send = functools.partial(start_copy, phase)
    scatters, places = scatter_sections(at, sources, spans, scratches, phase)
    begins, events, _ = pipelined(scatters)
    steps, rest = lagged(events, 64, phase)
    other = 1 - at.core

    def vectors_g():
        for step in range(1, at.ng):
            device = at.device(at.z, at.f, (at.g + step) % at.ng)
            send(True, sq_g.at[at.g], sq_g.at[at.g], sq_send.at[0, step], sq_recv.at[0, at.g], device)

    def vectors_f():
        for step in range(1, at.nf):
            device = at.device(at.z, (at.f + step) % at.nf, at.g)
            send(True, sq_f.at[at.f], sq_f.at[at.f], sq_send.at[1, step], sq_recv.at[1, at.f], device)

    def line_send(condition, held, kind):
        device = at.device(at.z - 1 if kind else at.z + 1, at.f, at.g)
        send(condition, sq_z.at[held], sq_z.at[held], sq_send.at[2 + kind, held], sq_recv.at[2, held], device)

    def vectors_line(distance):
        for kind, held in enumerate((at.z - distance, at.z + distance)):
            there = held < LINE if kind else held >= 0
            onward = at.z > 0 if kind else at.z < LINE - 1
            if distance and not phase.ending:
                when(
                    there,
                    functools.partial(await_block, sq_z.at[held], sq_recv.at[2, held]),
                )
            line_send(both(there, onward), held, kind)

    def vectors_pair():
        send(
            True,
            sq_c.at[at.core],
            sq_c.at[at.core],
            sq_send.at[4, 0],
            sq_recv.at[3, at.core],
            at.partner(),
        )

    def sums():
        def g():
            for step in range(1, at.ng):
                peer = (at.g + step) % at.ng
                await_block(sq_g.at[peer], sq_recv.at[0, peer])
            total = sq_g[0]
            for number in range(1, at.ng):
                total = total + sq_g[number]
            sq_f[at.f] = total
            vectors_f()

        def f():
            for step in range(1, at.nf):
                peer = (at.f + step) % at.nf
                await_block(sq_f.at[peer], sq_recv.at[1, peer])
            total = sq_f[0]
            for number in range(1, at.nf):
                total = total + sq_f[number]
            sq_z[at.z] = total
            vectors_line(0)

        def pair():
            total = sq_z[0]
            for number in range(1, LINE):
                total = total + sq_z[number]
            sq_c[at.core] = total
            vectors_pair()

        return [g, f] + [functools.partial(vectors_line, d) for d in range(1, LINE)] + [pair]

    sq_g[at.g] = vector_ref[...]
    run_all(begins)
    vectors_g()
    trade_out(at, input_ref, grad_ref, trade_send, trade_recv, phase)
    run_all(mixed(steps, sums()))
    for scatter, (number, start) in zip(scatters, places):
        scatter.store(owned[number], start)
    await_block(sq_c.at[other], sq_recv.at[3, other])
    total_ref[...] = sq_c[0] + sq_c[1]

    rest()
    phase.ending = True
    run_all(begins)
    trade_out(at, input_ref, grad_ref, trade_send, trade_recv, phase)
    vectors_g()
    vectors_f()
    for distance in range(LINE):
        vectors_line(distance)
    vectors_pair()


def scatter_last(sources, spans, input_grad, vectors, slots, seq_size, fsdp_size):
    rows = sources[0].shape[0] // (seq_size * fsdp_size)
    own_rows, model = input_grad.shape
    positions = own_rows // slots
    nf, ng = seq_size // (2 * LINE), fsdp_size
    dma = pltpu.SemaphoreType.DMA
    widest = max(nf, ng, LINE)
    vmem = pl.BlockSpec(memory_space=pltpu.VMEM)
    scratch = []
    for parts in spans:
        for size, order in parts:
            scratch += Scatter.scratch(order, rows, size, nf, ng)
    return pl.pallas_call(
        functools.partial(scatter_kernel, (seq_size, fsdp_size), spans),
        out_shape=tuple(
            [
                jax.ShapeDtypeStruct((slots, positions, model), BF16),
                jax.ShapeDtypeStruct(vectors.shape, F32),
            ]
            + [jax.ShapeDtypeStruct((rows, source.shape[1]), F32) for source in sources]
        ),
        in_specs=[pl.BlockSpec(memory_space=pl.ANY)] * len(sources) + [vmem] * 2,
        out_specs=[vmem] * (2 + len(sources)),
        scratch_shapes=scratch
        + [pltpu.VMEM((size, *vectors.shape), F32) for size in (ng, nf, LINE, 2)]
        + [dma((slots,)), dma((slots,)), dma((5, widest)), dma((4, widest))],
        compiler_params=pltpu.CompilerParams(
            collective_id=3, has_side_effects=True, vmem_limit_bytes=63_000_000
        ),
        name="scatter_last",
    )(*sources, input_grad, vectors)


def first_half(shape):
    lane = lax.broadcasted_iota(jnp.int32, shape, 1)
    return lane % 64 < 32


def turn(values, cosine, sine):
    half = first_half(values.shape)
    away = jnp.where(half, -pltpu.roll(values, 96, 1), pltpu.roll(values, 32, 1))
    return values * cosine + away * sine


def turn_back(grads, cosine, sine):
    half = first_half(grads.shape)
    moved = grads * sine
    away = jnp.where(half, pltpu.roll(moved, 96, 1), -pltpu.roll(moved, 32, 1))
    return grads * cosine + away


def normalize(values):
    average = jnp.mean(values, axis=-1, keepdims=True)
    centered = values - average
    variance = jnp.mean(centered * centered, axis=-1, keepdims=True)
    inverse = lax.rsqrt(variance + EPS)
    return centered * inverse, inverse


def norm_back(grad_normed, normed, inverse, gain_values):
    scaled = grad_normed * gain_values
    first_mean = jnp.mean(scaled, axis=-1, keepdims=True)
    second_mean = jnp.mean(scaled * normed, axis=-1, keepdims=True)
    return inverse * (scaled - first_mean - normed * second_mean)


def head_lanes(shape, head):
    return lax.broadcasted_iota(jnp.int32, shape, 1) // 64 == head


def scores_of(keys, queries, bias):
    scores = lax.dot_general(keys, queries, (((1,), (1,)), ((), ())), preferred_element_type=F32)
    return scores + bias


def key_bias(length, shape):
    return jnp.where(lax.broadcasted_iota(jnp.int32, shape, 0) < length, 0.0, -jnp.inf)


def attend(length, queries, keys, values):
    queries = queries * 0.125
    bias = key_bias(length, (keys.shape[0], 1))
    zero = jnp.zeros((), BF16)
    total, logs = None, []
    for head in range(2):
        only = head_lanes(queries.shape, head)
        scores = scores_of(keys, jnp.where(only, queries, zero), bias)
        largest = jnp.max(scores, axis=0, keepdims=True)
        weights = jnp.exp(scores - largest)
        summed = jnp.sum(weights, axis=0, keepdims=True)
        logs.append(largest + jnp.log(summed))
        held = jnp.where(head_lanes(values.shape, head), values, zero)
        part = lax.dot_general(
            held, weights.astype(BF16), (((0,), (0,)), ((), ())), preferred_element_type=F32
        )
        part = part / summed
        total = part if total is None else total + part
    return total.T.astype(BF16), logs


FRONT_TILE = 512


def front_kernel(sizes, group, spans, *refs):
    at = Place(*sizes)
    count = len(spans)
    length_ref, x_ref, gains_ref, cos_ref, sin_ref, w_ref, dy_ref = refs[:7]
    sources, refs = refs[7 : 7 + count], refs[7 + count :]
    act_ref, gain_ref, q_ref, shared_out, o_ref, log_ref, dy_rows_ref = refs[:7]
    wholes, refs = refs[7 : 7 + count], refs[7 + count :]
    sems, (trade_send, trade_recv, share_send, share_recv, shared_ref, out_sem) = refs[:3], refs[3:]
    step = pl.program_id(0)
    rows, model = q_ref.shape
    slots = dy_ref.shape[0]
    tile = o_ref.shape[0]
    tiles = rows // tile
    projecting = 3 * model // FRONT_TILE
    steps = projecting + model // LANES * tiles
    kept = 2 * model // FRONT_TILE
    phase = Phase()
    sections = []
    for number, parts in enumerate(spans):
        start = 0
        for size, order in parts:
            sections.append((sources[number], wholes[number], pl.ds(start, size), order))
            start += size
    gather = Gather(at, sections, sems, phase)
    base, part = (at.seq // group) * group, at.seq % group
    members = [base + (part + other) % group for other in range(1, group)]
    own_rows = pl.ds(pl.multiple_of(part * rows, rows), rows)

    @pl.when(step == 0)
    def _():
        peers, number = plane_peers(at)
        more, extra = slot_peers(at, slots)
        others = [(True, (member, at.y)) for member in members]
        meet(peers + more + others, number + extra + group - 1)

    @pl.when(step == 0)
    def _():
        gather.begin()
        trade_in(at, dy_ref, dy_rows_ref, trade_send, trade_recv, phase)

    @pl.when(step == 0)
    def _():
        normed, _ = normalize(x_ref[...].astype(F32))
        turned = gains_ref[...].astype(F32).T
        gain_ref[...] = turned[:8]
        act_ref[...] = (normed * turned[:1]).astype(BF16)

    def share(number):
        place = shared_ref.at[own_rows, pl.ds(number * FRONT_TILE, FRONT_TILE)]
        for other, member in enumerate(members):
            start_copy(
                phase,
                True,
                place,
                place,
                share_send.at[number, other],
                share_recv.at[number, part],
                (member, at.y),
            )

    def receive():
        for number in range(kept):
            for other in range(1, group):
                source = (part + other) % group
                place = shared_ref.at[
                    pl.ds(pl.multiple_of(source * rows, rows), rows),
                    pl.ds(number * FRONT_TILE, FRONT_TILE),
                ]
                await_block(place, share_recv.at[number, source])
        pltpu.make_async_copy(shared_ref, shared_out, out_sem).start()

    for number in range(kept):
        pl.when(step == number + 1)(functools.partial(share, number))
    pl.when(step == projecting)(receive)

    @pl.when(step < projecting)
    def _():
        mixed = jnp.dot(act_ref[...], w_ref[...], preferred_element_type=F32)

        def turned():
            cosine, sine = cos_ref[...], sin_ref[...]
            pieces = [
                turn(mixed[:, start : start + LANES], cosine, sine).astype(BF16)
                for start in range(0, FRONT_TILE, LANES)
            ]
            return jnp.concatenate(pieces, axis=1)

        @pl.when(step < kept // 2)
        def _():
            columns = pl.ds(pl.multiple_of(step * FRONT_TILE, FRONT_TILE), FRONT_TILE)
            shared_ref[own_rows, columns] = turned()

        @pl.when(both(step >= kept // 2, step < kept))
        def _():
            columns = pl.ds(pl.multiple_of(step * FRONT_TILE, FRONT_TILE), FRONT_TILE)
            shared_ref[own_rows, columns] = mixed.astype(BF16)

        @pl.when(step >= kept)
        def _():
            columns = pl.ds(pl.multiple_of((step - kept) * FRONT_TILE, FRONT_TILE), FRONT_TILE)
            q_ref[:, columns] = turned()

    @pl.when(step >= projecting)
    def _():
        pair, piece = (step - projecting) // tiles, (step - projecting) % tiles
        start = pl.multiple_of(pair * LANES, LANES)
        out, logs = attend(
            length_ref[0],
            q_ref[pl.ds(pl.multiple_of(piece * tile, tile), tile), pl.ds(start, LANES)],
            shared_ref[:, pl.ds(start, LANES)],
            shared_ref[:, pl.ds(pl.multiple_of(model + start, LANES), LANES)],
        )
        o_ref[...] = out
        for head in range(2):
            log_ref[0, head : head + 1, :] = logs[head]

    events, rest = gather.steps(24)
    pace = FRONT_PACE
    for number in range(steps - 1):
        group_events = events[number * pace : (number + 1) * pace]
        if group_events:
            pl.when(step == number)(functools.partial(run_all, group_events))

    @pl.when(step == steps - 1)
    def _():
        run_all(events[(steps - 1) * pace :])
        rest()
        phase.ending = True
        trade_in(at, dy_ref, dy_rows_ref, trade_send, trade_recv, phase)
        for number in range(kept):
            share(number)
        pltpu.make_async_copy(shared_ref, shared_out, out_sem).wait()
        phase.ending = False


FRONT_PACE = 4


def front(length, x_rows, cosine, sine, weight, dy, sources, spans, group, tile, seq_size, fsdp_size):
    rows, model = x_rows.shape
    slots, positions, _ = dy.shape
    pairs, tiles = model // LANES, rows // tile
    projecting, kept = 3 * model // FRONT_TILE, 2 * model // FRONT_TILE
    nf, ng = seq_size // (2 * LINE), fsdp_size
    devices = seq_size * fsdp_size
    count = sum(len(parts) for parts in spans)
    dma = pltpu.SemaphoreType.DMA
    vmem, anywhere = pl.BlockSpec(memory_space=pltpu.VMEM), pl.BlockSpec(memory_space=pl.ANY)

    def pair_of(i):
        return jnp.maximum(i - projecting, 0) // tiles

    def tile_of(i):
        return jnp.maximum(i - projecting, 0) % tiles

    return pl.pallas_call(
        functools.partial(front_kernel, (seq_size, fsdp_size), group, spans),
        grid=(projecting + pairs * tiles,),
        out_shape=tuple(
            [
                jax.ShapeDtypeStruct((rows, model), BF16),
                jax.ShapeDtypeStruct((8, model), F32),
                jax.ShapeDtypeStruct((rows, model), BF16),
                jax.ShapeDtypeStruct((rows * group, 2 * model), BF16),
                jax.ShapeDtypeStruct((rows, model), BF16),
                jax.ShapeDtypeStruct((pairs, 8, rows), F32),
                jax.ShapeDtypeStruct((slots * positions, model), BF16),
            ]
            + [
                jax.ShapeDtypeStruct((source.shape[0] * devices, source.shape[1]), BF16)
                for source in sources
            ]
        ),
        in_specs=[pl.BlockSpec(memory_space=pltpu.SMEM), vmem]
        + [pl.BlockSpec((model, LANES), lambda i: (0, 3 * model // LANES)), vmem, vmem]
        + [
            pl.BlockSpec(
                (model, FRONT_TILE),
                lambda i: (0, (jnp.minimum(i, projecting - 1) + projecting - kept) % projecting),
            )
        ]
        + [vmem] * (1 + len(sources)),
        out_specs=[
            vmem,
            vmem,
            vmem,
            anywhere,
            pl.BlockSpec((tile, LANES), lambda i: (tile_of(i), pair_of(i))),
            pl.BlockSpec((1, 8, tile), lambda i: (pair_of(i), 0, tile_of(i))),
        ]
        + [anywhere] * (1 + len(sources)),
        scratch_shapes=Gather.scratch(count, nf, ng)
        + [dma((slots,)), dma((slots,)), dma((kept, group)), dma((kept, group))]
        + [pltpu.VMEM((rows * group, 2 * model), BF16), dma],
        compiler_params=pltpu.CompilerParams(
            collective_id=1, has_side_effects=True, vmem_limit_bytes=63_000_000
        ),
        name="front",
    )(length, x_rows, weight, cosine, sine, weight, dy, *sources)


def attend_back(length, queries, keys, values, grads, heads_out, logs):
    queries = queries * 0.125
    bias = key_bias(length, (keys.shape[0], 1))
    zero = jnp.zeros((), BF16)
    product = (grads.astype(F32) * heads_out.astype(F32)).T
    dq = dk = dv = None
    for head in range(2):
        only = head_lanes(queries.shape, head)
        query = jnp.where(only, queries, zero)
        grad = jnp.where(only, grads, zero)
        key = jnp.where(head_lanes(keys.shape, head), keys, zero)
        delta = jnp.sum(product[64 * head : 64 * head + 64], axis=0, keepdims=True)
        scores = scores_of(keys, query, bias)
        probs = jnp.exp(scores - logs[head : head + 1])
        grad_probs = lax.dot_general(
            values, grad, (((1,), (1,)), ((), ())), preferred_element_type=F32
        )
        grad_scores = (probs * (grad_probs - delta)).astype(BF16)
        value_part = jnp.dot(probs.astype(BF16), grad, preferred_element_type=F32)
        key_part = jnp.dot(grad_scores, query, preferred_element_type=F32)
        query_part = lax.dot_general(
            key, grad_scores, (((0,), (0,)), ((), ())), preferred_element_type=F32
        )
        dq = query_part if dq is None else dq + query_part
        dk = key_part if dk is None else dk + key_part
        dv = value_part if dv is None else dv + value_part
    return dq.T * 0.125, dk, dv


def back_kernel(sizes, group, spans, *refs):
    at = Place(*sizes)
    sections = sum(len(parts) for parts in spans)
    count = len(spans)
    length_ref, q_ref, k_ref, v_ref, g_ref, o_ref, log_ref, cos_ref, sin_ref, result_ref = refs[:10]
    act_ref, x_ref, middle_ref, gain_ref, vectors_ref, w_ref = refs[10:16]
    sources, refs = refs[16 : 16 + count], refs[16 + count :]
    out_ref, part_ref, grad_x_ref, sums_ref = refs[:4]
    owned, refs = refs[4 : 4 + count], refs[4 + count :]
    scratches, refs = split_scratch(refs, sections)
    dk_acc, dv_acc, parts_ref, arrived, sum_send, sum_recv, trade_send, trade_recv = refs[:8]
    mixed_ref, act_turned, grad_act = refs[8:]
    step = pl.program_id(0)
    tile = q_ref.shape[0]
    rows, model = result_ref.shape
    tiles, pairs = rows // tile, model // LANES
    attending = pairs * tiles
    steps = attending + 1 + 3 * model // FRONT_TILE
    slots = out_ref.shape[0]
    phase = Phase()
    scatters, places = scatter_sections(at, sources, spans, scratches, phase)
    begins, events, ahead = pipelined(scatters)
    events, rest = lagged(events, 120, phase)
    base, part = (at.seq // group) * group, at.seq % group
    members = [base + (part + other) % group for other in range(1, group)]

    def columns_of(pair):
        return pl.ds(pl.multiple_of(pair * LANES, LANES), LANES)

    def share(pair):
        for kind in range(2):
            for other, member in enumerate(members):
                owner = (part + other + 1) % group
                start_copy(
                    phase,
                    True,
                    parts_ref.at[kind, pl.ds(pl.multiple_of(owner * rows, rows), rows), columns_of(pair)],
                    arrived.at[kind, other, :, columns_of(pair)],
                    sum_send.at[kind, other, pair],
                    sum_recv.at[kind, other, pair],
                    (member, at.y),
                )

    @pl.when(step == 0)
    def _():
        peers, number = plane_peers(at)
        more, extra = slot_peers(at, slots)
        others = [(True, (member, at.y)) for member in members]
        meet(peers + more + others, number + extra + group - 1)
        run_all(begins)
        trade_out(at, result_ref, out_ref, trade_send, trade_recv, phase)
        run_all(events[:ahead])

    for number in range(1, steps):
        some = events[ahead + (number - 1) * BACK_PACE : ahead + number * BACK_PACE]
        if some:
            pl.when(step == number)(functools.partial(run_all, some))

    shared_now = jnp.logical_and(both(step > 0, step <= attending), step % tiles == 0)
    pl.when(shared_now)(lambda: share(step // tiles - 1))

    @pl.when(step < attending)
    def _():
        pair, piece = step // tiles, step % tiles
        own = pl.ds(pl.multiple_of(piece * tile, tile), tile)
        dq, dk, dv = attend_back(
            length_ref[0], q_ref[...], k_ref[...], v_ref[...], g_ref[...], o_ref[...], log_ref[0]
        )
        mixed_ref[own, columns_of(pair)] = turn_back(dq, cos_ref[own], sin_ref[own]).astype(BF16)
        if tiles == 1:
            parts_ref[0, :, columns_of(pair)] = dk.astype(BF16)
            parts_ref[1, :, columns_of(pair)] = dv.astype(BF16)
            return

        @pl.when(piece == 0)
        def _():
            dk_acc[...] = dk
            dv_acc[...] = dv

        @pl.when(piece > 0)
        def _():
            dk_acc[...] += dk
            dv_acc[...] += dv

        @pl.when(piece == tiles - 1)
        def _():
            parts_ref[0, :, columns_of(pair)] = dk_acc[...].astype(BF16)
            parts_ref[1, :, columns_of(pair)] = dv_acc[...].astype(BF16)

    def add_parts():
        own = pl.ds(pl.multiple_of(part * rows, rows), rows)

        def body(pair, carry):
            for kind in range(2):
                total = parts_ref[kind, own, columns_of(pair)].astype(F32)
                for other in range(group - 1):
                    piece = arrived.at[kind, other, :, columns_of(pair)]
                    await_block(piece, sum_recv.at[kind, other, pair])
                    total = total + piece[...].astype(F32)
                if kind == 0:
                    total = turn_back(total, cos_ref[...], sin_ref[...])
                start = pl.multiple_of((kind + 1) * model + pair * LANES, LANES)
                mixed_ref[:, pl.ds(start, LANES)] = total.astype(BF16)
            return carry

        lax.fori_loop(0, pairs, body, 0)

    @pl.when(step == attending)
    def _():
        add_parts()
        act_turned[...] = act_ref[...].astype(F32).T.astype(BF16)
        grad_act[...] = jnp.zeros_like(grad_act)

    @pl.when(step > attending)
    def _():
        start = pl.multiple_of((step - attending - 1) * FRONT_TILE, FRONT_TILE)
        grad_mixed = mixed_ref[:, pl.ds(start, FRONT_TILE)]
        grad_act[...] += mm_right_t(grad_mixed, w_ref[...])
        part_ref[...] = mm(act_turned[...], grad_mixed).astype(BF16)

    @pl.when(step == steps - 1)
    def _():
        normed, inverse = normalize(x_ref[...].astype(F32))
        sums_ref[...] = vectors_ref[...]
        sums_ref[5:6, :] = jnp.sum(grad_act[...] * normed, axis=0, keepdims=True)
        grad_x = middle_ref[...] + norm_back(grad_act[...], normed, inverse, gain_ref[0:1, :])
        grad_x_ref[...] = grad_x.astype(BF16)
        run_all(events[ahead + (steps - 1) * BACK_PACE :])
        for scatter, (number, start) in zip(scatters, places):
            scatter.store(owned[number], start)
        rest()
        phase.ending = True
        run_all(begins)
        trade_out(at, result_ref, out_ref, trade_send, trade_recv, phase)

        def body(pair, carry):
            share(pair)
            return carry

        lax.fori_loop(0, pairs, body, 0)
        phase.ending = False


BACK_PACE = 3


def back(
    length,
    queries,
    shared,
    grads,
    heads_out,
    logs,
    cosine,
    sine,
    result,
    act,
    x_rows,
    grad_middle,
    gain,
    vectors,
    weight,
    sources,
    spans,
    tile,
    slots,
    seq_size,
    fsdp_size,
):
    rows, keys, model = queries.shape[0], shared.shape[0], queries.shape[1]
    group, positions = keys // rows, rows // slots
    pairs, tiles = model // LANES, rows // tile
    nf, ng = seq_size // (2 * LINE), fsdp_size
    devices = seq_size * fsdp_size
    shard = model // devices
    vmem, anywhere = pl.BlockSpec(memory_space=pltpu.VMEM), pl.BlockSpec(memory_space=pl.ANY)
    dma = pltpu.SemaphoreType.DMA

    def pair_of(i):
        return jnp.minimum(i, pairs * tiles - 1) // tiles

    def tile_of(i):
        return jnp.minimum(i, pairs * tiles - 1) % tiles

    by_row = pl.BlockSpec((tile, LANES), lambda i: (tile_of(i), pair_of(i)))
    last = 3 * model // FRONT_TILE - 1
    by_column = pl.BlockSpec(
        (model, FRONT_TILE), lambda i: (0, jnp.clip(i - pairs * tiles - 1, 0, last))
    )
    scratch = []
    for parts in spans:
        for size, order in parts:
            scratch += Scatter.scratch(order, shard, size, nf, ng)
    return pl.pallas_call(
        functools.partial(back_kernel, (seq_size, fsdp_size), group, spans),
        grid=(pairs * tiles + 2 + last,),
        out_shape=tuple(
            [
                jax.ShapeDtypeStruct((slots, positions, model), BF16),
                jax.ShapeDtypeStruct((model, 3 * model), BF16),
                jax.ShapeDtypeStruct((rows, model), BF16),
                jax.ShapeDtypeStruct(vectors.shape, F32),
            ]
            + [jax.ShapeDtypeStruct((shard, source.shape[1]), F32) for source in sources]
        ),
        in_specs=[
            pl.BlockSpec(memory_space=pltpu.SMEM),
            by_row,
            pl.BlockSpec((keys, LANES), lambda i: (0, pair_of(i))),
            pl.BlockSpec((keys, LANES), lambda i: (0, pairs + pair_of(i))),
            by_row,
            by_row,
            pl.BlockSpec((1, 8, tile), lambda i: (pair_of(i), 0, tile_of(i))),
            vmem,
            vmem,
            vmem,
        ]
        + [vmem] * 5
        + [by_column]
        + [anywhere] * len(sources),
        out_specs=[anywhere, by_column, vmem, vmem] + [vmem] * len(sources),
        scratch_shapes=scratch
        + [
            pltpu.VMEM((keys, LANES), F32),
            pltpu.VMEM((keys, LANES), F32),
            pltpu.VMEM((2, keys, model), BF16),
            pltpu.VMEM((2, group - 1, rows, model), BF16),
            dma((2, group - 1, pairs)),
            dma((2, group - 1, pairs)),
            dma((slots,)),
            dma((slots,)),
            pltpu.VMEM((rows, 3 * model), BF16),
            pltpu.VMEM((model, rows), BF16),
            pltpu.VMEM((rows, model), F32),
        ],
        compiler_params=pltpu.CompilerParams(
            collective_id=2, has_side_effects=True, vmem_limit_bytes=67_000_000
        ),
        name="back",
    )(
        length,
        queries,
        shared,
        shared,
        grads,
        heads_out,
        logs,
        cosine,
        sine,
        result,
        act,
        x_rows,
        grad_middle,
        gain,
        vectors,
        weight,
        *sources,
    )


def rotary_tables(places, head_size):
    halfway = head_size // 2
    ladder = jnp.arange(halfway, dtype=F32) * (2.0 / head_size)
    inverse = 1.0 / THETA**ladder
    angles = places.astype(F32)[:, None] * inverse[None, :]
    angles = jnp.concatenate([angles] * 4, axis=-1)
    return jnp.cos(angles), jnp.sin(angles)


def mm(left, right):
    return jnp.dot(left, right, preferred_element_type=F32)


def mm_right_t(left, right):
    return lax.dot_general(left, right, (((1,), (1,)), ((), ())), preferred_element_type=F32)


def mm_left_t(left, right):
    return lax.dot_general(left, right, (((0,), (0,)), ((), ())), preferred_element_type=F32)


SQRT_HALF = 0.7071067811865476
INV_SQRT_TAU = 0.3989422804014327


def gelu_and_slope(values):
    share = 0.5 + 0.5 * lax.erf(values * SQRT_HALF)
    density = INV_SQRT_TAU * jnp.exp(-0.5 * values * values)
    return values * share, share + values * density


def mlp_kernel(
    bounds_ref,
    x_ref,
    heads_ref,
    dy_ref,
    w_attn_ref,
    gain_ref,
    w_in_ref,
    w_gate_ref,
    w_down_ref,
    result_ref,
    vectors_ref,
    grad_middle_ref,
    grad_heads_ref,
    attn_part_ref,
    in_part_ref,
    gate_part_ref,
    down_part_ref,
    act,
    act_turned,
    grad_branch,
    grad_turned,
    middle,
    branch,
    grad_act,
):
    step = pl.program_id(0)
    rows = x_ref.shape[0]
    gain = gain_ref[1:2, :]
    position = bounds_ref[1] + lax.broadcasted_iota(jnp.int32, (rows, 1), 0)
    valid = jnp.where(position < bounds_ref[0], 1.0, 0.0).astype(F32)

    def squares(row, values):
        vectors_ref[row : row + 1, :] = jnp.sum(valid * values * values, axis=0, keepdims=True)

    @pl.when(step == 0)
    def _():
        x_wide = x_ref[...].astype(F32)
        attn = mm(heads_ref[...], w_attn_ref[...])
        total = x_wide + attn
        middle[...] = total
        vectors_ref[...] = jnp.zeros_like(vectors_ref)
        squares(0, x_wide)
        squares(1, total)
        squares(3, attn)
        scaled = normalize(total)[0] * gain
        act[...] = scaled.astype(BF16)
        act_turned[...] = scaled.T.astype(BF16)
        grad_y = dy_ref[...].astype(F32) * valid
        grad_branch[...] = grad_y.astype(BF16)
        grad_turned[...] = grad_y.T.astype(BF16)
        branch[...] = jnp.zeros_like(branch)
        grad_act[...] = jnp.zeros_like(grad_act)

    input_half = mm(act[...], w_in_ref[...])
    gate_half = mm(act[...], w_gate_ref[...])
    grad_product = mm(grad_branch[...], w_down_ref[...])
    active, slope = gelu_and_slope(input_half)
    product = (active * gate_half).astype(BF16)
    grad_input = (grad_product * gate_half * slope).astype(BF16)
    grad_gate = (grad_product * active).astype(BF16)
    branch[...] += mm_right_t(product, w_down_ref[...])
    grad_act[...] += mm_right_t(grad_input, w_in_ref[...]) + mm_right_t(grad_gate, w_gate_ref[...])
    in_part_ref[...] = mm(act_turned[...], grad_input).astype(BF16)
    gate_part_ref[...] = mm(act_turned[...], grad_gate).astype(BF16)
    down_part_ref[...] = mm(grad_turned[...], product).astype(BF16)

    @pl.when(step == pl.num_programs(0) - 1)
    def _():
        result = (middle[...] + branch[...]) * valid
        squares(2, result)
        squares(4, branch[...])
        result_ref[...] = result.astype(BF16)
        normed, inverse = normalize(middle[...])
        vectors_ref[6:7, :] = jnp.sum(grad_act[...] * normed, axis=0, keepdims=True)
        grad_y = dy_ref[...].astype(F32) * valid
        grad_middle = grad_y + norm_back(grad_act[...], normed, inverse, gain)
        grad_middle_ref[...] = grad_middle
        grad_attn = grad_middle.astype(BF16)
        grad_heads_ref[...] = mm_right_t(grad_attn, w_attn_ref[...]).astype(BF16)
        attn_part_ref[...] = mm_left_t(heads_ref[...], grad_attn).astype(BF16)


MLP_TILE = 896


def mlp(bounds, x_rows, heads_out, dy_rows, w_attn, gain, w_input, w_down):
    rows, model = x_rows.shape
    wide = w_down.shape[1]
    tile = MLP_TILE if wide % MLP_TILE == 0 else LANES
    steps = wide // tile
    vmem = pl.BlockSpec(memory_space=pltpu.VMEM)
    by_column = pl.BlockSpec((model, tile), lambda i: (0, i))
    part = jax.ShapeDtypeStruct((model, wide), BF16)
    return pl.pallas_call(
        mlp_kernel,
        grid=(steps,),
        out_shape=(
            jax.ShapeDtypeStruct((rows, model), BF16),
            jax.ShapeDtypeStruct((8, model), F32),
            jax.ShapeDtypeStruct((rows, model), F32),
            jax.ShapeDtypeStruct((rows, model), BF16),
            jax.ShapeDtypeStruct((model, model), BF16),
            part,
            part,
            part,
        ),
        in_specs=[pl.BlockSpec(memory_space=pltpu.SMEM)]
        + [vmem] * 5
        + [by_column, pl.BlockSpec((model, tile), lambda i: (0, steps + i)), by_column],
        out_specs=[vmem] * 5 + [by_column] * 3,
        scratch_shapes=[
            pltpu.VMEM((rows, model), BF16),
            pltpu.VMEM((model, rows), BF16),
            pltpu.VMEM((rows, model), BF16),
            pltpu.VMEM((model, rows), BF16),
            pltpu.VMEM((rows, model), F32),
            pltpu.VMEM((rows, model), F32),
            pltpu.VMEM((rows, model), F32),
        ],
        compiler_params=pltpu.CompilerParams(vmem_limit_bytes=63_000_000),
        name="mlp",
    )(bounds, x_rows, heads_out, dy_rows, w_attn, gain, w_input, w_input, w_down)


def shards(
    hidden_in,
    out_grad,
    qkv_weight,
    attn_out_weight,
    in_weight,
    down_weight,
    attn_gain,
    mlp_gain,
    seq_lengths,
    slot_order,
):
    seq_size, fsdp_size = lax.axis_size("seq"), lax.axis_size("fsdp")
    seq_place, fsdp_place = lax.axis_index("seq"), lax.axis_index("fsdp")
    slots, positions, model = hidden_in.shape
    shard = qkv_weight.shape[0]
    ff = down_weight.shape[0]
    wide = up_to(ff, LANES)
    spare = wide - ff
    group = seq_size // slots
    rows = slots * positions
    head_size = model // HEADS

    lead = jnp.zeros((shard, spare), BF16)
    gains = jnp.concatenate(
        [attn_gain[:, None], mlp_gain[:, None], jnp.zeros((shard, LANES - 2), BF16)], axis=1
    )
    in_pack = jnp.concatenate([in_weight[:, :ff], lead, in_weight[:, ff:], lead], axis=1)
    down_pack = jnp.concatenate([down_weight.T, lead], axis=1)
    w_qkv, x_rows = gather_first(qkv_weight, gains, hidden_in, seq_size, fsdp_size)

    slot = fsdp_place * slots + seq_place // group
    order = jnp.sum(jnp.where(jnp.arange(slot_order.shape[0]) == slot, slot_order, 0))
    length = jnp.sum(jnp.where(jnp.arange(seq_lengths.shape[0]) == order, seq_lengths, 0))
    base = (seq_place % group) * rows
    bounds = jnp.stack([length.astype(jnp.int32), base.astype(jnp.int32)])
    places = base + jnp.arange(rows, dtype=jnp.int32)
    cosine, sine = rotary_tables(places, head_size)

    tile = 512 if rows % 512 == 0 and rows * group <= 1024 else 128
    act_one, gain_rows, queries, shared, heads_out, logs, dy_rows, w_attn, w_input, w_down = front(
        bounds,
        x_rows,
        cosine,
        sine,
        w_qkv,
        out_grad,
        (attn_out_weight, in_pack, down_pack),
        (((model, "fzg-"),), ((wide, "zfg"), (wide, "zfg")), ((wide, "fzg"),)),
        group,
        tile,
        seq_size,
        fsdp_size,
    )

    result, vectors, grad_middle, grad_heads, attn_part, in_part, gate_part, down_part = mlp(
        bounds, x_rows, heads_out, dy_rows, w_attn, gain_rows, w_input, w_down
    )

    second = "zf" if seq_size == 4 * LINE else "fz"
    early = [
        (down_part, ((wide, second),)),
        (in_part, ((wide, "fz"),)),
        (gate_part, ((wide, "fz"),)),
        (attn_part, ((model, second),)),
    ]
    late = []
    if rows * group > 1024:
        early, late = late, early
    out_rows, qkv_part, grad_x, vectors, *owned = back(
        bounds,
        queries,
        shared,
        grad_heads,
        heads_out,
        logs,
        cosine,
        sine,
        result,
        act_one,
        x_rows,
        grad_middle,
        gain_rows,
        vectors,
        w_qkv,
        [part for part, _ in early],
        tuple(parts for _, parts in early),
        tile,
        slots,
        seq_size,
        fsdp_size,
    )
    half = 3 * model // 2
    late.append((qkv_part, ((half, "fz"), (half, second))))
    grad_rows, totals, *more = scatter_last(
        [part for part, _ in late],
        tuple(parts for _, parts in late),
        grad_x,
        vectors,
        slots,
        seq_size,
        fsdp_size,
    )
    own_down, own_in, own_gate, own_attn, own_qkv = owned + more
    tokens_valid = jnp.sum(seq_lengths).astype(F32)
    root_squares = jnp.sqrt(jnp.sum(totals[:5], axis=1) / (tokens_valid * model))
    own_gains = lax.dynamic_slice_in_dim(totals, (seq_place * fsdp_size + fsdp_place) * shard, shard, 1)
    return (
        out_rows,
        grad_rows,
        own_qkv,
        own_attn,
        jnp.concatenate([own_in[:, :ff], own_gate[:, :ff]], axis=1),
        own_down[:, :ff].T,
        own_gains[5],
        own_gains[6],
        root_squares,
    )


def solution(mesh):
    placed = (
        P("fsdp", "seq", None),
        P("fsdp", "seq", None),
        P(("seq", "fsdp"), None),
        P(("seq", "fsdp"), None),
        P(("seq", "fsdp"), None),
        P(None, ("seq", "fsdp")),
        P(("seq", "fsdp")),
        P(("seq", "fsdp")),
        P(),
        P(),
    )
    return jax.shard_map(
        shards,
        mesh=mesh,
        in_specs=placed,
        out_specs=(
            P("fsdp", "seq", None),
            P("fsdp", "seq", None),
            P(("seq", "fsdp"), None),
            P(("seq", "fsdp"), None),
            P(("seq", "fsdp"), None),
            P(None, ("seq", "fsdp")),
            P(("seq", "fsdp")),
            P(("seq", "fsdp")),
            P(),
        ),
        check_vma=False,
    )
```
